256 devices in a mesh: inst: 8 (over x, core), axial: 32 (over y, z).
Axes of the slice: x: 4, y: 4, z: 8, core: 2. Of those that a mesh axis runs over, the one named last changes fastest.
Arguments:
- flow_state: float32 [32, 512, 320], P('inst', 'axial'), may hold values from -6 to 6
- forcing: float32 [32, 512, 320], P('inst', 'axial'), may hold values from -6 to 6
- tile_inverse: bfloat16 [512, 320, 320], P('axial')
- coupling: bfloat16 [512, 320, 320], P('axial')
- sweep_order: int32 [512], P('axial'), may hold values from 0 to 15, as said below
Outputs:
- final_state: float32 [32, 512, 320], P('inst', 'axial')
The draws below stay inside these ranges and needn't reach their ends.
Inputs may be any that keep to these rules, and one draw needn't show every extreme that they name: `sweep_order`: the 16 entries of each axial group form a permutation of 0 to 15.
All inputs are finite; a program needn't handle non-finite values.
Results may differ from the reference program's by a relative error of at most 0.0003.
Values sent between devices are 32-bit elements; how exact they have to be, the bound alone decides.
A program may use at most 128 MiB of HBM per device.

```python
import math
import jax
import jax.numpy as jnp
from jax import lax

B = 320
INSTANCES = 32
TILES_DEV = 16
SLAB_TILE_COUNT = 512
ITERS = 2
N_AXIAL = 32


def draw_tile_inverse(key, part):
    noise = jax.random.normal(key, (SLAB_TILE_COUNT, B, B), jnp.float32)
    eye_block = jnp.eye(B, dtype=jnp.float32)
    return (0.5 * eye_block[None] + 0.02 / math.sqrt(B) * noise).astype(jnp.bfloat16)


def draw_coupling(key, part):
    key_rates = jax.random.fold_in(key, 11)
    pulse_group_key = jax.random.fold_in(key, 13)
    key_noise = jax.random.fold_in(key, 17)
    upper = math.log(max(SLAB_TILE_COUNT / 30.0, 0.5))
    decay = jnp.exp(jax.random.uniform(key_rates, (B,), jnp.float32, math.log(0.1), upper))
    relaxation_rates = 2.0 * jnp.exp(-decay / SLAB_TILE_COUNT)
    pulse_group = jax.random.randint(pulse_group_key, (SLAB_TILE_COUNT, 1), 0, SLAB_TILE_COUNT) < 3
    per_tile_relaxation = relaxation_rates[None, :] * jnp.where(pulse_group, 0.6, 1.0)
    noise = jax.random.normal(key_noise, (SLAB_TILE_COUNT, B, B), jnp.float32)
    eye_block = jnp.eye(B, dtype=jnp.float32)
    blocks = -(eye_block[None] * per_tile_relaxation[:, None, :]) + 0.04 / math.sqrt(B) * noise
    return blocks.astype(jnp.bfloat16)


def draw_sweep_order(key, part):
    scores = jax.random.randint(key, (N_AXIAL, TILES_DEV), 0, 1 << 20) * TILES_DEV
    scores = scores + jnp.arange(TILES_DEV, dtype=jnp.int32)[None, :]
    ranks = jnp.argsort(scores, axis=1, stable=True).astype(jnp.int32)
    return ranks.reshape(SLAB_TILE_COUNT)


def block_levels(key, extent, cuts, low, high):
    gain = 1.0
    for dim, shards_of in cuts:
        heights = jax.random.uniform(jax.random.fold_in(jax.random.fold_in(key, 6), dim), (shards_of,), jnp.float32, low / len(cuts), high / len(cuts))
        gain = gain * jnp.repeat(jnp.exp(heights), extent[dim] // shards_of).reshape((-1,) + (1,) * (len(extent) - 1 - dim))
    return gain


def scatter_about(stream_key, extent, scale, bound, pieces=(), held_as=jnp.bfloat16):
    factor_of = block_levels(stream_key, extent, pieces, -0.22, 0.18) if pieces else 1.0
    result = jax.random.normal(stream_key, extent, jnp.float32) * scale * factor_of
    return jnp.minimum(jnp.maximum(result, -bound), bound).astype(held_as)


def setup_inputs(seed: int = 0) -> dict:
    keys = jax.random.split(jax.random.key(seed), 6)
    flow_state = scatter_about(keys[0], (INSTANCES, SLAB_TILE_COUNT, B), 1.0, 6.0, ((0, 8), (1, 32)), jnp.float32)
    forcing = scatter_about(keys[1], (INSTANCES, SLAB_TILE_COUNT, B), 1.0, 6.0, ((0, 8), (1, 32)), jnp.float32)
    tile_inverse = draw_tile_inverse(jax.random.fold_in(keys[5], 71), 0)
    coupling = draw_coupling(jax.random.fold_in(keys[5], 71), 0)
    sweep_order = draw_sweep_order(jax.random.fold_in(keys[5], 71), 0)
    return {"flow_state": flow_state, "forcing": forcing, "tile_inverse": tile_inverse, "coupling": coupling, "sweep_order": sweep_order}


highest = lax.Precision.HIGHEST
spectral_gain = 2.0


def spectral_rows(row_ids, col_ids, period):
    distance = row_ids[:, None] - col_ids[None, :]
    parity = 1.0 - 2.0 * jnp.mod(distance, 2).astype(jnp.float32)
    angles = jnp.pi * distance.astype(jnp.float32) / period
    on_diag = distance == 0
    sine_safe = jnp.where(on_diag, 1.0, jnp.sin(angles))
    return jnp.where(on_diag, 0.0, 0.5 * parity * jnp.cos(angles) / sine_safe)


def visit_tile(upstream, tile_items):
    right_side, inverse, couple_tile = tile_items
    collapsed_result = right_side - jnp.dot(upstream, couple_tile.astype(jnp.float32).T, precision=highest)
    updated = jnp.dot(collapsed_result, inverse.astype(jnp.float32).T, precision=highest)
    return updated, updated


def reference(flow_state, forcing, tile_inverse, coupling, sweep_order):
    period = flow_state.shape[0]
    total_tiles = flow_state.shape[1]
    width = flow_state.shape[2]
    positions = jnp.arange(total_tiles, dtype=jnp.int32)
    visit_ids = (positions // TILES_DEV) * TILES_DEV + sweep_order.astype(jnp.int32)
    inst_ids = jnp.arange(period, dtype=jnp.int32)
    derivative = spectral_rows(inst_ids, inst_ids, period) * (spectral_gain / period)
    inverse_seq = tile_inverse[visit_ids]
    couple_seq = coupling[visit_ids]
    for repeat in range(ITERS):
        source_term = jnp.einsum("ij,jtb->itb", derivative, flow_state, precision=highest)
        right_side = forcing - source_term - flow_state
        ordered = jnp.swapaxes(right_side[:, visit_ids], 0, 1)
        start_zero = jnp.zeros((period, width), jnp.float32)
        _, updates = lax.scan(visit_tile, start_zero, (ordered, inverse_seq, couple_seq))
        increment = jnp.zeros_like(flow_state).at[:, visit_ids].set(jnp.swapaxes(updates, 0, 1))
        flow_state = flow_state + increment
    return flow_state
```

```python
import functools

import jax
import jax.numpy as jnp
import numpy as np
from jax import lax
from jax.experimental import pallas as pl
from jax.experimental.pallas import tpu as pltpu
from jax.sharding import PartitionSpec as P

ITERS = 2
SPECTRAL_GAIN = 2.0
MESH = pl.DeviceIdType.MESH
F32, BF16 = jnp.float32, jnp.bfloat16
NT = (((1,), (1,)), ((), ()))
NN = (((1,), (0,)), ((), ()))


def exchange_matrix(period, groups):
    idx = np.arange(period)
    dist = idx[:, None] - idx[None, :]
    angle = np.pi * dist / period
    safe = np.where(dist == 0, 1.0, np.sin(angle))
    deriv = np.where(dist == 0, 0.0, 0.5 * (1.0 - 2.0 * (dist % 2)) * np.cos(angle) / safe)
    e = deriv * (SPECTRAL_GAIN / period) + np.eye(period)
    whole = np.block([[-e @ e, e], [-2.0 * e, 2.0 * np.eye(period)]])
    local = period // groups
    perm = np.array(
        [part * period + dev * local + n for dev in range(groups) for part in range(2) for n in range(local)]
    )
    return whole[np.ix_(perm, perm)].astype(np.float32)


def halves(x):
    high = x.astype(BF16)
    low = (x - high.astype(F32)).astype(BF16)
    return high, low


def times(x, w, dims=NT):
    m = x.shape[0]
    y = lax.dot_general(jnp.concatenate(halves(x), 0), w, dims, preferred_element_type=F32)
    return y[:m] + y[m:]


def kernel(n_inst, n_axial, order, kmat, s0, f, a_hbm, c_hbm, out,
           wa, wc, sb, rb, ob, rq, u, tx, tw, inflow, outflow, inv,
           w_sem, x1_send, x1_recv, x2_send, x2_recv, pair_sem, chain_sem):
    i = lax.axis_index("inst")
    a = lax.axis_index("axial")
    local, tiles, width = s0.shape
    per = tiles // n_inst
    half = width // 2
    core = lax.rem(i, 2)
    partner = i + 1 - 2 * core
    nxt, prv = lax.rem(a + 1, n_axial), lax.rem(a + n_axial - 1, n_axial)

    load_a = pltpu.make_async_copy(a_hbm, wa, w_sem.at[0])
    load_c = pltpu.make_async_copy(c_hbm, wc, w_sem.at[1])
    load_a.start()
    load_c.start()

    barrier = pltpu.get_barrier_semaphore()
    for d in range(1, n_inst):
        pl.semaphore_signal(barrier, inc=1, device_id={"inst": lax.rem(i + d, n_inst)}, device_id_type=MESH)
    for there in (nxt, prv):
        pl.semaphore_signal(barrier, inc=1, device_id={"axial": there}, device_id_type=MESH)

    for t in range(tiles):
        sb[t, 0:local, :] = s0[:, t, :]
        sb[t, local:2 * local, :] = f[:, t, :]
    for t in range(tiles):
        pos = jnp.int32(0)
        for k in range(tiles):
            pos = jnp.where(order[k] == t, k, pos)
        inv[t] = pos
    row = lax.broadcasted_iota(jnp.int32, (half, width), 0)
    col = lax.broadcasted_iota(jnp.int32, (half, width), 1)
    tx[core, 0] = jnp.where(col == row + core * half, 1.0, 0.0).astype(F32)
    tx[core, 1] = jnp.zeros((half, width), F32)

    pl.semaphore_wait(barrier, n_inst + 1)

    def first(d):
        peer = lax.rem(i + d, n_inst)
        return pltpu.make_async_remote_copy(
            src_ref=sb.at[pl.ds(per * peer, per)], dst_ref=rb.at[i],
            send_sem=x1_send.at[d], recv_sem=x1_recv.at[d],
            device_id={"inst": peer}, device_id_type=MESH)

    def second(d):
        peer = lax.rem(i + d, n_inst)
        return pltpu.make_async_remote_copy(
            src_ref=ob.at[peer], dst_ref=rq.at[pl.ds(per * i, per)],
            send_sem=x2_send.at[d], recv_sem=x2_recv.at[d],
            device_id={"inst": peer}, device_id_type=MESH)

    for d in range(1, n_inst):
        first(d).start()
    rb[i] = sb[pl.ds(per * i, per)]

    load_a.wait()
    load_c.wait()

    def column_step(k, carry):
        t = order[k]
        c, ai = wc[t], wa[t]
        b = times(tx[core].reshape(2 * half, width), c)
        p = -times(b[:half], ai)
        tx[core, 0] = p
        tx[core, 1] = -times(p + b[half:], ai)
        return carry

    lax.fori_loop(0, tiles // 2, column_step, 0)

    for d in range(1, n_inst):
        first(d).wait_recv()
    for t in range(per):
        mixed = jnp.dot(kmat[...], rb[:, t].reshape(2 * local * n_inst, width),
                        precision=lax.Precision.HIGHEST, preferred_element_type=F32)
        ob[:, t] = mixed.reshape(n_inst, 2 * local, width)
    for d in range(1, n_inst):
        second(d).start()
    rq[pl.ds(per * i, per)] = ob[i]

    lax.fori_loop(tiles // 2, tiles, column_step, 0)

    pair = pltpu.make_async_remote_copy(
        src_ref=tx.at[core], dst_ref=tx.at[core], send_sem=pair_sem.at[0], recv_sem=pair_sem.at[1],
        device_id={"inst": partner}, device_id_type=MESH)
    pair.start()
    for d in range(1, n_inst):
        second(d).wait_recv()

    lower = lax.broadcasted_iota(jnp.int32, (2 * local, width), 0) >= local

    def data_step(k, x):
        t = order[k]
        y = times(rq[t] - times(x, wc[t]), wa[t])
        z = times(pltpu.roll(y, local, 0), wa[t])
        return jnp.where(lower, y - z, y)

    zero = jnp.zeros((2 * local, width), F32)
    shift = lax.fori_loop(0, tiles, data_step, zero)

    other = pltpu.make_async_remote_copy(
        src_ref=tx.at[1 - core], dst_ref=tx.at[1 - core], send_sem=pair_sem.at[0], recv_sem=pair_sem.at[1],
        device_id={"inst": partner}, device_id_type=MESH)
    other.wait_recv()
    pad = tw.shape[1] // 4
    for h in range(2):
        for part in range(2):
            high, low = halves(tx[h, part])
            tw[pl.ds(h * half, half), part * pad:part * pad + width] = high
            tw[pl.ds(h * half, half), (2 + part) * pad:(2 + part) * pad + width] = low

    def through(x):
        y = lax.dot_general(jnp.concatenate(halves(x), 0), tw[...], NN, preferred_element_type=F32)
        y = y[:2 * local] + y[2 * local:]
        y = y[:, :2 * pad] + y[:, 2 * pad:]
        own, cross = y[:, :width], y[:, pad:pad + width]
        return own + jnp.where(lower, pltpu.roll(cross, local, 0), 0.0)

    forward = pltpu.make_async_remote_copy(
        src_ref=outflow, dst_ref=inflow, send_sem=chain_sem.at[0], recv_sem=chain_sem.at[1],
        device_id={"axial": nxt}, device_id_type=MESH)

    @pl.when(a == 0)
    def _():
        inflow[...] = zero
        outflow[...] = shift

    @pl.when(a > 0)
    def _():
        forward.wait_recv()
        outflow[...] = through(inflow[...]) + shift

    @pl.when(a < n_axial - 1)
    def _():
        forward.start()

    def final_step(k, x):
        x = data_step(k, x)
        u[k] = x
        return x

    lax.fori_loop(0, tiles, final_step, inflow[...])
    for t in range(tiles):
        out[:, t, :] = s0[:, t, :] + u[inv[t], local:2 * local, :]

    for d in range(1, n_inst):
        first(d).wait_send()
        second(d).wait_send()
    pair.wait_send()

    @pl.when(a < n_axial - 1)
    def _():
        forward.wait_send()


def solution(mesh):
    n_inst, n_axial = mesh.shape["inst"], mesh.shape["axial"]

    def on_device(flow_state, forcing, tile_inverse, coupling, sweep_order):
        local, tiles, width = flow_state.shape
        per = tiles // n_inst
        half = width // 2
        pad = -(-width // 128) * 128
        rows = 2 * local
        kmat = jnp.asarray(exchange_matrix(local * n_inst, n_inst))
        vmem = pl.BlockSpec(memory_space=pltpu.VMEM)
        return pl.pallas_call(
            functools.partial(kernel, n_inst, n_axial),
            out_shape=jax.ShapeDtypeStruct(flow_state.shape, F32),
            in_specs=[pl.BlockSpec(memory_space=pltpu.SMEM), vmem, vmem, vmem,
                      pl.BlockSpec(memory_space=pl.ANY), pl.BlockSpec(memory_space=pl.ANY)],
            out_specs=vmem,
            scratch_shapes=[
                pltpu.VMEM((tiles, width, width), BF16),
                pltpu.VMEM((tiles, width, width), BF16),
                pltpu.VMEM((tiles, rows, width), F32),
                pltpu.VMEM((n_inst, per, rows, width), F32),
                pltpu.VMEM((n_inst, per, rows, width), F32),
                pltpu.VMEM((tiles, rows, width), F32),
                pltpu.VMEM((tiles, rows, width), F32),
                pltpu.VMEM((2, 2, half, width), F32),
                pltpu.VMEM((width, 4 * pad), BF16),
                pltpu.VMEM((rows, width), F32),
                pltpu.VMEM((rows, width), F32),
                pltpu.SMEM((tiles,), jnp.int32),
                pltpu.SemaphoreType.DMA((2,)),
                pltpu.SemaphoreType.DMA((n_inst,)),
                pltpu.SemaphoreType.DMA((n_inst,)),
                pltpu.SemaphoreType.DMA((n_inst,)),
                pltpu.SemaphoreType.DMA((n_inst,)),
                pltpu.SemaphoreType.DMA((2,)),
                pltpu.SemaphoreType.DMA((2,)),
            ],
            compiler_params=pltpu.CompilerParams(collective_id=0, has_side_effects=True),
        )(sweep_order, kmat, flow_state, forcing, tile_inverse, coupling)

    return jax.shard_map(
        on_device,
        mesh=mesh,
        in_specs=(P("inst", "axial", None), P("inst", "axial", None), P("axial", None, None),
                  P("axial", None, None), P("axial")),
        out_specs=P("inst", "axial", None),
        check_vma=False,
    )
```

```python
import functools

import jax
import jax.numpy as jnp
import numpy as np
from jax import lax
from jax.experimental import pallas as pl
from jax.experimental.pallas import tpu as pltpu
from jax.sharding import PartitionSpec as P

ITERS = 2
SPECTRAL_GAIN = 2.0
NZ = 8
CHUNK = 16
MESH = pl.DeviceIdType.MESH
F32, BF16 = jnp.float32, jnp.bfloat16
NT = (((1,), (1,)), ((), ()))
NN = (((1,), (0,)), ((), ()))


def exchange_matrix(period, groups):
    idx = np.arange(period)
    dist = idx[:, None] - idx[None, :]
    angle = np.pi * dist / period
    safe = np.where(dist == 0, 1.0, np.sin(angle))
    deriv = np.where(dist == 0, 0.0, 0.5 * (1.0 - 2.0 * (dist % 2)) * np.cos(angle) / safe)
    e = deriv * (SPECTRAL_GAIN / period) + np.eye(period)
    whole = np.block([[-e @ e, e], [-2.0 * e, 2.0 * np.eye(period)]])
    local = period // groups
    perm = np.array(
        [part * period + dev * local + n for dev in range(groups) for part in range(2) for n in range(local)]
    )
    return whole[np.ix_(perm, perm)].astype(np.float32)


def halves(x):
    high = x.astype(BF16)
    low = (x - high.astype(F32)).astype(BF16)
    return high, low


def split(x):
    high = x.astype(BF16).astype(F32)
    return jnp.concatenate([high, x - high], 0).astype(BF16)


def times(x, w, dims=NT):
    m = x.shape[0]
    y = lax.dot_general(split(x), w, dims, preferred_element_type=F32)
    return y[:m] + y[m:]


def store_map(dst, row, part, block):
    pad = dst.shape[1] // 4
    rows, width = block.shape
    high, low = halves(block)
    dst[pl.ds(row, rows), part * pad:part * pad + width] = high
    dst[pl.ds(row, rows), (2 + part) * pad:(2 + part) * pad + width] = low


def through(m, p, g):
    rows, width = p.shape
    pad = m.shape[1] // 4
    y = lax.dot_general(split(jnp.concatenate([p, g], 0)), m[...], NN, preferred_element_type=F32)
    y = y[:2 * rows] + y[2 * rows:]
    y = y[:, :2 * pad] + y[:, 2 * pad:]
    return y[:rows, :width], y[rows:, :width] + y[:rows, pad:pad + width]


def kernel(n_inst, n_axial, order, kmat, s0, f, a_hbm, c_hbm, out,
           wa, wc, sb, rb, ob, rq, u, tx, tg, tw, tp, si, so, pm, sh, uin, fwd_out, fwd_in, xin, xout, inv,
           w_sem, x1_send, x1_recv, x2_send, x2_recv, g1_send, g1_recv, sh_sem, sc_send, sc_recv,
           g2_send, g2_recv, up_send, up_recv, fw_sem, in_sem):
    i = lax.axis_index("inst")
    a = lax.axis_index("axial")
    local, tiles, width = s0.shape
    per = tiles // n_inst
    cols = width // n_inst
    chips = n_inst // 2
    x, core = i // 2, lax.rem(i, 2)
    y, z = a // NZ, lax.rem(a, NZ)
    last = n_axial // NZ - 1
    rows = si.shape[1]
    chunks = rows // CHUNK
    both = 2 * local
    hub = core == 1
    lead = (z == NZ - 1) & (y < last)

    load_a = pltpu.make_async_copy(a_hbm, wa, w_sem.at[0])
    load_c = pltpu.make_async_copy(c_hbm, wc, w_sem.at[1])
    load_a.start()
    load_c.start()

    barrier = pltpu.get_barrier_semaphore()
    for d in range(1, n_inst):
        pl.semaphore_signal(barrier, inc=1, device_id={"inst": lax.rem(i + d, n_inst)}, device_id_type=MESH)

    @pl.when(hub)
    def _():
        for d in (1, NZ - 1):
            there = y * NZ + lax.rem(z + d, NZ)
            pl.semaphore_signal(barrier, inc=1, device_id={"axial": there}, device_id_type=MESH)

        @pl.when(lead)
        def _():
            for zz in range(NZ):
                pl.semaphore_signal(barrier, inc=1, device_id={"axial": (y + 1) * NZ + zz}, device_id_type=MESH)

        @pl.when(y > 0)
        def _():
            pl.semaphore_signal(barrier, inc=1, device_id={"axial": y * NZ - 1}, device_id_type=MESH)

    for t in range(tiles):
        sb[t, 0:local, :] = s0[:, t, :]
        sb[t, local:both, :] = f[:, t, :]
    row = lax.broadcasted_iota(jnp.int32, (cols, width), 0)
    col = lax.broadcasted_iota(jnp.int32, (cols, width), 1)
    tx[0] = jnp.where(col == row + i * cols, 1.0, 0.0).astype(F32)
    tx[1] = jnp.zeros((cols, width), F32)

    pl.semaphore_wait(barrier, n_inst - 1 + jnp.where(
        hub, 2 + jnp.where(lead, NZ, 0) + jnp.where(y > 0, 1, 0), 0))

    def first(d):
        peer = lax.rem(i + d, n_inst)
        return pltpu.make_async_remote_copy(
            src_ref=sb.at[pl.ds(per * peer, per)], dst_ref=rb.at[i],
            send_sem=x1_send.at[d], recv_sem=x1_recv.at[d],
            device_id={"inst": peer}, device_id_type=MESH)

    def second(d):
        peer = lax.rem(i + d, n_inst)
        return pltpu.make_async_remote_copy(
            src_ref=ob.at[peer], dst_ref=rq.at[pl.ds(per * i, per)],
            send_sem=x2_send.at[d], recv_sem=x2_recv.at[d],
            device_id={"inst": peer}, device_id_type=MESH)

    for d in range(1, n_inst):
        first(d).start()
    rb[i] = sb[pl.ds(per * i, per)]
    for t in range(tiles):
        pos = jnp.int32(0)
        for k in range(tiles):
            pos = jnp.where(order[k] == t, k, pos)
        inv[t] = pos

    load_a.wait()
    load_c.wait()

    def column_step(k, carry):
        t = order[k]
        c, ai = wc[t], wa[t]
        b = times(tx[...].reshape(2 * cols, width), c)
        p = -times(b[:cols], ai)
        tx[0] = p
        tx[1] = -times(p + b[cols:], ai)
        return carry

    lax.fori_loop(0, tiles // 2, column_step, 0)

    for d in range(1, n_inst):
        first(d).wait_recv()
    for t in range(per):
        mixed = jnp.dot(kmat[...], rb[:, t].reshape(both * n_inst, width),
                        precision=lax.Precision.HIGHEST, preferred_element_type=F32)
        ob[:, t] = mixed.reshape(n_inst, both, width)
    for d in range(1, n_inst):
        second(d).start()
    rq[pl.ds(per * i, per)] = ob[i]

    lax.fori_loop(tiles // 2, tiles, column_step, 0)

    def gather(xx, sender):
        return pltpu.make_async_remote_copy(
            src_ref=tx, dst_ref=tg.at[sender // 2, :, pl.ds(pl.multiple_of(lax.rem(sender, 2) * cols, 8), cols)],
            send_sem=g1_send.at[xx], recv_sem=g1_recv.at[sender],
            device_id={"inst": 2 * xx + 1}, device_id_type=MESH)

    for xx in range(chips):
        @pl.when(2 * xx + 1 != i)
        def _(xx=xx):
            gather(xx, i).start()

    for d in range(1, n_inst):
        second(d).wait_recv()

    lower = lax.broadcasted_iota(jnp.int32, (both, width), 0) >= local

    def data_step(k, v):
        t = order[k]
        r = times(rq[t] - times(v, wc[t]), wa[t])
        q = times(pltpu.roll(r, local, 0), wa[t])
        return jnp.where(lower, r - q, r)

    zero = jnp.zeros((both, width), F32)
    shift = lax.fori_loop(0, tiles, data_step, zero)

    share = pltpu.make_async_remote_copy(
        src_ref=sh.at[0], dst_ref=sh.at[1], send_sem=sh_sem.at[0], recv_sem=sh_sem.at[1],
        device_id={"inst": lax.rem(i + 1, n_inst)}, device_id_type=MESH)
    give = pltpu.make_async_remote_copy(
        src_ref=xout, dst_ref=xin, send_sem=in_sem.at[0], recv_sem=in_sem.at[1],
        device_id={"inst": lax.rem(i + n_inst - 1, n_inst)}, device_id_type=MESH)

    @pl.when(core == 0)
    def _():
        sh[0] = shift
        share.start()
        share.wait_send()
        give.wait_recv()

    @pl.when(hub)
    def _():
        tg[x, :, pl.ds(cols, cols)] = tx[...]
        for j in range(n_inst):
            @pl.when(j != i)
            def _(j=j):
                gather(0, j).wait_recv()
        for xx in range(chips):
            for part in range(2):
                store_map(tw, 2 * cols * xx, part, tg[xx, part])
        share.wait_recv()
        other = sh[1]
        bp = jnp.where(lower, pltpu.roll(shift, local, 0), other)
        bg = jnp.where(lower, shift, pltpu.roll(other, local, 0))

        def scan(c):
            part = pl.ds(pl.multiple_of(c * CHUNK, CHUNK), CHUNK)
            return pltpu.make_async_remote_copy(
                src_ref=so.at[:, part], dst_ref=si.at[:, part],
                send_sem=sc_send.at[c], recv_sem=sc_recv.at[c],
                device_id={"axial": y * NZ + lax.rem(z + 1, NZ)}, device_id_type=MESH)

        def spread(src, c, d):
            part = pl.ds(pl.multiple_of(c * CHUNK, CHUNK), CHUNK)
            return pltpu.make_async_remote_copy(
                src_ref=src.at[:, part], dst_ref=pm.at[x, :, part],
                send_sem=g2_send.at[d - 1, c], recv_sem=g2_recv.at[d - 1, c],
                device_id={"inst": lax.rem(i + 2 * d, n_inst)}, device_id_type=MESH)

        def down(zz):
            return pltpu.make_async_remote_copy(
                src_ref=uin.at[0], dst_ref=uin.at[1], send_sem=up_send.at[zz], recv_sem=up_recv.at[0],
                device_id={"axial": lax.rem(y + 1, last + 1) * NZ + zz}, device_id_type=MESH)

        hop = pltpu.make_async_remote_copy(
            src_ref=fwd_out, dst_ref=fwd_in, send_sem=fw_sem.at[0], recv_sem=fw_sem.at[1],
            device_id={"axial": y * NZ + lax.rem(z + 1, NZ)}, device_id_type=MESH)

        count = jnp.where(y == 0, 1, chunks)
        mapped = (y > 0) & (z > 0)

        @pl.when(z == 0)
        def _():
            so[0, 0:both] = bp
            so[1, 0:both] = bg
            so[:, both:both + 2 * cols] = tg[x]
            so[:, both + 2 * cols:] = jnp.zeros((2, rows - both - 2 * cols, width), F32)
            lax.fori_loop(0, count, lambda c, k: (scan(c).start(), k)[1], 0)

        @pl.when(z > 0)
        def _():
            empty = jnp.zeros((CHUNK - both, width), F32)
            add_p = jnp.concatenate([bp, empty], 0)
            add_g = jnp.concatenate([bg, empty], 0)

            def chunk_step(c, carry):
                scan(c).wait_recv()
                part = pl.ds(pl.multiple_of(c * CHUNK, CHUNK), CHUNK)

                @pl.when(mapped & jnp.logical_not(lead))
                def _():
                    for d in range(1, chips):
                        spread(si, c, d).start()

                p, g = through(tw, si[0, part], si[1, part])
                so[0, part] = p + jnp.where(c == 0, add_p, 0.0)
                so[1, part] = g + jnp.where(c == 0, add_g, 0.0)

                @pl.when(z < NZ - 1)
                def _():
                    scan(c).start()

                @pl.when(mapped & lead)
                def _():
                    for d in range(1, chips):
                        spread(so, c, d).start()
                return carry

            lax.fori_loop(0, count, chunk_step, 0)

        @pl.when(mapped)
        def _():
            @pl.when(lead)
            def _():
                pm[x] = so[...]

            @pl.when(jnp.logical_not(lead))
            def _():
                pm[x] = si[...]

            for d in range(1, chips):
                for c in range(chunks):
                    spread(si, c, d).wait_recv()
            for xx in range(chips):
                for part in range(2):
                    store_map(tp, 2 * cols * xx, part, pm[xx, part, both:both + 2 * cols])

        @pl.when((y == 0) & (z == NZ - 1))
        def _():
            uin[0] = so[:, 0:both]
            for zz in range(NZ):
                down(zz).start()

        @pl.when(y > 0)
        def _():
            down(0).wait_recv()

        def give_out(p, g):
            xout[...] = jnp.where(lower, pltpu.roll(g, local, 0), p)
            give.start()
            xin[...] = jnp.where(lower, g, pltpu.roll(p, local, 0))

        @pl.when(mapped)
        def _():
            p, g = through(tp, uin[1, 0], uin[1, 1])

            @pl.when(lead)
            def _():
                uin[0, 0] = p + so[0, 0:both]
                uin[0, 1] = g + so[1, 0:both]
                for zz in range(NZ):
                    down(zz).start()
                hop.wait_recv()
                give_out(fwd_in[0], fwd_in[1])

            @pl.when(jnp.logical_not(lead))
            def _():
                here_p, here_g = p + si[0, 0:both], g + si[1, 0:both]
                give_out(here_p, here_g)

                @pl.when((z == NZ - 2) & (y < last))
                def _():
                    next_p, next_g = through(tw, here_p, here_g)
                    fwd_out[0] = next_p + bp
                    fwd_out[1] = next_g + bg
                    hop.start()

        @pl.when((y > 0) & (z == 0))
        def _():
            give_out(uin[1, 0], uin[1, 1])

        @pl.when((y == 0) & (z == 0))
        def _():
            give_out(zero, zero)

        @pl.when((y == 0) & (z > 0))
        def _():
            give_out(si[0, 0:both], si[1, 0:both])

    def final_step(k, v):
        v = data_step(k, v)
        u[k] = v
        return v

    lax.fori_loop(0, tiles, final_step, xin[...])
    for t in range(tiles):
        out[:, t, :] = s0[:, t, :] + u[inv[t], local:both, :]

    for d in range(1, n_inst):
        first(d).wait_send()
        second(d).wait_send()
    for xx in range(chips):
        @pl.when(2 * xx + 1 != i)
        def _(xx=xx):
            gather(xx, i).wait_send()

    @pl.when(hub)
    def _():
        give.wait_send()
        count = jnp.where(y == 0, 1, chunks)

        @pl.when(z < NZ - 1)
        def _():
            lax.fori_loop(0, count, lambda c, k: (pltpu.make_async_remote_copy(
                src_ref=so.at[:, pl.ds(0, CHUNK)], dst_ref=si.at[:, pl.ds(0, CHUNK)],
                send_sem=sc_send.at[c], recv_sem=sc_recv.at[c],
                device_id={"axial": y * NZ + lax.rem(z + 1, NZ)}, device_id_type=MESH).wait_send(), k)[1], 0)

        @pl.when((y > 0) & (z > 0))
        def _():
            for d in range(1, chips):
                for c in range(chunks):
                    pltpu.make_async_remote_copy(
                        src_ref=si.at[:, pl.ds(0, CHUNK)], dst_ref=pm.at[x, :, pl.ds(0, CHUNK)],
                        send_sem=g2_send.at[d - 1, c], recv_sem=g2_recv.at[d - 1, c],
                        device_id={"inst": lax.rem(i + 2 * d, n_inst)}, device_id_type=MESH).wait_send()

        @pl.when(lead)
        def _():
            for zz in range(NZ):
                pltpu.make_async_remote_copy(
                    src_ref=uin.at[0], dst_ref=uin.at[1], send_sem=up_send.at[zz], recv_sem=up_recv.at[0],
                    device_id={"axial": lax.rem(y + 1, last + 1) * NZ + zz}, device_id_type=MESH).wait_send()

        @pl.when((y > 0) & (z == NZ - 2) & (y < last))
        def _():
            pltpu.make_async_remote_copy(
                src_ref=fwd_out, dst_ref=fwd_in, send_sem=fw_sem.at[0], recv_sem=fw_sem.at[1],
                device_id={"axial": y * NZ + lax.rem(z + 1, NZ)}, device_id_type=MESH).wait_send()


def solution(mesh):
    n_inst, n_axial = mesh.shape["inst"], mesh.shape["axial"]

    def on_device(flow_state, forcing, tile_inverse, coupling, sweep_order):
        local, tiles, width = flow_state.shape
        per = tiles // n_inst
        cols = width // n_inst
        chips = n_inst // 2
        pad = -(-width // 128) * 128
        both = 2 * local
        rows = -(-(both + 2 * cols) // CHUNK) * CHUNK
        chunks = rows // CHUNK
        kmat = jnp.asarray(exchange_matrix(local * n_inst, n_inst))
        vmem = pl.BlockSpec(memory_space=pltpu.VMEM)
        dma = pltpu.SemaphoreType.DMA
        return pl.pallas_call(
            functools.partial(kernel, n_inst, n_axial),
            out_shape=jax.ShapeDtypeStruct(flow_state.shape, F32),
            in_specs=[pl.BlockSpec(memory_space=pltpu.SMEM), vmem, vmem, vmem,
                      pl.BlockSpec(memory_space=pl.ANY), pl.BlockSpec(memory_space=pl.ANY)],
            out_specs=vmem,
            scratch_shapes=[
                pltpu.VMEM((tiles, width, width), BF16),
                pltpu.VMEM((tiles, width, width), BF16),
                pltpu.VMEM((tiles, both, width), F32),
                pltpu.VMEM((n_inst, per, both, width), F32),
                pltpu.VMEM((n_inst, per, both, width), F32),
                pltpu.VMEM((tiles, both, width), F32),
                pltpu.VMEM((tiles, both, width), F32),
                pltpu.VMEM((2, cols, width), F32),
                pltpu.VMEM((chips, 2, 2 * cols, width), F32),
                pltpu.VMEM((width, 4 * pad), BF16),
                pltpu.VMEM((width, 4 * pad), BF16),
                pltpu.VMEM((2, rows, width), F32),
                pltpu.VMEM((2, rows, width), F32),
                pltpu.VMEM((chips, 2, rows, width), F32),
                pltpu.VMEM((2, both, width), F32),
                pltpu.VMEM((2, 2, both, width), F32),
                pltpu.VMEM((2, both, width), F32),
                pltpu.VMEM((2, both, width), F32),
                pltpu.VMEM((both, width), F32),
                pltpu.VMEM((both, width), F32),
                pltpu.SMEM((tiles,), jnp.int32),
                dma((2,)),
                dma((n_inst,)), dma((n_inst,)), dma((n_inst,)), dma((n_inst,)),
                dma((chips,)), dma((n_inst,)),
                dma((2,)),
                dma((chunks,)), dma((chunks,)),
                dma((chips - 1, chunks)), dma((chips - 1, chunks)),
                dma((NZ,)), dma((1,)),
                dma((2,)), dma((2,)),
            ],
            compiler_params=pltpu.CompilerParams(collective_id=0, has_side_effects=True),
        )(sweep_order, kmat, flow_state, forcing, tile_inverse, coupling)

    return jax.shard_map(
        on_device,
        mesh=mesh,
        in_specs=(P("inst", "axial", None), P("inst", "axial", None), P("axial", None, None),
                  P("axial", None, None), P("axial")),
        out_specs=P("inst", "axial", None),
        check_vma=False,
    )
```

```python
import functools

import jax
import jax.numpy as jnp
import numpy as np
from jax import lax
from jax.experimental import pallas as pl
from jax.experimental.pallas import tpu as pltpu
from jax.sharding import PartitionSpec as P

ITERS = 2
SPECTRAL_GAIN = 2.0
NZ = 8
MIX_AT = 12
CHUNK = 16
MESH = pl.DeviceIdType.MESH
F32, BF16 = jnp.float32, jnp.bfloat16
NT = (((1,), (1,)), ((), ()))
NN = (((1,), (0,)), ((), ()))


def exchange_matrix(period, groups):
    idx = np.arange(period)
    dist = idx[:, None] - idx[None, :]
    angle = np.pi * dist / period
    safe = np.where(dist == 0, 1.0, np.sin(angle))
    deriv = np.where(dist == 0, 0.0, 0.5 * (1.0 - 2.0 * (dist % 2)) * np.cos(angle) / safe)
    e = deriv * (SPECTRAL_GAIN / period) + np.eye(period)
    whole = np.block([[-e @ e, e], [-2.0 * e, 2.0 * np.eye(period)]])
    local = period // groups
    given = [part * period + dev * local + n for dev in range(groups) for part in range(2) for n in range(local)]
    wide = 2 * local
    made = [part * period + chip * wide + n for chip in range(groups // 2) for part in range(2) for n in range(wide)]
    return whole[np.ix_(made, given)].astype(np.float32)


def halves(x):
    high = x.astype(BF16)
    low = (x - high.astype(F32)).astype(BF16)
    return high, low


def split(x):
    high = x.astype(BF16).astype(F32)
    return jnp.concatenate([high, x - high], 0).astype(BF16)


def times(x, w, dims=NT):
    m = x.shape[0]
    y = lax.dot_general(split(x), w, dims, preferred_element_type=F32)
    return y[:m] + y[m:]


def store_map(dst, row, part, block):
    pad = dst.shape[1] // 4
    rows, width = block.shape
    high, low = halves(block)
    dst[pl.ds(row, rows), part * pad:part * pad + width] = high
    dst[pl.ds(row, rows), (2 + part) * pad:(2 + part) * pad + width] = low


def through(m, p, g):
    rows, width = p.shape
    pad = m.shape[1] // 4
    y = lax.dot_general(split(jnp.concatenate([p, g], 0)), m[...], NN, preferred_element_type=F32)
    y = y[:2 * rows] + y[2 * rows:]
    y = y[:, :2 * pad] + y[:, 2 * pad:]
    return y[:rows, :width], y[rows:, :width] + y[:rows, pad:pad + width]


def kernel(n_inst, n_axial, order, kmat, s0, f, a_hbm, c_hbm, out,
           wa, wc, sb, rb, ob, rq, u, tx, txm, tg, tgm, tw, tp, si, so, pm, sh, uin, fwd, vin, inv,
           w_sem, x1_send, x1_recv, x2_send, x2_recv, g1_send, g1_recv, gm_send, gm_recv, pair_sem,
           sc_send, sc_recv, sd_sem, g2_send, g2_recv, up_send, up_recv, fw_sem):
    i = lax.axis_index("inst")
    a = lax.axis_index("axial")
    local, tiles, width = s0.shape
    chips = n_inst // 2
    per = tiles // chips
    mid = tiles // 2
    cols = width // n_inst
    block = 2 * cols
    both = 2 * local
    x, core = i // 2, lax.rem(i, 2)
    y, z = a // NZ, lax.rem(a, NZ)
    last = n_axial // NZ - 1
    chunks = block // CHUNK
    hub = core == 1
    lead = (z == NZ - 1) & (y < last)
    mapped = (y > 0) & (z > 0)
    data = pl.ds(block, both)

    load_a = pltpu.make_async_copy(a_hbm, wa, w_sem.at[0])
    load_c = pltpu.make_async_copy(c_hbm, wc, w_sem.at[1])
    load_a.start()
    load_c.start()

    def remote(src, dst, send, recv, **there):
        return pltpu.make_async_remote_copy(
            src_ref=src, dst_ref=dst, send_sem=send, recv_sem=recv, device_id=there, device_id_type=MESH)

    barrier = pltpu.get_barrier_semaphore()
    for d in range(1, n_inst):
        pl.semaphore_signal(barrier, inc=1, device_id={"inst": lax.rem(i + d, n_inst)}, device_id_type=MESH)

    @pl.when(hub)
    def _():
        for d in (1, NZ - 1):
            there = y * NZ + lax.rem(z + d, NZ)
            pl.semaphore_signal(barrier, inc=1, device_id={"axial": there}, device_id_type=MESH)

        @pl.when(lead)
        def _():
            for zz in range(NZ):
                pl.semaphore_signal(barrier, inc=1, device_id={"axial": (y + 1) * NZ + zz}, device_id_type=MESH)

        @pl.when(y > 0)
        def _():
            pl.semaphore_signal(barrier, inc=1, device_id={"axial": y * NZ - 1}, device_id_type=MESH)

    for t in range(tiles):
        sb[t, 0:local, :] = s0[:, t, :]
        sb[t, local:both, :] = f[:, t, :]
    row = lax.broadcasted_iota(jnp.int32, (cols, width), 0)
    col = lax.broadcasted_iota(jnp.int32, (cols, width), 1)
    tx[0] = jnp.where(col == row + i * cols, 1.0, 0.0).astype(F32)
    tx[1] = jnp.zeros((cols, width), F32)

    pl.semaphore_wait(barrier, n_inst - 1 + jnp.where(
        hub, 2 + jnp.where(lead, NZ, 0) + jnp.where(y > 0, 1, 0), 0))

    def first(xx, sender):
        return remote(sb.at[pl.ds(per * xx, per)], rb.at[sender], x1_send.at[xx], x1_recv.at[sender], inst=2 * xx)

    def second(d):
        xx = lax.rem(x + d, chips)
        return remote(ob.at[xx], rq.at[pl.ds(per * x, per)], x2_send.at[d], x2_recv.at[d], inst=2 * xx)

    def gather(src, dst, send, recv, xx, sender):
        half = pl.ds(pl.multiple_of(lax.rem(sender, 2) * cols, 8), cols)
        return remote(src, dst.at[sender // 2, :, half], send.at[xx], recv.at[sender], inst=2 * xx + 1)

    def whole(xx, sender):
        return gather(tx, tg, g1_send, g1_recv, xx, sender)

    def halfway(xx, sender):
        return gather(txm, tgm, gm_send, gm_recv, xx, sender)

    def to_hubs(copy):
        for xx in range(chips):
            @pl.when(2 * xx + 1 != i)
            def _(xx=xx):
                copy(xx, i).start()

    other = i + 1 - 2 * core
    pass_rq = remote(rq, rq, pair_sem.at[0], pair_sem.at[1], inst=other)
    share = remote(sh.at[0], sh.at[1], pair_sem.at[2], pair_sem.at[3], inst=other)
    give = remote(vin.at[0], vin.at[1], pair_sem.at[4], pair_sem.at[5], inst=other)
    early = remote(u.at[pl.ds(0, mid)], u.at[pl.ds(0, mid)], pair_sem.at[6], pair_sem.at[7], inst=other)
    late = remote(u.at[pl.ds(mid, mid)], u.at[pl.ds(mid, mid)], pair_sem.at[8], pair_sem.at[9], inst=other)

    for xx in range(chips):
        @pl.when(2 * xx != i)
        def _(xx=xx):
            first(xx, i).start()
    for t in range(tiles):
        pos = jnp.int32(0)
        for k in range(tiles):
            pos = jnp.where(order[k] == t, k, pos)
        inv[t] = pos

    load_a.wait()
    load_c.wait()

    def column_step(k, carry):
        t = order[k]
        c, ai = wc[t], wa[t]
        b = times(tx[...].reshape(block, width), c)
        p = -times(b[:cols], ai)
        tx[0] = p
        tx[1] = -times(p + b[cols:], ai)
        return carry

    lax.fori_loop(0, mid, column_step, 0)
    txm[...] = tx[...]
    lax.fori_loop(mid, MIX_AT, column_step, 0)

    @pl.when(core == 0)
    def _():
        rb[i] = sb[pl.ds(per * x, per)]
        for j in range(n_inst):
            @pl.when(j != i)
            def _(j=j):
                first(0, j).wait_recv()
        for t in range(per):
            mixed = jnp.dot(kmat[...], rb[:, t].reshape(both * n_inst, width),
                            precision=lax.Precision.HIGHEST, preferred_element_type=F32)
            ob[:, t] = mixed.reshape(chips, 2 * both, width)
        for d in range(1, chips):
            second(d).start()
        rq[pl.ds(per * x, per)] = ob[x]

    lax.fori_loop(MIX_AT, tiles, column_step, 0)
    to_hubs(whole)

    def data_step(k, v):
        t = order[k]
        r = times(rq[t] - times(v, wc[t]), wa[t])
        q = times(r[:both], wa[t])
        return jnp.concatenate([r[:both], r[both:] - q], 0)

    def final_step(k, v):
        v = data_step(k, v)
        u[k] = v[both:]
        return v

    zero = jnp.zeros((both, width), F32)

    @pl.when(core == 0)
    def _():
        for d in range(1, chips):
            second(d).wait_recv()
        pass_rq.start()
        v = lax.fori_loop(0, mid, data_step, jnp.zeros((2 * both, width), F32))
        sh[0, 0] = v
        sh[0, 1] = lax.fori_loop(mid, tiles, data_step, v)
        share.start()
        to_hubs(halfway)
        give.wait_recv()
        lax.fori_loop(0, mid, final_step, vin[1])
        early.start()
        late.wait_recv()
        for t in range(tiles):
            out[:, t, :] = s0[:, t, :] + u[inv[t], 0:local, :]
        early.wait_send()
        share.wait_send()
        pass_rq.wait_send()
        for d in range(1, chips):
            second(d).wait_send()

    @pl.when(hub)
    def _():
        def scan(c):
            part = pl.ds(pl.multiple_of(c * CHUNK, CHUNK), CHUNK)
            return remote(so.at[:, part], si.at[:, part], sc_send.at[c], sc_recv.at[c],
                          axial=y * NZ + lax.rem(z + 1, NZ))

        scan_data = remote(so.at[:, data], si.at[:, data], sd_sem.at[0], sd_sem.at[1],
                           axial=y * NZ + lax.rem(z + 1, NZ))

        def spread(src, c, d):
            part = pl.ds(pl.multiple_of(c * CHUNK, CHUNK), CHUNK)
            return remote(src.at[:, part], pm.at[x, :, part], g2_send.at[d - 1, c], g2_recv.at[d - 1, c],
                          inst=lax.rem(i + 2 * d, n_inst))

        def down(zz):
            return remote(uin.at[0], uin.at[1], up_send.at[zz], up_recv.at[0],
                          axial=lax.rem(y + 1, last + 1) * NZ + zz)

        hop = remote(fwd.at[0], fwd.at[1], fw_sem.at[0], fw_sem.at[1], axial=y * NZ + lax.rem(z + 1, NZ))
        count = jnp.where(y == 0, 0, chunks)

        tg[x, :, pl.ds(cols, cols)] = tx[...]
        tgm[x, :, pl.ds(cols, cols)] = txm[...]
        whole(0, i - 1).wait_recv()

        @pl.when((z == 0) & (y > 0))
        def _():
            so[:, 0:block] = tg[x]
            lax.fori_loop(0, count, lambda c, k: (scan(c).start(), k)[1], 0)

        for j in range(n_inst):
            @pl.when((j != i) & (j != i - 1))
            def _(j=j):
                whole(0, j).wait_recv()

        @pl.when(z > 0)
        def _():
            for xx in range(chips):
                for part in range(2):
                    store_map(tw, block * xx, part, tg[xx, part])

        to_hubs(halfway)

        @pl.when(z > 0)
        def _():
            def chunk_step(c, carry):
                scan(c).wait_recv()
                part = pl.ds(pl.multiple_of(c * CHUNK, CHUNK), CHUNK)

                @pl.when(jnp.logical_not(lead))
                def _():
                    for d in range(1, chips):
                        spread(si, c, d).start()

                @pl.when((y < last) | (z < NZ - 1))
                def _():
                    p, g = through(tw, si[0, part], si[1, part])
                    so[0, part] = p
                    so[1, part] = g

                @pl.when(z < NZ - 1)
                def _():
                    scan(c).start()

                @pl.when(lead)
                def _():
                    for d in range(1, chips):
                        spread(so, c, d).start()
                return carry

            lax.fori_loop(0, count, chunk_step, 0)

        share.wait_recv()
        bp, bg = sh[1, 1, 0:both], sh[1, 1, both:]

        @pl.when(z == 0)
        def _():
            so[0, data] = bp
            so[1, data] = bg
            scan_data.start()

        @pl.when(z > 0)
        def _():
            scan_data.wait_recv()

            @pl.when((y < last) | (z < NZ - 1))
            def _():
                p, g = through(tw, si[0, data], si[1, data])
                so[0, data] = p + bp
                so[1, data] = g + bg

            @pl.when(z < NZ - 1)
            def _():
                scan_data.start()

        @pl.when((y == 0) & (z == NZ - 1))
        def _():
            uin[0] = so[:, data]
            for zz in range(NZ):
                down(zz).start()

        @pl.when(mapped)
        def _():
            @pl.when(lead)
            def _():
                pm[x] = so[:, 0:block]

            @pl.when(jnp.logical_not(lead))
            def _():
                pm[x] = si[:, 0:block]

            for d in range(1, chips):
                for c in range(chunks):
                    spread(si, c, d).wait_recv()
            for xx in range(chips):
                for part in range(2):
                    store_map(tp, block * xx, part, pm[xx, part])

        def give_out(p, g):
            vin[0, 0:both] = p
            vin[0, both:] = g
            give.start()

        @pl.when(y == 0)
        def _():
            @pl.when(z == 0)
            def _():
                give_out(zero, zero)

            @pl.when(z > 0)
            def _():
                give_out(si[0, data], si[1, data])

        for j in range(n_inst):
            @pl.when(j != i)
            def _(j=j):
                halfway(0, j).wait_recv()

        def middle_map():
            for xx in range(chips):
                for part in range(2):
                    store_map(tw, block * xx, part, tgm[xx, part])

        @pl.when((y == 0) | (z != NZ - 2) | (y == last))
        def _():
            middle_map()

        @pl.when(y > 0)
        def _():
            down(0).wait_recv()

        @pl.when(mapped)
        def _():
            p, g = through(tp, uin[1, 0], uin[1, 1])

            @pl.when(lead)
            def _():
                uin[0, 0] = p + so[0, data]
                uin[0, 1] = g + so[1, data]
                for zz in range(NZ):
                    down(zz).start()
                hop.wait_recv()
                give_out(fwd[1, 0], fwd[1, 1])

            @pl.when(jnp.logical_not(lead))
            def _():
                here_p, here_g = p + si[0, data], g + si[1, data]
                give_out(here_p, here_g)

                @pl.when((z == NZ - 2) & (y < last))
                def _():
                    next_p, next_g = through(tw, here_p, here_g)
                    fwd[0, 0] = next_p + bp
                    fwd[0, 1] = next_g + bg
                    hop.start()
                    middle_map()

        @pl.when((y > 0) & (z == 0))
        def _():
            give_out(uin[1, 0], uin[1, 1])

        p, g = through(tw, vin[0, 0:both], vin[0, both:])
        pass_rq.wait_recv()
        lax.fori_loop(mid, tiles, final_step, jnp.concatenate([p, g], 0) + sh[1, 0])
        late.start()
        early.wait_recv()
        for t in range(tiles):
            out[:, t, :] = s0[:, t, :] + u[inv[t], local:both, :]

        late.wait_send()
        give.wait_send()

        @pl.when(z < NZ - 1)
        def _():
            scan_data.wait_send()
            lax.fori_loop(0, count, lambda c, k: (scan(c).wait_send(), k)[1], 0)

        @pl.when(mapped)
        def _():
            for d in range(1, chips):
                for c in range(chunks):
                    spread(si, c, d).wait_send()

        @pl.when(lead)
        def _():
            for zz in range(NZ):
                down(zz).wait_send()

        @pl.when((y > 0) & (z == NZ - 2) & (y < last))
        def _():
            hop.wait_send()

    for xx in range(chips):
        @pl.when(2 * xx != i)
        def _(xx=xx):
            first(xx, i).wait_send()

        @pl.when(2 * xx + 1 != i)
        def _(xx=xx):
            whole(xx, i).wait_send()
            halfway(xx, i).wait_send()


def solution(mesh):
    n_inst, n_axial = mesh.shape["inst"], mesh.shape["axial"]

    def on_device(flow_state, forcing, tile_inverse, coupling, sweep_order):
        local, tiles, width = flow_state.shape
        chips = n_inst // 2
        per = tiles // chips
        cols = width // n_inst
        block = 2 * cols
        pad = -(-width // 128) * 128
        both = 2 * local
        chunks = block // CHUNK
        kmat = jnp.asarray(exchange_matrix(local * n_inst, n_inst))
        vmem = pl.BlockSpec(memory_space=pltpu.VMEM)
        dma = pltpu.SemaphoreType.DMA
        return pl.pallas_call(
            functools.partial(kernel, n_inst, n_axial),
            out_shape=jax.ShapeDtypeStruct(flow_state.shape, F32),
            in_specs=[pl.BlockSpec(memory_space=pltpu.SMEM), vmem, vmem, vmem,
                      pl.BlockSpec(memory_space=pl.ANY), pl.BlockSpec(memory_space=pl.ANY)],
            out_specs=vmem,
            scratch_shapes=[
                pltpu.VMEM((tiles, width, width), BF16),
                pltpu.VMEM((tiles, width, width), BF16),
                pltpu.VMEM((tiles, both, width), F32),
                pltpu.VMEM((n_inst, per, both, width), F32),
                pltpu.VMEM((chips, per, 2 * both, width), F32),
                pltpu.VMEM((tiles, 2 * both, width), F32),
                pltpu.VMEM((tiles, both, width), F32),
                pltpu.VMEM((2, cols, width), F32),
                pltpu.VMEM((2, cols, width), F32),
                pltpu.VMEM((chips, 2, block, width), F32),
                pltpu.VMEM((chips, 2, block, width), F32),
                pltpu.VMEM((width, 4 * pad), BF16),
                pltpu.VMEM((width, 4 * pad), BF16),
                pltpu.VMEM((2, block + both, width), F32),
                pltpu.VMEM((2, block + both, width), F32),
                pltpu.VMEM((chips, 2, block, width), F32),
                pltpu.VMEM((2, 2, 2 * both, width), F32),
                pltpu.VMEM((2, 2, both, width), F32),
                pltpu.VMEM((2, 2, both, width), F32),
                pltpu.VMEM((2, 2 * both, width), F32),
                pltpu.SMEM((tiles,), jnp.int32),
                dma((2,)),
                dma((chips,)), dma((n_inst,)), dma((chips,)), dma((chips,)),
                dma((chips,)), dma((n_inst,)), dma((chips,)), dma((n_inst,)),
                dma((10,)),
                dma((chunks,)), dma((chunks,)), dma((2,)),
                dma((chips - 1, chunks)), dma((chips - 1, chunks)),
                dma((NZ,)), dma((1,)),
                dma((2,)),
            ],
            compiler_params=pltpu.CompilerParams(collective_id=0, has_side_effects=True),
        )(sweep_order, kmat, flow_state, forcing, tile_inverse, coupling)

    return jax.shard_map(
        on_device,
        mesh=mesh,
        in_specs=(P("inst", "axial", None), P("inst", "axial", None), P("axial", None, None),
                  P("axial", None, None), P("axial")),
        out_specs=P("inst", "axial", None),
        check_vma=False,
    )
```

```python
import functools

import jax
import jax.numpy as jnp
import numpy as np
from jax import lax
from jax.experimental import pallas as pl
from jax.experimental.pallas import tpu as pltpu
from jax.sharding import PartitionSpec as P

ITERS = 2
SPECTRAL_GAIN = 2.0
NZ = 8
UNROLL = 4
CHUNK = 16
MESH = pl.DeviceIdType.MESH
F32, BF16 = jnp.float32, jnp.bfloat16
NT = (((1,), (1,)), ((), ()))
NN = (((1,), (0,)), ((), ()))


def exchange_matrix(period, groups):
    idx = np.arange(period)
    dist = idx[:, None] - idx[None, :]
    angle = np.pi * dist / period
    safe = np.where(dist == 0, 1.0, np.sin(angle))
    deriv = np.where(dist == 0, 0.0, 0.5 * (1.0 - 2.0 * (dist % 2)) * np.cos(angle) / safe)
    e = deriv * (SPECTRAL_GAIN / period) + np.eye(period)
    whole = np.block([[-e @ e, e], [-2.0 * e, 2.0 * np.eye(period)]])
    local = period // groups
    given = [part * period + dev * local + n for dev in range(groups) for part in range(2) for n in range(local)]
    wide = 2 * local
    made = [part * period + chip * wide + n for chip in range(groups // 2) for part in range(2) for n in range(wide)]
    return whole[np.ix_(made, given)].astype(np.float32)


def halves(x):
    high = x.astype(BF16)
    low = (x - high.astype(F32)).astype(BF16)
    return high, low


def split(x):
    high = x.astype(BF16).astype(F32)
    return jnp.concatenate([high, x - high], 0).astype(BF16)


def times(x, w, dims=NT):
    m = x.shape[0]
    y = lax.dot_general(split(x), w, dims, preferred_element_type=F32)
    return y[:m] + y[m:]


def store_map(dst, row, part, block):
    pad = dst.shape[1] // 4
    rows, width = block.shape
    high, low = halves(block)
    dst[pl.ds(row, rows), part * pad:part * pad + width] = high
    dst[pl.ds(row, rows), (2 + part) * pad:(2 + part) * pad + width] = low


def through(m, p, g):
    rows, width = p.shape
    pad = m.shape[1] // 4
    y = lax.dot_general(split(jnp.concatenate([p, g], 0)), m[...], NN, preferred_element_type=F32)
    y = y[:2 * rows] + y[2 * rows:]
    y = y[:, :2 * pad] + y[:, 2 * pad:]
    return y[:rows, :width], y[rows:, :width] + y[:rows, pad:pad + width]


def kernel(n_inst, n_axial, order, kmat, s0, f, a_hbm, c_hbm, out,
           wa, wc, sb, rb, ob, rq, u, tx, txm, tg, tgm, raw, rawm, tw, tp, tq, si, so, pm, uin, vin, at, nt, ya, inv,
           w_sem, x1_send, x1_recv, x2_send, x2_recv, g1_send, g1_recv, gm_send, gm_recv, r1_send, r1_recv, rm_send, rm_recv, pair_sem,
           sc_send, sc_recv, sd_sem, g2_send, g2_recv, up_send, up_recv):
    i = lax.axis_index("inst")
    a = lax.axis_index("axial")
    local, tiles, width = s0.shape
    chips = n_inst // 2
    per = tiles // chips
    mid = tiles // 2
    cols = width // n_inst
    block = 2 * cols
    both = 2 * local
    x, core = i // 2, lax.rem(i, 2)
    y, z = a // NZ, lax.rem(a, NZ)
    last = n_axial // NZ - 1
    chunks = block // CHUNK
    hub = core == 1
    lead = (z == NZ - 1) & (y < last)
    mapped = (y > 0) & (z > 0)
    data = pl.ds(block, both)

    load_a = pltpu.make_async_copy(a_hbm, wa, w_sem.at[0])
    load_c = pltpu.make_async_copy(c_hbm, wc, w_sem.at[1])
    load_a.start()
    load_c.start()

    def remote(src, dst, send, recv, **there):
        return pltpu.make_async_remote_copy(
            src_ref=src, dst_ref=dst, send_sem=send, recv_sem=recv, device_id=there, device_id_type=MESH)

    barrier = pltpu.get_barrier_semaphore()
    for d in range(1, n_inst):
        pl.semaphore_signal(barrier, inc=1, device_id={"inst": lax.rem(i + d, n_inst)}, device_id_type=MESH)

    @pl.when(hub)
    def _():
        for d in (1, NZ - 1):
            there = y * NZ + lax.rem(z + d, NZ)
            pl.semaphore_signal(barrier, inc=1, device_id={"axial": there}, device_id_type=MESH)

        @pl.when(lead)
        def _():
            for zz in range(NZ):
                pl.semaphore_signal(barrier, inc=1, device_id={"axial": (y + 1) * NZ + zz}, device_id_type=MESH)

        @pl.when(y > 0)
        def _():
            pl.semaphore_signal(barrier, inc=1, device_id={"axial": y * NZ - 1}, device_id_type=MESH)

    for t in range(tiles):
        sb[t, 0:local, :] = s0[:, t, :]
        sb[t, local:both, :] = f[:, t, :]
    row = lax.broadcasted_iota(jnp.int32, (cols, width), 0)
    col = lax.broadcasted_iota(jnp.int32, (cols, width), 1)
    tx[0, 0:cols] = jnp.where(col == row + i * cols, 1.0, 0.0).astype(F32)
    tx[0, cols:] = jnp.zeros((both, width), F32)
    tx[1] = jnp.zeros((cols + both, width), F32)

    pl.semaphore_wait(barrier, n_inst - 1 + jnp.where(
        hub, 2 + jnp.where(lead, NZ, 0) + jnp.where(y > 0, 1, 0), 0))

    def first(xx, sender):
        return remote(sb.at[pl.ds(per * xx, per)], rb.at[sender], x1_send.at[xx], x1_recv.at[sender], inst=2 * xx)

    def second(d):
        xx = lax.rem(x + d, chips)
        return remote(ob.at[xx], rq.at[pl.ds(per * x, per)], x2_send.at[d], x2_recv.at[d], inst=2 * xx)

    def gather(src, dst, send, recv, xx, sender):
        half = pl.ds(pl.multiple_of(lax.rem(sender, 2) * cols, 8), cols)
        return remote(src.at[:, 0:cols], dst.at[sender // 2, :, half], send.at[xx], recv.at[sender], inst=2 * xx + 1)

    def whole(xx, sender):
        return gather(tx, tg, g1_send, g1_recv, xx, sender)

    def halfway(xx, sender):
        return gather(txm, tgm, gm_send, gm_recv, xx, sender)

    def raw_whole(xx, sender):
        return remote(tx.at[:, cols:cols + both], raw.at[sender], r1_send.at[xx], r1_recv.at[sender], inst=2 * xx + 1)

    def raw_half(xx, sender):
        return remote(txm.at[:, cols:cols + both], rawm.at[sender], rm_send.at[xx], rm_recv.at[sender], inst=2 * xx + 1)

    def to_hubs(copy):
        for xx in range(chips):
            @pl.when(2 * xx + 1 != i)
            def _(xx=xx):
                copy(xx, i).start()

    other = i + 1 - 2 * core
    pass_rq = remote(rq, rq, pair_sem.at[0], pair_sem.at[1], inst=other)
    give = remote(vin.at[0], vin.at[1], pair_sem.at[4], pair_sem.at[5], inst=other)
    early = remote(u.at[pl.ds(0, mid)], u.at[pl.ds(0, mid)], pair_sem.at[6], pair_sem.at[7], inst=other)
    late = remote(u.at[pl.ds(mid, mid)], u.at[pl.ds(mid, mid)], pair_sem.at[8], pair_sem.at[9], inst=other)

    for xx in range(chips):
        @pl.when(2 * xx != i)
        def _(xx=xx):
            first(xx, i).start()
    for t in range(tiles):
        pos = jnp.int32(0)
        for k in range(tiles):
            pos = jnp.where(order[k] == t, k, pos)
        inv[t] = pos

    load_a.wait()
    load_c.wait()

    def column_step(k):
        t = order[k]
        c, ai = wc[t], wa[t]
        b = times(tx[...].reshape(2 * (cols + both), width), c)
        p = times(jnp.concatenate([-b[:cols], sb[t] - b[cols:cols + both]], 0), ai)
        tx[0] = p
        tx[1] = -times(p + b[cols + both:], ai)

    def column_steps(first_tile, count):
        def steps(n, carry):
            for j in range(UNROLL):
                column_step(first_tile + n * UNROLL + j)
            return carry
        lax.fori_loop(0, count // UNROLL, steps, 0)

    column_steps(0, mid)
    txm[...] = tx[...]
    column_steps(mid, tiles - mid)
    to_hubs(whole)
    to_hubs(raw_whole)

    pad = nt.shape[2] // 2

    def prepare(n, carry):
        t = order[mid * core + n]
        turned = wa[t].T
        at[n] = turned
        high, low = halves(lax.dot_general(wc[t].T, turned, NN, preferred_element_type=F32))
        nt[n, :, 0:width] = high
        nt[n, :, pad:pad + width] = low
        return carry

    def drive(n, carry):
        ya[n] = times(rq[order[mid * core + n]], at[n], NN)
        return carry

    def final_step(n, v):
        m = lax.dot_general(split(v), nt[n], NN, preferred_element_type=F32)
        m = m[:2 * both] + m[2 * both:]
        r = ya[n] - (m[:, :width] + m[:, pad:pad + width])
        g = r[both:] - times(r[:both], at[n], NN)
        u[mid * core + n] = g
        return jnp.concatenate([r[:both], g], 0)

    zero = jnp.zeros((both, width), F32)

    @pl.when(core == 0)
    def _():
        rb[i] = sb[pl.ds(per * x, per)]
        for j in range(n_inst):
            @pl.when(j != i)
            def _(j=j):
                first(0, j).wait_recv()
        for t in range(per):
            mixed = jnp.dot(kmat[...], rb[:, t].reshape(both * n_inst, width),
                            precision=lax.Precision.HIGHEST, preferred_element_type=F32)
            ob[:, t] = mixed.reshape(chips, 2 * both, width)
        lax.fori_loop(0, mid, prepare, 0)
        for d in range(1, chips):
            second(d).start()
        rq[pl.ds(per * x, per)] = ob[x]
        to_hubs(raw_half)
        to_hubs(halfway)
        for d in range(1, chips):
            second(d).wait_recv()
        pass_rq.start()
        lax.fori_loop(0, mid, drive, 0)
        give.wait_recv()
        lax.fori_loop(0, mid, final_step, vin[1])
        early.start()
        late.wait_recv()
        for t in range(tiles):
            out[:, t, :] = s0[:, t, :] + u[inv[t], 0:local, :]
        early.wait_send()
        pass_rq.wait_send()
        for d in range(1, chips):
            second(d).wait_send()

    @pl.when(hub)
    def _():
        def scan(c):
            part = pl.ds(pl.multiple_of(c * CHUNK, CHUNK), CHUNK)
            return remote(so.at[:, part], si.at[:, part], sc_send.at[c], sc_recv.at[c],
                          axial=y * NZ + lax.rem(z + 1, NZ))

        scan_data = remote(so.at[:, data], si.at[:, data], sd_sem.at[0], sd_sem.at[1],
                           axial=y * NZ + lax.rem(z + 1, NZ))

        def spread(src, c, d):
            part = pl.ds(pl.multiple_of(c * CHUNK, CHUNK), CHUNK)
            return remote(src.at[:, part], pm.at[x, :, part], g2_send.at[d - 1, c], g2_recv.at[d - 1, c],
                          inst=lax.rem(i + 2 * d, n_inst))

        def down(zz):
            return remote(uin.at[0], uin.at[1], up_send.at[zz], up_recv.at[0],
                          axial=lax.rem(y + 1, last + 1) * NZ + zz)

        def mix(rows):
            made = [jnp.dot(kmat[pl.ds(pl.multiple_of(2 * both * x, 8), 2 * both)], rows[:, n].reshape(both * n_inst, width),
                            precision=lax.Precision.HIGHEST, preferred_element_type=F32) for n in range(2)]
            return made[0][:both], made[0][both:] + made[1][:both]

        count = jnp.where(y == 0, 0, chunks)

        tg[x, :, pl.ds(cols, cols)] = tx[:, 0:cols]
        tgm[x, :, pl.ds(cols, cols)] = txm[:, 0:cols]
        raw[i] = tx[:, cols:]
        rawm[i] = txm[:, cols:]
        whole(0, i - 1).wait_recv()

        @pl.when((z == 0) & (y > 0))
        def _():
            so[:, 0:block] = tg[x]
            lax.fori_loop(0, count, lambda c, k: (scan(c).start(), k)[1], 0)

        lax.fori_loop(0, mid, prepare, 0)
        for j in range(n_inst):
            @pl.when((j != i) & (j != i - 1))
            def _(j=j):
                whole(0, j).wait_recv()

        @pl.when(z > 0)
        def _():
            for xx in range(chips):
                for part in range(2):
                    store_map(tw, block * xx, part, tg[xx, part])

        to_hubs(raw_half)
        to_hubs(halfway)

        @pl.when(z > 0)
        def _():
            def chunk_step(c, carry):
                scan(c).wait_recv()
                part = pl.ds(pl.multiple_of(c * CHUNK, CHUNK), CHUNK)

                @pl.when(z < NZ - 1)
                def _():
                    p, g = through(tw, si[0, part], si[1, part])
                    so[0, part] = p
                    so[1, part] = g
                    scan(c).start()

                for d in range(1, chips):
                    spread(si, c, d).start()
                return carry

            lax.fori_loop(0, count, chunk_step, 0)

        for j in range(n_inst):
            @pl.when(j != i)
            def _(j=j):
                raw_whole(0, j).wait_recv()
        bp, bg = mix(raw)

        @pl.when(z == 0)
        def _():
            so[0, data] = bp
            so[1, data] = bg
            scan_data.start()

        @pl.when(z > 0)
        def _():
            scan_data.wait_recv()

            @pl.when((z < NZ - 1) | (y == 0))
            def _():
                p, g = through(tw, si[0, data], si[1, data])
                so[0, data] = p + bp
                so[1, data] = g + bg

            @pl.when(z < NZ - 1)
            def _():
                scan_data.start()

        @pl.when((y == 0) & (z == NZ - 1))
        def _():
            uin[0] = so[:, data]
            for zz in range(NZ):
                down(zz).start()

        def give_out(p, g):
            vin[0, 0:both] = p
            vin[0, both:] = g
            give.start()

        @pl.when(y == 0)
        def _():
            @pl.when(z == 0)
            def _():
                give_out(zero, zero)

            @pl.when(z > 0)
            def _():
                give_out(si[0, data], si[1, data])

        pass_rq.wait_recv()
        lax.fori_loop(0, mid, drive, 0)
        for j in range(n_inst):
            @pl.when(j != i)
            def _(j=j):
                raw_half(0, j).wait_recv()
                halfway(0, j).wait_recv()
        mp, mg = mix(rawm)
        for xx in range(chips):
            for part in range(2):
                store_map(tq, block * xx, part, tgm[xx, part])

        @pl.when(mapped)
        def _():
            pm[x] = si[:, 0:block]
            for d in range(1, chips):
                for c in range(chunks):
                    spread(si, c, d).wait_recv()
            for xx in range(chips):
                for part in range(2):
                    store_map(tp, block * xx, part, pm[xx, part])

        @pl.when(y > 0)
        def _():
            down(0).wait_recv()

        @pl.when(mapped)
        def _():
            p, g = through(tp, uin[1, 0], uin[1, 1])
            p, g = p + si[0, data], g + si[1, data]

            @pl.when(lead)
            def _():
                next_p, next_g = through(tw, p, g)
                uin[0, 0] = next_p + bp
                uin[0, 1] = next_g + bg
                for zz in range(NZ):
                    down(zz).start()

            give_out(p, g)

        @pl.when((y > 0) & (z == 0))
        def _():
            give_out(uin[1, 0], uin[1, 1])

        p, g = through(tq, vin[0, 0:both], vin[0, both:])
        lax.fori_loop(0, mid, final_step, jnp.concatenate([p + mp, g + mg], 0))
        late.start()
        early.wait_recv()
        for t in range(tiles):
            out[:, t, :] = s0[:, t, :] + u[inv[t], local:both, :]

        late.wait_send()
        give.wait_send()

        @pl.when(z < NZ - 1)
        def _():
            scan_data.wait_send()
            lax.fori_loop(0, count, lambda c, k: (scan(c).wait_send(), k)[1], 0)

        @pl.when(mapped)
        def _():
            for d in range(1, chips):
                for c in range(chunks):
                    spread(si, c, d).wait_send()

        @pl.when(lead)
        def _():
            for zz in range(NZ):
                down(zz).wait_send()

    for xx in range(chips):
        @pl.when(2 * xx != i)
        def _(xx=xx):
            first(xx, i).wait_send()

        @pl.when(2 * xx + 1 != i)
        def _(xx=xx):
            whole(xx, i).wait_send()
            halfway(xx, i).wait_send()
            raw_whole(xx, i).wait_send()
            raw_half(xx, i).wait_send()


def solution(mesh):
    n_inst, n_axial = mesh.shape["inst"], mesh.shape["axial"]

    def on_device(flow_state, forcing, tile_inverse, coupling, sweep_order):
        local, tiles, width = flow_state.shape
        chips = n_inst // 2
        per = tiles // chips
        cols = width // n_inst
        block = 2 * cols
        pad = -(-width // 128) * 128
        both = 2 * local
        chunks = block // CHUNK
        kmat = jnp.asarray(exchange_matrix(local * n_inst, n_inst))
        vmem = pl.BlockSpec(memory_space=pltpu.VMEM)
        dma = pltpu.SemaphoreType.DMA
        return pl.pallas_call(
            functools.partial(kernel, n_inst, n_axial),
            out_shape=jax.ShapeDtypeStruct(flow_state.shape, F32),
            in_specs=[pl.BlockSpec(memory_space=pltpu.SMEM), vmem, vmem, vmem,
                      pl.BlockSpec(memory_space=pl.ANY), pl.BlockSpec(memory_space=pl.ANY)],
            out_specs=vmem,
            scratch_shapes=[
                pltpu.VMEM((tiles, width, width), BF16),
                pltpu.VMEM((tiles, width, width), BF16),
                pltpu.VMEM((tiles, both, width), F32),
                pltpu.VMEM((n_inst, per, both, width), F32),
                pltpu.VMEM((chips, per, 2 * both, width), F32),
                pltpu.VMEM((tiles, 2 * both, width), F32),
                pltpu.VMEM((tiles, both, width), F32),
                pltpu.VMEM((2, cols + both, width), F32),
                pltpu.VMEM((2, cols + both, width), F32),
                pltpu.VMEM((chips, 2, block, width), F32),
                pltpu.VMEM((chips, 2, block, width), F32),
                pltpu.VMEM((n_inst, 2, both, width), F32),
                pltpu.VMEM((n_inst, 2, both, width), F32),
                pltpu.VMEM((width, 4 * pad), BF16),
                pltpu.VMEM((width, 4 * pad), BF16),
                pltpu.VMEM((width, 4 * pad), BF16),
                pltpu.VMEM((2, block + both, width), F32),
                pltpu.VMEM((2, block + both, width), F32),
                pltpu.VMEM((chips, 2, block, width), F32),
                pltpu.VMEM((2, 2, both, width), F32),
                pltpu.VMEM((2, 2 * both, width), F32),
                pltpu.VMEM((tiles // 2, width, width), BF16),
                pltpu.VMEM((tiles // 2, width, 2 * pad), BF16),
                pltpu.VMEM((tiles // 2, 2 * both, width), F32),
                pltpu.SMEM((tiles,), jnp.int32),
                dma((2,)),
                dma((chips,)), dma((n_inst,)), dma((chips,)), dma((chips,)),
                dma((chips,)), dma((n_inst,)), dma((chips,)), dma((n_inst,)),
                dma((chips,)), dma((n_inst,)), dma((chips,)), dma((n_inst,)),
                dma((10,)),
                dma((chunks,)), dma((chunks,)), dma((2,)),
                dma((chips - 1, chunks)), dma((chips - 1, chunks)),
                dma((NZ,)), dma((1,)),
            ],
            compiler_params=pltpu.CompilerParams(collective_id=0, has_side_effects=True),
        )(sweep_order, kmat, flow_state, forcing, tile_inverse, coupling)

    return jax.shard_map(
        on_device,
        mesh=mesh,
        in_specs=(P("inst", "axial", None), P("inst", "axial", None), P("axial", None, None),
                  P("axial", None, None), P("axial")),
        out_specs=P("inst", "axial", None),
        check_vma=False,
    )
```

```python
import functools

import jax
import jax.numpy as jnp
import numpy as np
from jax import lax
from jax.experimental import pallas as pl
from jax.experimental.pallas import tpu as pltpu
from jax.sharding import PartitionSpec as P

ITERS = 2
SPECTRAL_GAIN = 2.0
NZ = 8
UNROLL = 4
CHUNK = 16
MESH = pl.DeviceIdType.MESH
F32, BF16 = jnp.float32, jnp.bfloat16
NT = (((1,), (1,)), ((), ()))
NN = (((1,), (0,)), ((), ()))


def exchange_matrix(period, groups):
    idx = np.arange(period)
    dist = idx[:, None] - idx[None, :]
    angle = np.pi * dist / period
    safe = np.where(dist == 0, 1.0, np.sin(angle))
    deriv = np.where(dist == 0, 0.0, 0.5 * (1.0 - 2.0 * (dist % 2)) * np.cos(angle) / safe)
    e = deriv * (SPECTRAL_GAIN / period) + np.eye(period)
    whole = np.block([[-e @ e, e], [-2.0 * e, 2.0 * np.eye(period)]])
    local = period // groups
    given = [part * period + dev * local + n for dev in range(groups) for part in range(2) for n in range(local)]
    wide = 2 * local
    made = [part * period + chip * wide + n for chip in range(groups // 2) for part in range(2) for n in range(wide)]
    return whole[np.ix_(made, given)].astype(np.float32)


def halves(x):
    high = x.astype(BF16)
    low = (x - high.astype(F32)).astype(BF16)
    return high, low


def split(x):
    high = x.astype(BF16).astype(F32)
    return jnp.concatenate([high, x - high], 0).astype(BF16)


def times(x, w, dims=NT):
    m = x.shape[0]
    y = lax.dot_general(split(x), w, dims, preferred_element_type=F32)
    return y[:m] + y[m:]


def store_map(dst, row, part, block):
    pad = dst.shape[1] // 4
    rows, width = block.shape
    high, low = halves(block)
    dst[pl.ds(row, rows), part * pad:part * pad + width] = high
    dst[pl.ds(row, rows), (2 + part) * pad:(2 + part) * pad + width] = low


def through(m, p, g):
    rows, width = p.shape
    pad = m.shape[1] // 4
    y = lax.dot_general(split(jnp.concatenate([p, g], 0)), m[...], NN, preferred_element_type=F32)
    y = y[:2 * rows] + y[2 * rows:]
    y = y[:, :2 * pad] + y[:, 2 * pad:]
    return y[:rows, :width], y[rows:, :width] + y[:rows, pad:pad + width]


def kernel(n_inst, n_axial, order, kmat, s0, f, a_hbm, c_hbm, out,
           wa, wc, sb, rb, ob, rq, u, ps, gs, tx, txm, tg, tgm, raw, rawm, tw, tp, tq, si, so, pm, uin, vin, at, nt, ya, inv,
           w_sem, x1_send, x1_recv, x2_send, x2_recv, g1_send, g1_recv, gm_send, gm_recv, r1_send, r1_recv, rm_send, rm_recv, pair_sem,
           sc_send, sc_recv, sd_sem, g2_send, g2_recv, up_send, up_recv):
    i = lax.axis_index("inst")
    a = lax.axis_index("axial")
    local, tiles, width = s0.shape
    chips = n_inst // 2
    per = tiles // chips
    mid = tiles // 2
    cols = width // n_inst
    block = 2 * cols
    both = 2 * local
    x, core = i // 2, lax.rem(i, 2)
    y, z = a // NZ, lax.rem(a, NZ)
    last = n_axial // NZ - 1
    chunks = block // CHUNK
    hub = core == 1
    lead = (z == NZ - 1) & (y < last)
    mapped = (y > 0) & (z > 0)
    data = pl.ds(block, both)

    load_a = pltpu.make_async_copy(a_hbm, wa, w_sem.at[0])
    load_c = pltpu.make_async_copy(c_hbm, wc, w_sem.at[1])
    load_a.start()
    load_c.start()

    def remote(src, dst, send, recv, **there):
        return pltpu.make_async_remote_copy(
            src_ref=src, dst_ref=dst, send_sem=send, recv_sem=recv, device_id=there, device_id_type=MESH)

    barrier = pltpu.get_barrier_semaphore()
    for d in range(1, n_inst):
        pl.semaphore_signal(barrier, inc=1, device_id={"inst": lax.rem(i + d, n_inst)}, device_id_type=MESH)

    @pl.when(hub)
    def _():
        for d in (1, NZ - 1):
            there = y * NZ + lax.rem(z + d, NZ)
            pl.semaphore_signal(barrier, inc=1, device_id={"axial": there}, device_id_type=MESH)

        @pl.when(lead)
        def _():
            for zz in range(NZ):
                pl.semaphore_signal(barrier, inc=1, device_id={"axial": (y + 1) * NZ + zz}, device_id_type=MESH)

        @pl.when(y > 0)
        def _():
            pl.semaphore_signal(barrier, inc=1, device_id={"axial": y * NZ - 1}, device_id_type=MESH)

    for t in range(tiles):
        sb[t, 0:local, :] = s0[:, t, :]
        sb[t, local:both, :] = f[:, t, :]
    row = lax.broadcasted_iota(jnp.int32, (cols, width), 0)
    col = lax.broadcasted_iota(jnp.int32, (cols, width), 1)
    ps[0:cols] = jnp.where(col == row + i * cols, 1.0, 0.0).astype(F32)
    ps[cols:] = jnp.zeros((both, width), F32)
    gs[...] = jnp.zeros((cols + both, width), F32)

    def first(xx, sender):
        return remote(sb.at[pl.ds(per * xx, per)], rb.at[sender], x1_send.at[xx], x1_recv.at[sender], inst=2 * xx)

    def second(d):
        xx = lax.rem(x + d, chips)
        return remote(ob.at[xx], rq.at[pl.ds(per * x, per)], x2_send.at[d], x2_recv.at[d], inst=2 * xx)

    def gather(src, dst, send, recv, xx, sender):
        half = pl.ds(pl.multiple_of(lax.rem(sender, 2) * cols, 8), cols)
        return remote(src.at[:, 0:cols], dst.at[sender // 2, :, half], send.at[xx], recv.at[sender], inst=2 * xx + 1)

    def whole(xx, sender):
        return gather(tx, tg, g1_send, g1_recv, xx, sender)

    def halfway(xx, sender):
        return gather(txm, tgm, gm_send, gm_recv, xx, sender)

    def raw_whole(xx, sender):
        return remote(tx.at[:, cols:cols + both], raw.at[sender], r1_send.at[xx], r1_recv.at[sender], inst=2 * xx + 1)

    def raw_half(xx, sender):
        return remote(txm.at[:, cols:cols + both], rawm.at[sender], rm_send.at[xx], rm_recv.at[sender], inst=2 * xx + 1)

    def to_hubs(copy):
        for xx in range(chips):
            @pl.when(2 * xx + 1 != i)
            def _(xx=xx):
                copy(xx, i).start()

    other = i + 1 - 2 * core
    pass_rq = remote(rq, rq, pair_sem.at[0], pair_sem.at[1], inst=other)
    give = remote(vin.at[0], vin.at[1], pair_sem.at[4], pair_sem.at[5], inst=other)
    early = remote(u.at[pl.ds(0, mid)], u.at[pl.ds(0, mid)], pair_sem.at[6], pair_sem.at[7], inst=other)
    late = remote(u.at[pl.ds(mid, mid)], u.at[pl.ds(mid, mid)], pair_sem.at[8], pair_sem.at[9], inst=other)

    load_a.wait()
    load_c.wait()

    def nt_dot(v, w):
        return lax.dot_general(v, w, NT, preferred_element_type=F32)

    def joined(v):
        m = v.shape[0] // 2
        return v[:m] + v[m:]

    def driven(t, b):
        return jnp.concatenate([-b[:cols], sb[t] - b[cols:]], 0)

    t = order[0]
    ps[...] = times(driven(t, times(ps[...], wc[t])), wa[t])

    def column_steps(start):
        def steps(n, carry):
            p, g = ps[...], gs[...]
            for j in range(UNROLL):
                k = start + n * UNROLL + j
                before, here = order[k], order[jnp.minimum(k + 1, tiles - 1)]
                high_p, high_g = split(p), split(g)
                bp, bg = nt_dot(high_p, wc[here]), nt_dot(high_g, wc[before])
                last_p = p
                bp, bg = driven(here, joined(bp)), p + joined(bg)
                p, g = nt_dot(split(bp), wa[here]), nt_dot(split(bg), wa[before])
                p, g = joined(p), -joined(g)
            ps[...] = p
            gs[...] = g
            tx[0] = last_p
            return carry
        lax.fori_loop(0, mid // UNROLL, steps, 0)
        tx[1] = gs[...]

    column_steps(0)
    txm[...] = tx[...]

    pl.semaphore_wait(barrier, n_inst - 1 + jnp.where(
        hub, 2 + jnp.where(lead, NZ, 0) + jnp.where(y > 0, 1, 0), 0))
    for xx in range(chips):
        @pl.when(2 * xx != i)
        def _(xx=xx):
            first(xx, i).start()

    column_steps(mid)
    to_hubs(whole)
    to_hubs(raw_whole)

    for t in range(tiles):
        pos = jnp.int32(0)
        for k in range(tiles):
            pos = jnp.where(order[k] == t, k, pos)
        inv[t] = pos

    pad = nt.shape[2] // 2

    def prepare(n, carry):
        t = order[mid * core + n]
        turned = wa[t].T
        at[n] = turned
        high, low = halves(lax.dot_general(wc[t].T, turned, NN, preferred_element_type=F32))
        nt[n, :, 0:width] = high
        nt[n, :, pad:pad + width] = low
        return carry

    def drive(n, carry):
        ya[n] = times(rq[order[mid * core + n]], at[n], NN)
        return carry

    def by_pair(v, n):
        m = joined(lax.dot_general(split(v), nt[n], NN, preferred_element_type=F32))
        return m[:, :width] + m[:, pad:pad + width]

    def rerun(p, g):
        p = ya[0, 0:both] - by_pair(p, 0)
        for n in range(mid):
            old = p
            if n + 1 < mid:
                p = ya[n + 1, 0:both] - by_pair(old, n + 1)
            g = ya[n, both:] - by_pair(g, n) - times(old, at[n], NN)
            u[mid * core + n] = g

    zero = jnp.zeros((both, width), F32)

    @pl.when(core == 0)
    def _():
        rb[i] = sb[pl.ds(per * x, per)]
        for j in range(n_inst):
            @pl.when(j != i)
            def _(j=j):
                first(0, j).wait_recv()
        for t in range(per):
            mixed = jnp.dot(kmat[...], rb[:, t].reshape(both * n_inst, width),
                            precision=lax.Precision.HIGHEST, preferred_element_type=F32)
            ob[:, t] = mixed.reshape(chips, 2 * both, width)
        lax.fori_loop(0, mid, prepare, 0)
        for d in range(1, chips):
            second(d).start()
        rq[pl.ds(per * x, per)] = ob[x]
        to_hubs(raw_half)
        to_hubs(halfway)
        for d in range(1, chips):
            second(d).wait_recv()
        pass_rq.start()
        lax.fori_loop(0, mid, drive, 0)
        give.wait_recv()
        rerun(vin[1, 0:both], vin[1, both:])
        early.start()
        late.wait_recv()
        for t in range(tiles):
            out[:, t, :] = s0[:, t, :] + u[inv[t], 0:local, :]
        early.wait_send()
        pass_rq.wait_send()
        for d in range(1, chips):
            second(d).wait_send()

    @pl.when(hub)
    def _():
        def scan(c):
            part = pl.ds(pl.multiple_of(c * CHUNK, CHUNK), CHUNK)
            return remote(so.at[:, part], si.at[:, part], sc_send.at[c], sc_recv.at[c],
                          axial=y * NZ + lax.rem(z + 1, NZ))

        scan_data = remote(so.at[:, data], si.at[:, data], sd_sem.at[0], sd_sem.at[1],
                           axial=y * NZ + lax.rem(z + 1, NZ))

        def spread(src, c, d):
            part = pl.ds(pl.multiple_of(c * CHUNK, CHUNK), CHUNK)
            return remote(src.at[:, part], pm.at[x, :, part], g2_send.at[d - 1, c], g2_recv.at[d - 1, c],
                          inst=lax.rem(i + 2 * d, n_inst))

        def down(zz):
            return remote(uin.at[0], uin.at[1], up_send.at[zz], up_recv.at[0],
                          axial=lax.rem(y + 1, last + 1) * NZ + zz)

        def mix(rows):
            made = [jnp.dot(kmat[pl.ds(pl.multiple_of(2 * both * x, 8), 2 * both)], rows[:, n].reshape(both * n_inst, width),
                            precision=lax.Precision.HIGHEST, preferred_element_type=F32) for n in range(2)]
            return made[0][:both], made[0][both:] + made[1][:both]

        count = jnp.where(y == 0, 0, chunks)

        tg[x, :, pl.ds(cols, cols)] = tx[:, 0:cols]
        tgm[x, :, pl.ds(cols, cols)] = txm[:, 0:cols]
        raw[i] = tx[:, cols:]
        rawm[i] = txm[:, cols:]
        whole(0, i - 1).wait_recv()

        @pl.when((z == 0) & (y > 0))
        def _():
            so[:, 0:block] = tg[x]
            lax.fori_loop(0, count, lambda c, k: (scan(c).start(), k)[1], 0)

        lax.fori_loop(0, mid, prepare, 0)
        for j in range(n_inst):
            @pl.when((j != i) & (j != i - 1))
            def _(j=j):
                whole(0, j).wait_recv()

        @pl.when(z > 0)
        def _():
            for xx in range(chips):
                for part in range(2):
                    store_map(tw, block * xx, part, tg[xx, part])

        to_hubs(raw_half)
        to_hubs(halfway)

        @pl.when(z > 0)
        def _():
            def chunk_step(c, carry):
                scan(c).wait_recv()
                part = pl.ds(pl.multiple_of(c * CHUNK, CHUNK), CHUNK)

                @pl.when(z < NZ - 1)
                def _():
                    p, g = through(tw, si[0, part], si[1, part])
                    so[0, part] = p
                    so[1, part] = g
                    scan(c).start()

                for d in range(1, chips):
                    spread(si, c, d).start()
                return carry

            lax.fori_loop(0, count, chunk_step, 0)

        for j in range(n_inst):
            @pl.when(j != i)
            def _(j=j):
                raw_whole(0, j).wait_recv()
        bp, bg = mix(raw)

        @pl.when(z == 0)
        def _():
            so[0, data] = bp
            so[1, data] = bg
            scan_data.start()

        @pl.when(z > 0)
        def _():
            scan_data.wait_recv()

            @pl.when((z < NZ - 1) | (y == 0))
            def _():
                p, g = through(tw, si[0, data], si[1, data])
                so[0, data] = p + bp
                so[1, data] = g + bg

            @pl.when(z < NZ - 1)
            def _():
                scan_data.start()

        @pl.when((y == 0) & (z == NZ - 1))
        def _():
            uin[0] = so[:, data]
            for zz in range(NZ):
                down(zz).start()

        def give_out(p, g):
            vin[0, 0:both] = p
            vin[0, both:] = g
            give.start()

        @pl.when(y == 0)
        def _():
            @pl.when(z == 0)
            def _():
                give_out(zero, zero)

            @pl.when(z > 0)
            def _():
                give_out(si[0, data], si[1, data])

        pass_rq.wait_recv()
        lax.fori_loop(0, mid, drive, 0)
        for j in range(n_inst):
            @pl.when(j != i)
            def _(j=j):
                raw_half(0, j).wait_recv()
                halfway(0, j).wait_recv()
        mp, mg = mix(rawm)
        for xx in range(chips):
            for part in range(2):
                store_map(tq, block * xx, part, tgm[xx, part])

        @pl.when(mapped)
        def _():
            pm[x] = si[:, 0:block]
            for d in range(1, chips):
                for c in range(chunks):
                    spread(si, c, d).wait_recv()
            for xx in range(chips):
                for part in range(2):
                    store_map(tp, block * xx, part, pm[xx, part])

        @pl.when(y > 0)
        def _():
            down(0).wait_recv()

        @pl.when(mapped)
        def _():
            p, g = through(tp, uin[1, 0], uin[1, 1])
            p, g = p + si[0, data], g + si[1, data]

            @pl.when(lead)
            def _():
                next_p, next_g = through(tw, p, g)
                uin[0, 0] = next_p + bp
                uin[0, 1] = next_g + bg
                for zz in range(NZ):
                    down(zz).start()

            give_out(p, g)

        @pl.when((y > 0) & (z == 0))
        def _():
            give_out(uin[1, 0], uin[1, 1])

        p, g = through(tq, vin[0, 0:both], vin[0, both:])
        rerun(p + mp, g + mg)
        late.start()
        early.wait_recv()
        for t in range(tiles):
            out[:, t, :] = s0[:, t, :] + u[inv[t], local:both, :]

        late.wait_send()
        give.wait_send()

        @pl.when(z < NZ - 1)
        def _():
            scan_data.wait_send()
            lax.fori_loop(0, count, lambda c, k: (scan(c).wait_send(), k)[1], 0)

        @pl.when(mapped)
        def _():
            for d in range(1, chips):
                for c in range(chunks):
                    spread(si, c, d).wait_send()

        @pl.when(lead)
        def _():
            for zz in range(NZ):
                down(zz).wait_send()

    for xx in range(chips):
        @pl.when(2 * xx != i)
        def _(xx=xx):
            first(xx, i).wait_send()

        @pl.when(2 * xx + 1 != i)
        def _(xx=xx):
            whole(xx, i).wait_send()
            halfway(xx, i).wait_send()
            raw_whole(xx, i).wait_send()
            raw_half(xx, i).wait_send()


def solution(mesh):
    n_inst, n_axial = mesh.shape["inst"], mesh.shape["axial"]

    def on_device(flow_state, forcing, tile_inverse, coupling, sweep_order):
        local, tiles, width = flow_state.shape
        chips = n_inst // 2
        per = tiles // chips
        cols = width // n_inst
        block = 2 * cols
        pad = -(-width // 128) * 128
        both = 2 * local
        chunks = block // CHUNK
        kmat = jnp.asarray(exchange_matrix(local * n_inst, n_inst))
        vmem = pl.BlockSpec(memory_space=pltpu.VMEM)
        dma = pltpu.SemaphoreType.DMA
        return pl.pallas_call(
            functools.partial(kernel, n_inst, n_axial),
            out_shape=jax.ShapeDtypeStruct(flow_state.shape, F32),
            in_specs=[pl.BlockSpec(memory_space=pltpu.SMEM), vmem, vmem, vmem,
                      pl.BlockSpec(memory_space=pl.ANY), pl.BlockSpec(memory_space=pl.ANY)],
            out_specs=vmem,
            scratch_shapes=[
                pltpu.VMEM((tiles, width, width), BF16),
                pltpu.VMEM((tiles, width, width), BF16),
                pltpu.VMEM((tiles, both, width), F32),
                pltpu.VMEM((n_inst, per, both, width), F32),
                pltpu.VMEM((chips, per, 2 * both, width), F32),
                pltpu.VMEM((tiles, 2 * both, width), F32),
                pltpu.VMEM((tiles, both, width), F32),
                pltpu.VMEM((cols + both, width), F32),
                pltpu.VMEM((cols + both, width), F32),
                pltpu.VMEM((2, cols + both, width), F32),
                pltpu.VMEM((2, cols + both, width), F32),
                pltpu.VMEM((chips, 2, block, width), F32),
                pltpu.VMEM((chips, 2, block, width), F32),
                pltpu.VMEM((n_inst, 2, both, width), F32),
                pltpu.VMEM((n_inst, 2, both, width), F32),
                pltpu.VMEM((width, 4 * pad), BF16),
                pltpu.VMEM((width, 4 * pad), BF16),
                pltpu.VMEM((width, 4 * pad), BF16),
                pltpu.VMEM((2, block + both, width), F32),
                pltpu.VMEM((2, block + both, width), F32),
                pltpu.VMEM((chips, 2, block, width), F32),
                pltpu.VMEM((2, 2, both, width), F32),
                pltpu.VMEM((2, 2 * both, width), F32),
                pltpu.VMEM((tiles // 2, width, width), BF16),
                pltpu.VMEM((tiles // 2, width, 2 * pad), BF16),
                pltpu.VMEM((tiles // 2, 2 * both, width), F32),
                pltpu.SMEM((tiles,), jnp.int32),
                dma((2,)),
                dma((chips,)), dma((n_inst,)), dma((chips,)), dma((chips,)),
                dma((chips,)), dma((n_inst,)), dma((chips,)), dma((n_inst,)),
                dma((chips,)), dma((n_inst,)), dma((chips,)), dma((n_inst,)),
                dma((10,)),
                dma((chunks,)), dma((chunks,)), dma((2,)),
                dma((chips - 1, chunks)), dma((chips - 1, chunks)),
                dma((NZ,)), dma((1,)),
            ],
            compiler_params=pltpu.CompilerParams(collective_id=0, has_side_effects=True),
        )(sweep_order, kmat, flow_state, forcing, tile_inverse, coupling)

    return jax.shard_map(
        on_device,
        mesh=mesh,
        in_specs=(P("inst", "axial", None), P("inst", "axial", None), P("axial", None, None),
                  P("axial", None, None), P("axial")),
        out_specs=P("inst", "axial", None),
        check_vma=False,
    )
```

```python
import functools

import jax
import jax.numpy as jnp
import numpy as np
from jax import lax
from jax.experimental import pallas as pl
from jax.experimental.pallas import tpu as pltpu
from jax.sharding import PartitionSpec as P

ITERS = 2
SPECTRAL_GAIN = 2.0
NZ = 8
VMEM_BYTES = 56_400_000
UNROLL = 4
CHUNK = 16
MESH = pl.DeviceIdType.MESH
F32, BF16 = jnp.float32, jnp.bfloat16
NT = (((1,), (1,)), ((), ()))
NN = (((1,), (0,)), ((), ()))


def exchange_matrix(period, groups):
    idx = np.arange(period)
    dist = idx[:, None] - idx[None, :]
    angle = np.pi * dist / period
    safe = np.where(dist == 0, 1.0, np.sin(angle))
    deriv = np.where(dist == 0, 0.0, 0.5 * (1.0 - 2.0 * (dist % 2)) * np.cos(angle) / safe)
    e = deriv * (SPECTRAL_GAIN / period) + np.eye(period)
    whole = np.block([[-e @ e, e], [-2.0 * e, 2.0 * np.eye(period)]])
    local = period // groups
    given = [part * period + dev * local + n for dev in range(groups) for part in range(2) for n in range(local)]
    wide = 2 * local
    made = [part * period + chip * wide + n for chip in range(groups // 2) for part in range(2) for n in range(wide)]
    return whole[np.ix_(made, given)].astype(np.float32)


def halves(x):
    high = x.astype(BF16)
    low = (x - high.astype(F32)).astype(BF16)
    return high, low


def split(x):
    high = x.astype(BF16).astype(F32)
    return jnp.concatenate([high, x - high], 0).astype(BF16)


def times(x, w, dims=NT):
    m = x.shape[0]
    y = lax.dot_general(split(x), w, dims, preferred_element_type=F32)
    return y[:m] + y[m:]


def store_map(dst, row, part, block):
    pad = dst.shape[1] // 4
    rows, width = block.shape
    high, low = halves(block)
    dst[pl.ds(row, rows), part * pad:part * pad + width] = high
    dst[pl.ds(row, rows), (2 + part) * pad:(2 + part) * pad + width] = low


def through(m, p, g):
    rows, width = p.shape
    pad = m.shape[1] // 4
    y = lax.dot_general(split(jnp.concatenate([p, g], 0)), m[...], NN, preferred_element_type=F32)
    y = y[:2 * rows] + y[2 * rows:]
    y = y[:, :2 * pad] + y[:, 2 * pad:]
    return y[:rows, :width], y[rows:, :width] + y[:rows, pad:pad + width]


def kernel(n_inst, n_axial, order, k_hbm, s_hbm, f_hbm, a_hbm, c_hbm, out,
           kmat, s0, f, wa, wc, sb, rb, ob, rq, u, ps, gs, tx, txm, tg, tgm, raw, rawm, tw, tp, tq, si, so, pm, uin, vin, at, nt, ya, inv,
           w_sem, x1_send, x1_recv, x2_send, x2_recv, g1_send, g1_recv, gm_send, gm_recv, r1_send, r1_recv, rm_send, rm_recv, pair_sem,
           sc_send, sc_recv, sd_sem, g2_send, g2_recv, up_send, up_recv):
    i = lax.axis_index("inst")
    a = lax.axis_index("axial")
    local, tiles, width = s0.shape
    chips = n_inst // 2
    per = tiles // chips
    mid = tiles // 2
    cols = width // n_inst
    block = 2 * cols
    both = 2 * local
    x, core = i // 2, lax.rem(i, 2)
    y, z = a // NZ, lax.rem(a, NZ)
    last = n_axial // NZ - 1
    chunks = block // CHUNK
    hub = core == 1
    lead = (z == NZ - 1) & (y < last)
    mapped = (y > 0) & (z > 0)
    data = pl.ds(block, both)

    loads = [pltpu.make_async_copy(src, dst, w_sem.at[n]) for n, (src, dst) in enumerate(
        [(s_hbm, s0), (f_hbm, f), (c_hbm, wc), (a_hbm, wa), (k_hbm.at[pl.ds(0, kmat.shape[0])], kmat)])]
    for load in loads:
        load.start()

    def remote(src, dst, send, recv, **there):
        return pltpu.make_async_remote_copy(
            src_ref=src, dst_ref=dst, send_sem=send, recv_sem=recv, device_id=there, device_id_type=MESH)

    barrier = pltpu.get_barrier_semaphore()
    for d in range(1, n_inst):
        pl.semaphore_signal(barrier, inc=1, device_id={"inst": lax.rem(i + d, n_inst)}, device_id_type=MESH)

    @pl.when(hub)
    def _():
        for d in (1, NZ - 1):
            there = y * NZ + lax.rem(z + d, NZ)
            pl.semaphore_signal(barrier, inc=1, device_id={"axial": there}, device_id_type=MESH)

        @pl.when(lead)
        def _():
            for zz in range(NZ):
                pl.semaphore_signal(barrier, inc=1, device_id={"axial": (y + 1) * NZ + zz}, device_id_type=MESH)

        @pl.when(y > 0)
        def _():
            pl.semaphore_signal(barrier, inc=1, device_id={"axial": y * NZ - 1}, device_id_type=MESH)

    loads[0].wait()
    loads[1].wait()
    for t in range(tiles):
        sb[t, 0:local, :] = s0[:, t, :]
        sb[t, local:both, :] = f[:, t, :]
    row = lax.broadcasted_iota(jnp.int32, (cols, width), 0)
    col = lax.broadcasted_iota(jnp.int32, (cols, width), 1)
    ps[0:cols] = jnp.where(col == row + i * cols, 1.0, 0.0).astype(F32)
    ps[cols:] = jnp.zeros((both, width), F32)
    gs[...] = jnp.zeros((cols + both, width), F32)

    def first(xx, sender):
        return remote(sb.at[pl.ds(per * xx, per)], rb.at[sender], x1_send.at[xx], x1_recv.at[sender], inst=2 * xx)

    def second(d):
        xx = lax.rem(x + d, chips)
        return remote(ob.at[xx], rq.at[pl.ds(per * x, per)], x2_send.at[d], x2_recv.at[d], inst=2 * xx)

    def gather(src, dst, send, recv, xx, sender):
        half = pl.ds(pl.multiple_of(lax.rem(sender, 2) * cols, 8), cols)
        return remote(src.at[:, 0:cols], dst.at[sender // 2, :, half], send.at[xx], recv.at[sender], inst=2 * xx + 1)

    def whole(xx, sender):
        return gather(tx, tg, g1_send, g1_recv, xx, sender)

    def halfway(xx, sender):
        return gather(txm, tgm, gm_send, gm_recv, xx, sender)

    def raw_whole(xx, sender):
        return remote(tx.at[:, cols:cols + both], raw.at[sender], r1_send.at[xx], r1_recv.at[sender], inst=2 * xx + 1)

    def raw_half(xx, sender):
        return remote(txm.at[:, cols:cols + both], rawm.at[sender], rm_send.at[xx], rm_recv.at[sender], inst=2 * xx + 1)

    def to_hubs(copy):
        for xx in range(chips):
            @pl.when(2 * xx + 1 != i)
            def _(xx=xx):
                copy(xx, i).start()

    other = i + 1 - 2 * core
    pass_rq = remote(rq, rq, pair_sem.at[0], pair_sem.at[1], inst=other)
    give = remote(vin.at[0], vin.at[1], pair_sem.at[4], pair_sem.at[5], inst=other)
    early = remote(u.at[pl.ds(0, mid)], u.at[pl.ds(0, mid)], pair_sem.at[6], pair_sem.at[7], inst=other)
    late = remote(u.at[pl.ds(mid, mid)], u.at[pl.ds(mid, mid)], pair_sem.at[8], pair_sem.at[9], inst=other)

    for load in loads[2:]:
        load.wait()

    def nt_dot(v, w):
        return lax.dot_general(v, w, NT, preferred_element_type=F32)

    def joined(v):
        m = v.shape[0] // 2
        return v[:m] + v[m:]

    def driven(t, b):
        return jnp.concatenate([-b[:cols], sb[t] - b[cols:]], 0)

    t = order[0]
    ps[...] = times(driven(t, times(ps[...], wc[t])), wa[t])

    def column_steps(start):
        def steps(n, carry):
            p, g = ps[...], gs[...]
            for j in range(UNROLL):
                k = start + n * UNROLL + j
                before, here = order[k], order[jnp.minimum(k + 1, tiles - 1)]
                high_p, high_g = split(p), split(g)
                bp, bg = nt_dot(high_p, wc[here]), nt_dot(high_g, wc[before])
                last_p = p
                bp, bg = driven(here, joined(bp)), p + joined(bg)
                p, g = nt_dot(split(bp), wa[here]), nt_dot(split(bg), wa[before])
                p, g = joined(p), -joined(g)
            ps[...] = p
            gs[...] = g
            tx[0] = last_p
            return carry
        lax.fori_loop(0, mid // UNROLL, steps, 0)
        tx[1] = gs[...]

    column_steps(0)
    txm[...] = tx[...]

    pl.semaphore_wait(barrier, n_inst - 1 + jnp.where(
        hub, 2 + jnp.where(lead, NZ, 0) + jnp.where(y > 0, 1, 0), 0))
    for xx in range(chips):
        @pl.when(2 * xx != i)
        def _(xx=xx):
            first(xx, i).start()

    column_steps(mid)
    to_hubs(whole)
    to_hubs(raw_whole)

    for t in range(tiles):
        pos = jnp.int32(0)
        for k in range(tiles):
            pos = jnp.where(order[k] == t, k, pos)
        inv[t] = pos

    pad = nt.shape[2] // 2

    def prepare(n, carry):
        t = order[mid * core + n]
        turned = wa[t].T
        at[n] = turned
        high, low = halves(lax.dot_general(wc[t].T, turned, NN, preferred_element_type=F32))
        nt[n, :, 0:width] = high
        nt[n, :, pad:pad + width] = low
        return carry

    def drive(n, carry):
        ya[n] = times(rq[order[mid * core + n]], at[n], NN)
        return carry

    def by_pair(v, n):
        m = joined(lax.dot_general(split(v), nt[n], NN, preferred_element_type=F32))
        return m[:, :width] + m[:, pad:pad + width]

    def rerun(p, g):
        p = ya[0, 0:both] - by_pair(p, 0)
        for n in range(mid):
            old = p
            if n + 1 < mid:
                p = ya[n + 1, 0:both] - by_pair(old, n + 1)
            g = ya[n, both:] - by_pair(g, n) - times(old, at[n], NN)
            u[mid * core + n] = g

    zero = jnp.zeros((both, width), F32)

    @pl.when(core == 0)
    def _():
        rb[i] = sb[pl.ds(per * x, per)]
        for j in range(n_inst):
            @pl.when(j != i)
            def _(j=j):
                first(0, j).wait_recv()
        for t in range(per):
            mixed = jnp.dot(kmat[:, 0:both * n_inst], rb[:, t].reshape(both * n_inst, width),
                            precision=lax.Precision.HIGHEST, preferred_element_type=F32)
            ob[:, t] = mixed.reshape(chips, 2 * both, width)
        lax.fori_loop(0, mid, prepare, 0)
        for d in range(1, chips):
            second(d).start()
        rq[pl.ds(per * x, per)] = ob[x]
        to_hubs(raw_half)
        to_hubs(halfway)
        for d in range(1, chips):
            second(d).wait_recv()
        pass_rq.start()
        lax.fori_loop(0, mid, drive, 0)
        give.wait_recv()
        rerun(vin[1, 0:both], vin[1, both:])
        early.start()
        late.wait_recv()
        for t in range(tiles):
            out[:, t, :] = s0[:, t, :] + u[inv[t], 0:local, :]
        early.wait_send()
        pass_rq.wait_send()
        for d in range(1, chips):
            second(d).wait_send()

    @pl.when(hub)
    def _():
        def scan(c):
            part = pl.ds(pl.multiple_of(c * CHUNK, CHUNK), CHUNK)
            return remote(so.at[:, part], si.at[:, part], sc_send.at[c], sc_recv.at[c],
                          axial=y * NZ + lax.rem(z + 1, NZ))

        scan_data = remote(so.at[:, data], si.at[:, data], sd_sem.at[0], sd_sem.at[1],
                           axial=y * NZ + lax.rem(z + 1, NZ))

        def spread(src, c, d):
            part = pl.ds(pl.multiple_of(c * CHUNK, CHUNK), CHUNK)
            return remote(src.at[:, part], pm.at[x, :, part], g2_send.at[d - 1, c], g2_recv.at[d - 1, c],
                          inst=lax.rem(i + 2 * d, n_inst))

        def down(zz):
            return remote(uin.at[0], uin.at[1], up_send.at[zz], up_recv.at[0],
                          axial=lax.rem(y + 1, last + 1) * NZ + zz)

        def mix(rows):
            made = [jnp.dot(kmat[pl.ds(pl.multiple_of(2 * both * x, 8), 2 * both), 0:both * n_inst], rows[:, n].reshape(both * n_inst, width),
                            precision=lax.Precision.HIGHEST, preferred_element_type=F32) for n in range(2)]
            return made[0][:both], made[0][both:] + made[1][:both]

        count = jnp.where(y == 0, 0, chunks)

        tg[x, :, pl.ds(cols, cols)] = tx[:, 0:cols]
        tgm[x, :, pl.ds(cols, cols)] = txm[:, 0:cols]
        raw[i] = tx[:, cols:]
        rawm[i] = txm[:, cols:]
        whole(0, i - 1).wait_recv()

        @pl.when((z == 0) & (y > 0))
        def _():
            so[:, 0:block] = tg[x]
            lax.fori_loop(0, count, lambda c, k: (scan(c).start(), k)[1], 0)

        lax.fori_loop(0, mid, prepare, 0)
        for j in range(n_inst):
            @pl.when((j != i) & (j != i - 1))
            def _(j=j):
                whole(0, j).wait_recv()

        @pl.when(z > 0)
        def _():
            for xx in range(chips):
                for part in range(2):
                    store_map(tw, block * xx, part, tg[xx, part])

        to_hubs(raw_half)
        to_hubs(halfway)

        @pl.when(z > 0)
        def _():
            def chunk_step(c, carry):
                scan(c).wait_recv()
                part = pl.ds(pl.multiple_of(c * CHUNK, CHUNK), CHUNK)

                @pl.when(z < NZ - 1)
                def _():
                    p, g = through(tw, si[0, part], si[1, part])
                    so[0, part] = p
                    so[1, part] = g
                    scan(c).start()

                for d in range(1, chips):
                    spread(si, c, d).start()
                return carry

            lax.fori_loop(0, count, chunk_step, 0)

        for j in range(n_inst):
            @pl.when(j != i)
            def _(j=j):
                raw_whole(0, j).wait_recv()
        bp, bg = mix(raw)

        @pl.when(z == 0)
        def _():
            so[0, data] = bp
            so[1, data] = bg
            scan_data.start()

        @pl.when(z > 0)
        def _():
            scan_data.wait_recv()

            @pl.when((z < NZ - 1) | (y == 0))
            def _():
                p, g = through(tw, si[0, data], si[1, data])
                so[0, data] = p + bp
                so[1, data] = g + bg

            @pl.when(z < NZ - 1)
            def _():
                scan_data.start()

        @pl.when((y == 0) & (z == NZ - 1))
        def _():
            uin[0] = so[:, data]
            for zz in range(NZ):
                down(zz).start()

        def give_out(p, g):
            vin[0, 0:both] = p
            vin[0, both:] = g
            give.start()

        @pl.when(y == 0)
        def _():
            @pl.when(z == 0)
            def _():
                give_out(zero, zero)

            @pl.when(z > 0)
            def _():
                give_out(si[0, data], si[1, data])

        pass_rq.wait_recv()
        lax.fori_loop(0, mid, drive, 0)
        for j in range(n_inst):
            @pl.when(j != i)
            def _(j=j):
                raw_half(0, j).wait_recv()
                halfway(0, j).wait_recv()
        mp, mg = mix(rawm)
        for xx in range(chips):
            for part in range(2):
                store_map(tq, block * xx, part, tgm[xx, part])

        @pl.when(mapped)
        def _():
            pm[x] = si[:, 0:block]
            for d in range(1, chips):
                for c in range(chunks):
                    spread(si, c, d).wait_recv()
            for xx in range(chips):
                for part in range(2):
                    store_map(tp, block * xx, part, pm[xx, part])

        @pl.when(y > 0)
        def _():
            down(0).wait_recv()

        @pl.when(mapped)
        def _():
            p, g = through(tp, uin[1, 0], uin[1, 1])
            p, g = p + si[0, data], g + si[1, data]

            @pl.when(lead)
            def _():
                next_p, next_g = through(tw, p, g)
                uin[0, 0] = next_p + bp
                uin[0, 1] = next_g + bg
                for zz in range(NZ):
                    down(zz).start()

            give_out(p, g)

        @pl.when((y > 0) & (z == 0))
        def _():
            give_out(uin[1, 0], uin[1, 1])

        p, g = through(tq, vin[0, 0:both], vin[0, both:])
        rerun(p + mp, g + mg)
        late.start()
        early.wait_recv()
        for t in range(tiles):
            out[:, t, :] = s0[:, t, :] + u[inv[t], local:both, :]

        late.wait_send()
        give.wait_send()

        @pl.when(z < NZ - 1)
        def _():
            scan_data.wait_send()
            lax.fori_loop(0, count, lambda c, k: (scan(c).wait_send(), k)[1], 0)

        @pl.when(mapped)
        def _():
            for d in range(1, chips):
                for c in range(chunks):
                    spread(si, c, d).wait_send()

        @pl.when(lead)
        def _():
            for zz in range(NZ):
                down(zz).wait_send()

    for xx in range(chips):
        @pl.when(2 * xx != i)
        def _(xx=xx):
            first(xx, i).wait_send()

        @pl.when(2 * xx + 1 != i)
        def _(xx=xx):
            whole(xx, i).wait_send()
            halfway(xx, i).wait_send()
            raw_whole(xx, i).wait_send()
            raw_half(xx, i).wait_send()


def solution(mesh):
    n_inst, n_axial = mesh.shape["inst"], mesh.shape["axial"]

    def on_device(flow_state, forcing, tile_inverse, coupling, sweep_order):
        local, tiles, width = flow_state.shape
        chips = n_inst // 2
        per = tiles // chips
        cols = width // n_inst
        block = 2 * cols
        pad = -(-width // 128) * 128
        both = 2 * local
        chunks = block // CHUNK
        size = both * n_inst
        kmat = np.zeros((10 * size, 128), np.float32)
        kmat[:size, :size] = exchange_matrix(local * n_inst, n_inst)
        kmat = jnp.asarray(kmat)
        hbm = pl.BlockSpec(memory_space=pl.ANY)
        vmem = pl.BlockSpec(memory_space=pltpu.VMEM)
        dma = pltpu.SemaphoreType.DMA
        return pl.pallas_call(
            functools.partial(kernel, n_inst, n_axial),
            out_shape=jax.ShapeDtypeStruct(flow_state.shape, F32),
            in_specs=[pl.BlockSpec(memory_space=pltpu.SMEM), hbm, hbm, hbm, hbm, hbm],
            out_specs=vmem,
            scratch_shapes=[
                pltpu.VMEM((size, 128), F32),
                pltpu.VMEM(flow_state.shape, F32),
                pltpu.VMEM(flow_state.shape, F32),
                pltpu.VMEM((tiles, width, width), BF16),
                pltpu.VMEM((tiles, width, width), BF16),
                pltpu.VMEM((tiles, both, width), F32),
                pltpu.VMEM((n_inst, per, both, width), F32),
                pltpu.VMEM((chips, per, 2 * both, width), F32),
                pltpu.VMEM((tiles, 2 * both, width), F32),
                pltpu.VMEM((tiles, both, width), F32),
                pltpu.VMEM((cols + both, width), F32),
                pltpu.VMEM((cols + both, width), F32),
                pltpu.VMEM((2, cols + both, width), F32),
                pltpu.VMEM((2, cols + both, width), F32),
                pltpu.VMEM((chips, 2, block, width), F32),
                pltpu.VMEM((chips, 2, block, width), F32),
                pltpu.VMEM((n_inst, 2, both, width), F32),
                pltpu.VMEM((n_inst, 2, both, width), F32),
                pltpu.VMEM((width, 4 * pad), BF16),
                pltpu.VMEM((width, 4 * pad), BF16),
                pltpu.VMEM((width, 4 * pad), BF16),
                pltpu.VMEM((2, block + both, width), F32),
                pltpu.VMEM((2, block + both, width), F32),
                pltpu.VMEM((chips, 2, block, width), F32),
                pltpu.VMEM((2, 2, both, width), F32),
                pltpu.VMEM((2, 2 * both, width), F32),
                pltpu.VMEM((tiles // 2, width, width), BF16),
                pltpu.VMEM((tiles // 2, width, 2 * pad), BF16),
                pltpu.VMEM((tiles // 2, 2 * both, width), F32),
                pltpu.SMEM((tiles,), jnp.int32),
                dma((5,)),
                dma((chips,)), dma((n_inst,)), dma((chips,)), dma((chips,)),
                dma((chips,)), dma((n_inst,)), dma((chips,)), dma((n_inst,)),
                dma((chips,)), dma((n_inst,)), dma((chips,)), dma((n_inst,)),
                dma((10,)),
                dma((chunks,)), dma((chunks,)), dma((2,)),
                dma((chips - 1, chunks)), dma((chips - 1, chunks)),
                dma((NZ,)), dma((1,)),
            ],
            compiler_params=pltpu.CompilerParams(collective_id=0, has_side_effects=True, vmem_limit_bytes=VMEM_BYTES),
        )(sweep_order, kmat, flow_state, forcing, tile_inverse, coupling)

    return jax.shard_map(
        on_device,
        mesh=mesh,
        in_specs=(P("inst", "axial", None), P("inst", "axial", None), P("axial", None, None),
                  P("axial", None, None), P("axial")),
        out_specs=P("inst", "axial", None),
        check_vma=False,
    )
```

```python
import functools

import jax
import jax.numpy as jnp
import numpy as np
from jax import lax
from jax.experimental import pallas as pl
from jax.experimental.pallas import tpu as pltpu
from jax.sharding import PartitionSpec as P

ITERS = 2
SPECTRAL_GAIN = 2.0
NZ = 8
VMEM_BYTES = 56_400_000
FAR_FIRST, FAR_LAST = (2, 1, 3), (1, 3, 2)
UNROLL = 4
CHUNK = 16
MESH = pl.DeviceIdType.MESH
F32, BF16 = jnp.float32, jnp.bfloat16
NT = (((1,), (1,)), ((), ()))
NN = (((1,), (0,)), ((), ()))


def exchange_matrix(period, groups):
    idx = np.arange(period)
    dist = idx[:, None] - idx[None, :]
    angle = np.pi * dist / period
    safe = np.where(dist == 0, 1.0, np.sin(angle))
    deriv = np.where(dist == 0, 0.0, 0.5 * (1.0 - 2.0 * (dist % 2)) * np.cos(angle) / safe)
    e = deriv * (SPECTRAL_GAIN / period) + np.eye(period)
    whole = np.block([[-e @ e, e], [-2.0 * e, 2.0 * np.eye(period)]])
    local = period // groups
    given = [part * period + dev * local + n for dev in range(groups) for part in range(2) for n in range(local)]
    wide = 2 * local
    made = [part * period + chip * wide + n for chip in range(groups // 2) for part in range(2) for n in range(wide)]
    return whole[np.ix_(made, given)].astype(np.float32)


def halves(x):
    high = x.astype(BF16)
    low = (x - high.astype(F32)).astype(BF16)
    return high, low


def split(x):
    high = x.astype(BF16).astype(F32)
    return jnp.concatenate([high, x - high], 0).astype(BF16)


def times(x, w, dims=NT):
    m = x.shape[0]
    y = lax.dot_general(split(x), w, dims, preferred_element_type=F32)
    return y[:m] + y[m:]


def pack(p, g):
    whole = p.shape[1] // 128 * 128
    return jnp.concatenate([p[:, :whole], g[:, :whole], p[:, whole:], g[:, whole:]], 1)


def unpack(b):
    width = b.shape[1] // 2
    whole = width // 128 * 128
    middle = whole + width
    return (jnp.concatenate([b[:, :whole], b[:, 2 * whole:middle]], 1),
            jnp.concatenate([b[:, whole:2 * whole], b[:, middle:]], 1))


def store_map(dst, row, block):
    pad = dst.shape[1] // 4
    for part, rows in enumerate(unpack(block)):
        width = rows.shape[1]
        at = pl.ds(pl.multiple_of(row, 16), rows.shape[0])
        high, low = halves(rows)
        dst[at, part * pad:part * pad + width] = high
        dst[at, (2 + part) * pad:(2 + part) * pad + width] = low


def through(m, p, g):
    rows, width = p.shape
    pad = m.shape[1] // 4
    y = lax.dot_general(split(jnp.concatenate([p, g], 0)), m[...], NN, preferred_element_type=F32)
    y = y[:2 * rows] + y[2 * rows:]
    y = y[:, :2 * pad] + y[:, 2 * pad:]
    return y[:rows, :width], y[rows:, :width] + y[:rows, pad:pad + width]


def kernel(n_inst, n_axial, order, k_hbm, s_hbm, f_hbm, a_hbm, c_hbm, out,
           kmat, s0, f, wa, wc, sb, rb, ob, rq, u, ps, gs, pv, tx, txm, tg, tgm, raw, rawm, tw, tp, tq, si, so, pm, uin, vin, at, nt, ya, inv,
           w_sem, x1_send, x1_recv, x2_send, x2_recv, g1_send, g1_recv, gm_send, gm_recv, r1_send, r1_recv, rm_send, rm_recv, pair_sem,
           sc_send, sc_recv, sd_sem, g2_send, g2_recv, up_send, up_recv):
    i = lax.axis_index("inst")
    a = lax.axis_index("axial")
    local, tiles, width = s0.shape
    chips = n_inst // 2
    per = tiles // chips
    mid = tiles // 2
    cols = width // n_inst
    block = 2 * cols
    both = 2 * local
    x, core = i // 2, lax.rem(i, 2)
    y, z = a // NZ, lax.rem(a, NZ)
    last = n_axial // NZ - 1
    chunks = block // CHUNK
    hub = core == 1
    lead = (z == NZ - 1) & (y < last)
    mapped = (y > 0) & (z > 0)
    data = pl.ds(block, both)

    loads = [pltpu.make_async_copy(src, dst, w_sem.at[n]) for n, (src, dst) in enumerate(
        [(s_hbm, s0), (f_hbm, f), (c_hbm, wc), (a_hbm, wa), (k_hbm.at[pl.ds(0, kmat.shape[0])], kmat)])]
    for load in loads:
        load.start()

    def remote(src, dst, send, recv, **there):
        return pltpu.make_async_remote_copy(
            src_ref=src, dst_ref=dst, send_sem=send, recv_sem=recv, device_id=there, device_id_type=MESH)

    barrier = pltpu.get_barrier_semaphore()
    for d in range(1, n_inst):
        pl.semaphore_signal(barrier, inc=1, device_id={"inst": lax.rem(i + d, n_inst)}, device_id_type=MESH)

    @pl.when(hub)
    def _():
        for d in (1, NZ - 1):
            there = y * NZ + lax.rem(z + d, NZ)
            pl.semaphore_signal(barrier, inc=1, device_id={"axial": there}, device_id_type=MESH)

        @pl.when(lead)
        def _():
            for zz in range(NZ):
                pl.semaphore_signal(barrier, inc=1, device_id={"axial": (y + 1) * NZ + zz}, device_id_type=MESH)

        @pl.when(y > 0)
        def _():
            pl.semaphore_signal(barrier, inc=1, device_id={"axial": y * NZ - 1}, device_id_type=MESH)

    loads[0].wait()
    loads[1].wait()
    for t in range(tiles):
        sb[t, 0:local, :] = s0[:, t, :]
        sb[t, local:both, :] = f[:, t, :]
    row = lax.broadcasted_iota(jnp.int32, (cols, width), 0)
    col = lax.broadcasted_iota(jnp.int32, (cols, width), 1)
    ps[0:cols] = jnp.where(col == row + i * cols, 1.0, 0.0).astype(F32)
    ps[cols:] = jnp.zeros((both, width), F32)
    gs[...] = jnp.zeros((cols + both, width), F32)

    def first(xx, sender):
        return remote(sb.at[pl.ds(per * xx, per)], rb.at[sender], x1_send.at[xx], x1_recv.at[sender], inst=2 * xx)

    def second(d):
        xx = lax.rem(x + d, chips)
        return remote(ob.at[xx], rq.at[pl.ds(per * x, per)], x2_send.at[d], x2_recv.at[d], inst=2 * xx)

    def gather(src, dst, send, recv, xx, sender):
        half = pl.ds(pl.multiple_of(lax.rem(sender, 2) * cols, 8), cols)
        return remote(src.at[0:cols], dst.at[sender // 2, half], send.at[xx], recv.at[sender], inst=2 * xx + 1)

    def whole(xx, sender):
        return gather(tx, tg, g1_send, g1_recv, xx, sender)

    def halfway(xx, sender):
        return gather(txm, tgm, gm_send, gm_recv, xx, sender)

    def raw_whole(xx, sender):
        return remote(tx.at[cols:cols + both], raw.at[sender], r1_send.at[xx], r1_recv.at[sender], inst=2 * xx + 1)

    def raw_half(xx, sender):
        return remote(txm.at[cols:cols + both], rawm.at[sender], rm_send.at[xx], rm_recv.at[sender], inst=2 * xx + 1)

    def to_hubs(copy):
        for xx in range(chips):
            @pl.when(2 * xx + 1 != i)
            def _(xx=xx):
                copy(xx, i).start()

    other = i + 1 - 2 * core
    pass_rq = remote(rq, rq, pair_sem.at[0], pair_sem.at[1], inst=other)
    give = remote(vin.at[0], vin.at[1], pair_sem.at[4], pair_sem.at[5], inst=other)
    early = remote(u.at[pl.ds(0, mid)], u.at[pl.ds(0, mid)], pair_sem.at[6], pair_sem.at[7], inst=other)
    late = remote(u.at[pl.ds(mid, mid)], u.at[pl.ds(mid, mid)], pair_sem.at[8], pair_sem.at[9], inst=other)

    for load in loads[2:]:
        load.wait()

    def nt_dot(v, w):
        return lax.dot_general(v, w, NT, preferred_element_type=F32)

    def joined(v):
        m = v.shape[0] // 2
        return v[:m] + v[m:]

    def driven(t, b):
        return jnp.concatenate([-b[:cols], sb[t] - b[cols:]], 0)

    t = order[0]
    ps[...] = times(driven(t, times(ps[...], wc[t])), wa[t])

    def column_steps(start, made):
        def steps(n, carry):
            p, g = ps[...], gs[...]
            for j in range(UNROLL):
                k = start + n * UNROLL + j
                before, here = order[k], order[jnp.minimum(k + 1, tiles - 1)]
                high_p, high_g = split(p), split(g)
                bp, bg = nt_dot(high_p, wc[here]), nt_dot(high_g, wc[before])
                last_p = p
                bp, bg = driven(here, joined(bp)), p + joined(bg)
                p, g = nt_dot(split(bp), wa[here]), nt_dot(split(bg), wa[before])
                p, g = joined(p), -joined(g)
            ps[...] = p
            gs[...] = g
            pv[...] = last_p
            return carry
        lax.fori_loop(0, mid // UNROLL, steps, 0)
        made[...] = pack(pv[...], gs[...])

    column_steps(0, txm)

    pl.semaphore_wait(barrier, n_inst - 1 + jnp.where(
        hub, 2 + jnp.where(lead, NZ, 0) + jnp.where(y > 0, 1, 0), 0))
    for xx in range(chips):
        @pl.when(2 * xx != i)
        def _(xx=xx):
            first(xx, i).start()

    column_steps(mid, tx)
    to_hubs(whole)
    to_hubs(raw_whole)

    for t in range(tiles):
        pos = jnp.int32(0)
        for k in range(tiles):
            pos = jnp.where(order[k] == t, k, pos)
        inv[t] = pos

    pad = nt.shape[2] // 2

    def prepare(n, carry):
        t = order[mid * core + n]
        turned = wa[t].T
        at[n] = turned
        high, low = halves(lax.dot_general(wc[t].T, turned, NN, preferred_element_type=F32))
        nt[n, :, 0:width] = high
        nt[n, :, pad:pad + width] = low
        return carry

    def drive(n, carry):
        ya[n] = times(rq[order[mid * core + n]], at[n], NN)
        return carry

    def by_pair(v, n):
        m = joined(lax.dot_general(split(v), nt[n], NN, preferred_element_type=F32))
        return m[:, :width] + m[:, pad:pad + width]

    def rerun(p, g):
        p = ya[0, 0:both] - by_pair(p, 0)
        for n in range(mid):
            old = p
            if n + 1 < mid:
                p = ya[n + 1, 0:both] - by_pair(old, n + 1)
            g = ya[n, both:] - by_pair(g, n) - times(old, at[n], NN)
            u[mid * core + n] = g

    zero = jnp.zeros((both, width), F32)

    @pl.when(core == 0)
    def _():
        rb[i] = sb[pl.ds(per * x, per)]
        for j in range(n_inst):
            @pl.when(j != i)
            def _(j=j):
                first(0, j).wait_recv()
        for t in range(per):
            mixed = jnp.dot(kmat[:, 0:both * n_inst], rb[:, t].reshape(both * n_inst, width),
                            precision=lax.Precision.HIGHEST, preferred_element_type=F32)
            ob[:, t] = mixed.reshape(chips, 2 * both, width)
        lax.fori_loop(0, mid, prepare, 0)
        for d in range(1, chips):
            second(d).start()
        rq[pl.ds(per * x, per)] = ob[x]
        to_hubs(raw_half)
        to_hubs(halfway)
        for d in range(1, chips):
            second(d).wait_recv()
        pass_rq.start()
        lax.fori_loop(0, mid, drive, 0)
        give.wait_recv()
        rerun(vin[1, 0:both], vin[1, both:])
        early.start()
        late.wait_recv()
        for t in range(tiles):
            out[:, t, :] = s0[:, t, :] + u[inv[t], 0:local, :]
        early.wait_send()
        pass_rq.wait_send()
        for d in range(1, chips):
            second(d).wait_send()

    @pl.when(hub)
    def _():
        def scan(c):
            part = pl.ds(pl.multiple_of(c * CHUNK, CHUNK), CHUNK)
            return remote(so.at[part], si.at[part], sc_send.at[c], sc_recv.at[c],
                          axial=y * NZ + lax.rem(z + 1, NZ))

        scan_data = remote(so.at[data], si.at[data], sd_sem.at[0], sd_sem.at[1],
                           axial=y * NZ + lax.rem(z + 1, NZ))

        def spread(src, c, d):
            part = pl.ds(pl.multiple_of(c * CHUNK, CHUNK), CHUNK)
            return remote(src.at[part], pm.at[x, part], g2_send.at[d - 1, c], g2_recv.at[d - 1, c],
                          inst=lax.rem(i + 2 * d, n_inst))

        def down(zz):
            return remote(uin.at[0], uin.at[1], up_send.at[zz], up_recv.at[0],
                          axial=lax.rem(y + 1, last + 1) * NZ + zz)

        def mix(rows):
            made = [jnp.dot(kmat[pl.ds(pl.multiple_of(2 * both * x, 8), 2 * both), 0:both * n_inst], part,
                            precision=lax.Precision.HIGHEST, preferred_element_type=F32)
                    for part in unpack(rows[...].reshape(both * n_inst, 2 * width))]
            return made[0][:both], made[0][both:] + made[1][:both]

        count = jnp.where(y == 0, 0, chunks)

        tg[x, pl.ds(cols, cols)] = tx[0:cols]
        tgm[x, pl.ds(cols, cols)] = txm[0:cols]
        raw[i] = tx[cols:]
        rawm[i] = txm[cols:]
        whole(0, i - 1).wait_recv()

        @pl.when((z == 0) & (y > 0))
        def _():
            so[0:block] = tg[x]
            lax.fori_loop(0, count, lambda c, k: (scan(c).start(), k)[1], 0)

        lax.fori_loop(0, mid, prepare, 0)
        store_map(tw, block * x, tg[x])
        for d in FAR_LAST:
            there = lax.rem(x + d, chips)
            for j in range(2):
                whole(0, 2 * there + j).wait_recv()
            store_map(tw, block * there, tg[there])

        to_hubs(raw_half)
        to_hubs(halfway)

        @pl.when(z > 0)
        def _():
            def chunk_step(c, carry):
                scan(c).wait_recv()
                part = pl.ds(pl.multiple_of(c * CHUNK, CHUNK), CHUNK)

                @pl.when(z < NZ - 1)
                def _():
                    so[part] = pack(*through(tw, *unpack(si[part])))
                    scan(c).start()

                for d in FAR_FIRST:
                    spread(si, c, d).start()
                return carry

            lax.fori_loop(0, count, chunk_step, 0)

        for j in range(n_inst):
            @pl.when(j != i)
            def _(j=j):
                raw_whole(0, j).wait_recv()
        bp, bg = mix(raw)

        @pl.when(z == 0)
        def _():
            so[data] = pack(bp, bg)
            scan_data.start()

        @pl.when(z > 0)
        def _():
            scan_data.wait_recv()

            @pl.when((z < NZ - 1) | (y == 0))
            def _():
                p, g = through(tw, *unpack(si[data]))
                so[data] = pack(p + bp, g + bg)

            @pl.when(z < NZ - 1)
            def _():
                scan_data.start()

        @pl.when((y == 0) & (z == NZ - 1))
        def _():
            uin[0] = so[data]
            for zz in range(NZ):
                down(zz).start()

        def give_out(p, g):
            vin[0, 0:both] = p
            vin[0, both:] = g
            give.start()

        @pl.when(y == 0)
        def _():
            @pl.when(z == 0)
            def _():
                give_out(zero, zero)

            @pl.when(z > 0)
            def _():
                give_out(*unpack(si[data]))

        pass_rq.wait_recv()
        lax.fori_loop(0, mid, drive, 0)
        for j in range(n_inst):
            @pl.when(j != i)
            def _(j=j):
                raw_half(0, j).wait_recv()
                halfway(0, j).wait_recv()
        mp, mg = mix(rawm)
        for xx in range(chips):
            store_map(tq, block * xx, tgm[xx])

        @pl.when(mapped)
        def _():
            store_map(tp, block * x, si[0:block])
            for d in FAR_LAST:
                there = lax.rem(x + chips - d, chips)
                for c in range(chunks):
                    spread(si, c, d).wait_recv()
                store_map(tp, block * there, pm[there])

        @pl.when(y > 0)
        def _():
            down(0).wait_recv()

        @pl.when(mapped)
        def _():
            p, g = through(tp, *unpack(uin[1]))
            own_p, own_g = unpack(si[data])
            p, g = p + own_p, g + own_g

            @pl.when(lead)
            def _():
                next_p, next_g = through(tw, p, g)
                uin[0] = pack(next_p + bp, next_g + bg)
                for zz in range(NZ):
                    down(zz).start()

            give_out(p, g)

        @pl.when((y > 0) & (z == 0))
        def _():
            give_out(*unpack(uin[1]))

        p, g = through(tq, vin[0, 0:both], vin[0, both:])
        rerun(p + mp, g + mg)
        late.start()
        early.wait_recv()
        for t in range(tiles):
            out[:, t, :] = s0[:, t, :] + u[inv[t], local:both, :]

        late.wait_send()
        give.wait_send()

        @pl.when(z < NZ - 1)
        def _():
            scan_data.wait_send()
            lax.fori_loop(0, count, lambda c, k: (scan(c).wait_send(), k)[1], 0)

        @pl.when(mapped)
        def _():
            for d in range(1, chips):
                for c in range(chunks):
                    spread(si, c, d).wait_send()

        @pl.when(lead)
        def _():
            for zz in range(NZ):
                down(zz).wait_send()

    for xx in range(chips):
        @pl.when(2 * xx != i)
        def _(xx=xx):
            first(xx, i).wait_send()

        @pl.when(2 * xx + 1 != i)
        def _(xx=xx):
            whole(xx, i).wait_send()
            halfway(xx, i).wait_send()
            raw_whole(xx, i).wait_send()
            raw_half(xx, i).wait_send()


def solution(mesh):
    n_inst, n_axial = mesh.shape["inst"], mesh.shape["axial"]

    def on_device(flow_state, forcing, tile_inverse, coupling, sweep_order):
        local, tiles, width = flow_state.shape
        chips = n_inst // 2
        per = tiles // chips
        cols = width // n_inst
        block = 2 * cols
        pad = -(-width // 128) * 128
        both = 2 * local
        chunks = block // CHUNK
        size = both * n_inst
        kmat = np.zeros((10 * size, 128), np.float32)
        kmat[:size, :size] = exchange_matrix(local * n_inst, n_inst)
        kmat = jnp.asarray(kmat)
        hbm = pl.BlockSpec(memory_space=pl.ANY)
        vmem = pl.BlockSpec(memory_space=pltpu.VMEM)
        dma = pltpu.SemaphoreType.DMA
        return pl.pallas_call(
            functools.partial(kernel, n_inst, n_axial),
            out_shape=jax.ShapeDtypeStruct(flow_state.shape, F32),
            in_specs=[pl.BlockSpec(memory_space=pltpu.SMEM), hbm, hbm, hbm, hbm, hbm],
            out_specs=vmem,
            scratch_shapes=[
                pltpu.VMEM((size, 128), F32),
                pltpu.VMEM(flow_state.shape, F32),
                pltpu.VMEM(flow_state.shape, F32),
                pltpu.VMEM((tiles, width, width), BF16),
                pltpu.VMEM((tiles, width, width), BF16),
                pltpu.VMEM((tiles, both, width), F32),
                pltpu.VMEM((n_inst, per, both, width), F32),
                pltpu.VMEM((chips, per, 2 * both, width), F32),
                pltpu.VMEM((tiles, 2 * both, width), F32),
                pltpu.VMEM((tiles, both, width), F32),
                pltpu.VMEM((cols + both, width), F32),
                pltpu.VMEM((cols + both, width), F32),
                pltpu.VMEM((cols + both, width), F32),
                pltpu.VMEM((cols + both, 2 * width), F32),
                pltpu.VMEM((cols + both, 2 * width), F32),
                pltpu.VMEM((chips, block, 2 * width), F32),
                pltpu.VMEM((chips, block, 2 * width), F32),
                pltpu.VMEM((n_inst, both, 2 * width), F32),
                pltpu.VMEM((n_inst, both, 2 * width), F32),
                pltpu.VMEM((width, 4 * pad), BF16),
                pltpu.VMEM((width, 4 * pad), BF16),
                pltpu.VMEM((width, 4 * pad), BF16),
                pltpu.VMEM((block + both, 2 * width), F32),
                pltpu.VMEM((block + both, 2 * width), F32),
                pltpu.VMEM((chips, block, 2 * width), F32),
                pltpu.VMEM((2, both, 2 * width), F32),
                pltpu.VMEM((2, 2 * both, width), F32),
                pltpu.VMEM((tiles // 2, width, width), BF16),
                pltpu.VMEM((tiles // 2, width, 2 * pad), BF16),
                pltpu.VMEM((tiles // 2, 2 * both, width), F32),
                pltpu.SMEM((tiles,), jnp.int32),
                dma((5,)),
                dma((chips,)), dma((n_inst,)), dma((chips,)), dma((chips,)),
                dma((chips,)), dma((n_inst,)), dma((chips,)), dma((n_inst,)),
                dma((chips,)), dma((n_inst,)), dma((chips,)), dma((n_inst,)),
                dma((10,)),
                dma((chunks,)), dma((chunks,)), dma((2,)),
                dma((chips - 1, chunks)), dma((chips - 1, chunks)),
                dma((NZ,)), dma((1,)),
            ],
            compiler_params=pltpu.CompilerParams(collective_id=0, has_side_effects=True, vmem_limit_bytes=VMEM_BYTES),
        )(sweep_order, kmat, flow_state, forcing, tile_inverse, coupling)

    return jax.shard_map(
        on_device,
        mesh=mesh,
        in_specs=(P("inst", "axial", None), P("inst", "axial", None), P("axial", None, None),
                  P("axial", None, None), P("axial")),
        out_specs=P("inst", "axial", None),
        check_vma=False,
    )
```

```python
import functools

import jax
import jax.numpy as jnp
import numpy as np
from jax import lax
from jax.experimental import pallas as pl
from jax.experimental.pallas import tpu as pltpu
from jax.sharding import PartitionSpec as P

ITERS = 2
SPECTRAL_GAIN = 2.0
NZ = 8
VMEM_BYTES = 56_400_000
FAR_FIRST, FAR_LAST = (2, 1, 3), (1, 3, 2)
UNROLL = 4
CHUNK = 8
MESH = pl.DeviceIdType.MESH
F32, BF16 = jnp.float32, jnp.bfloat16
NT = (((1,), (1,)), ((), ()))
NN = (((1,), (0,)), ((), ()))


def exchange_matrix(period, groups):
    idx = np.arange(period)
    dist = idx[:, None] - idx[None, :]
    angle = np.pi * dist / period
    safe = np.where(dist == 0, 1.0, np.sin(angle))
    deriv = np.where(dist == 0, 0.0, 0.5 * (1.0 - 2.0 * (dist % 2)) * np.cos(angle) / safe)
    e = deriv * (SPECTRAL_GAIN / period) + np.eye(period)
    whole = np.block([[-e @ e, e], [-2.0 * e, 2.0 * np.eye(period)]])
    local = period // groups
    given = [part * period + dev * local + n for dev in range(groups) for part in range(2) for n in range(local)]
    wide = 2 * local
    made = [part * period + chip * wide + n for chip in range(groups // 2) for part in range(2) for n in range(wide)]
    return whole[np.ix_(made, given)].astype(np.float32)


def halves(x):
    high = x.astype(BF16)
    low = (x - high.astype(F32)).astype(BF16)
    return high, low


def split(x):
    high = x.astype(BF16).astype(F32)
    return jnp.concatenate([high, x - high], 0).astype(BF16)


def times(x, w, dims=NT):
    m = x.shape[0]
    y = lax.dot_general(split(x), w, dims, preferred_element_type=F32)
    return y[:m] + y[m:]


def pack(p, g):
    whole = p.shape[1] // 128 * 128
    return jnp.concatenate([p[:, :whole], g[:, :whole], p[:, whole:], g[:, whole:]], 1)


def unpack(b):
    width = b.shape[1] // 2
    whole = width // 128 * 128
    middle = whole + width
    return (jnp.concatenate([b[:, :whole], b[:, 2 * whole:middle]], 1),
            jnp.concatenate([b[:, whole:2 * whole], b[:, middle:]], 1))


def store_map(dst, row, block):
    pad = dst.shape[1] // 4
    for part, rows in enumerate(unpack(block)):
        width = rows.shape[1]
        at = pl.ds(pl.multiple_of(row, 16), rows.shape[0])
        high, low = halves(rows)
        dst[at, part * pad:part * pad + width] = high
        dst[at, (2 + part) * pad:(2 + part) * pad + width] = low


def through(m, p, g):
    rows, width = p.shape
    pad = m.shape[1] // 4
    y = lax.dot_general(split(jnp.concatenate([p, g], 0)), m[...], NN, preferred_element_type=F32)
    y = y[:2 * rows] + y[2 * rows:]
    y = y[:, :2 * pad] + y[:, 2 * pad:]
    return y[:rows, :width], y[rows:, :width] + y[:rows, pad:pad + width]


def kernel(n_inst, n_axial, order, k_hbm, s_hbm, f_hbm, a_hbm, c_hbm, out,
           kmat, s0, f, wa, wc, sb, rb, ob, rq, u, ps, gs, pv, tx, txm, tg, tgm, raw, rawm, tw, tp, tq, si, so, pm, uin, vin, at, nt, ya, inv,
           w_sem, x1_send, x1_recv, x2_send, x2_recv, g1_send, g1_recv, gm_send, gm_recv, r1_send, r1_recv, rm_send, rm_recv, pair_sem,
           sc_send, sc_recv, sd_sem, g2_send, g2_recv, up_send, up_recv):
    i = lax.axis_index("inst")
    a = lax.axis_index("axial")
    local, tiles, width = s0.shape
    chips = n_inst // 2
    per = tiles // chips
    mid = tiles // 2
    cols = width // n_inst
    block = 2 * cols
    both = 2 * local
    x, core = i // 2, lax.rem(i, 2)
    y, z = a // NZ, lax.rem(a, NZ)
    last = n_axial // NZ - 1
    chunks = block // CHUNK
    hub = core == 1
    lead = (z == NZ - 1) & (y < last)
    mapped = (y > 0) & (z > 0)
    data = pl.ds(block, both)

    loads = [pltpu.make_async_copy(src, dst, w_sem.at[n]) for n, (src, dst) in enumerate(
        [(s_hbm, s0), (f_hbm, f), (c_hbm, wc), (a_hbm, wa), (k_hbm.at[pl.ds(0, kmat.shape[0])], kmat)])]
    for load in loads:
        load.start()

    def remote(src, dst, send, recv, **there):
        return pltpu.make_async_remote_copy(
            src_ref=src, dst_ref=dst, send_sem=send, recv_sem=recv, device_id=there, device_id_type=MESH)

    barrier = pltpu.get_barrier_semaphore()
    for d in range(1, n_inst):
        pl.semaphore_signal(barrier, inc=1, device_id={"inst": lax.rem(i + d, n_inst)}, device_id_type=MESH)

    @pl.when(hub)
    def _():
        for d in (1, NZ - 1):
            there = y * NZ + lax.rem(z + d, NZ)
            pl.semaphore_signal(barrier, inc=1, device_id={"axial": there}, device_id_type=MESH)

        @pl.when(lead)
        def _():
            for zz in range(NZ):
                pl.semaphore_signal(barrier, inc=1, device_id={"axial": (y + 1) * NZ + zz}, device_id_type=MESH)

        @pl.when(y > 0)
        def _():
            pl.semaphore_signal(barrier, inc=1, device_id={"axial": y * NZ - 1}, device_id_type=MESH)

    loads[0].wait()
    loads[1].wait()
    for t in range(tiles):
        sb[t, 0:local, :] = s0[:, t, :]
        sb[t, local:both, :] = f[:, t, :]
    row = lax.broadcasted_iota(jnp.int32, (cols, width), 0)
    col = lax.broadcasted_iota(jnp.int32, (cols, width), 1)
    ps[0:cols] = jnp.where(col == row + i * cols, 1.0, 0.0).astype(F32)
    ps[cols:] = jnp.zeros((both, width), F32)
    gs[...] = jnp.zeros((cols + both, width), F32)

    def first(xx, sender):
        return remote(sb.at[pl.ds(per * xx, per)], rb.at[sender], x1_send.at[xx], x1_recv.at[sender], inst=2 * xx)

    def second(d):
        xx = lax.rem(x + d, chips)
        return remote(ob.at[xx], rq.at[pl.ds(per * x, per)], x2_send.at[d], x2_recv.at[d], inst=2 * xx)

    def gather(src, dst, send, recv, xx, sender):
        half = pl.ds(pl.multiple_of(lax.rem(sender, 2) * cols, 8), cols)
        return remote(src.at[0:cols], dst.at[sender // 2, half], send.at[xx], recv.at[sender], inst=2 * xx + 1)

    def whole(xx, sender):
        return gather(tx, tg, g1_send, g1_recv, xx, sender)

    def halfway(xx, sender):
        return gather(txm, tgm, gm_send, gm_recv, xx, sender)

    def raw_whole(xx, sender):
        return remote(tx.at[cols:cols + both], raw.at[sender], r1_send.at[xx], r1_recv.at[sender], inst=2 * xx + 1)

    def raw_half(xx, sender):
        return remote(txm.at[cols:cols + both], rawm.at[sender], rm_send.at[xx], rm_recv.at[sender], inst=2 * xx + 1)

    def to_hubs(copy):
        for xx in range(chips):
            @pl.when(2 * xx + 1 != i)
            def _(xx=xx):
                copy(xx, i).start()

    other = i + 1 - 2 * core
    pass_rq = remote(rq, rq, pair_sem.at[0], pair_sem.at[1], inst=other)
    give = remote(vin.at[0], vin.at[1], pair_sem.at[4], pair_sem.at[5], inst=other)
    early = remote(u.at[pl.ds(0, mid)], u.at[pl.ds(0, mid)], pair_sem.at[6], pair_sem.at[7], inst=other)
    late = remote(u.at[pl.ds(mid, mid)], u.at[pl.ds(mid, mid)], pair_sem.at[8], pair_sem.at[9], inst=other)

    for load in loads[2:]:
        load.wait()

    def nt_dot(v, w):
        return lax.dot_general(v, w, NT, preferred_element_type=F32)

    def joined(v):
        m = v.shape[0] // 2
        return v[:m] + v[m:]

    def driven(t, b):
        return jnp.concatenate([-b[:cols], sb[t] - b[cols:]], 0)

    t = order[0]
    ps[...] = times(driven(t, times(ps[...], wc[t])), wa[t])

    def column_steps(start, made):
        def steps(n, carry):
            p, g = ps[...], gs[...]
            for j in range(UNROLL):
                k = start + n * UNROLL + j
                before, here = order[k], order[jnp.minimum(k + 1, tiles - 1)]
                high_p, high_g = split(p), split(g)
                bp, bg = nt_dot(high_p, wc[here]), nt_dot(high_g, wc[before])
                last_p = p
                bp, bg = driven(here, joined(bp)), p + joined(bg)
                p, g = nt_dot(split(bp), wa[here]), nt_dot(split(bg), wa[before])
                p, g = joined(p), -joined(g)
            ps[...] = p
            gs[...] = g
            pv[...] = last_p
            return carry
        lax.fori_loop(0, mid // UNROLL, steps, 0)
        made[...] = pack(pv[...], gs[...])

    column_steps(0, txm)

    pl.semaphore_wait(barrier, n_inst - 1 + jnp.where(
        hub, 2 + jnp.where(lead, NZ, 0) + jnp.where(y > 0, 1, 0), 0))
    for xx in range(chips):
        @pl.when(2 * xx != i)
        def _(xx=xx):
            first(xx, i).start()

    column_steps(mid, tx)
    to_hubs(whole)
    to_hubs(raw_whole)

    for t in range(tiles):
        pos = jnp.int32(0)
        for k in range(tiles):
            pos = jnp.where(order[k] == t, k, pos)
        inv[t] = pos

    pad = nt.shape[2] // 2

    def prepare(n, carry):
        t = order[mid * core + n]
        turned = wa[t].T
        at[n] = turned
        high, low = halves(lax.dot_general(wc[t].T, turned, NN, preferred_element_type=F32))
        nt[n, :, 0:width] = high
        nt[n, :, pad:pad + width] = low
        return carry

    def drive(n, carry):
        ya[n] = times(rq[order[mid * core + n]], at[n], NN)
        return carry

    def by_pair(v, n):
        m = joined(lax.dot_general(split(v), nt[n], NN, preferred_element_type=F32))
        return m[:, :width] + m[:, pad:pad + width]

    def rerun(p, g):
        p = ya[0, 0:both] - by_pair(p, 0)
        for n in range(mid):
            old = p
            if n + 1 < mid:
                p = ya[n + 1, 0:both] - by_pair(old, n + 1)
            g = ya[n, both:] - by_pair(g, n) - times(old, at[n], NN)
            u[mid * core + n] = g

    zero = jnp.zeros((both, width), F32)

    @pl.when(core == 0)
    def _():
        rb[i] = sb[pl.ds(per * x, per)]
        for j in range(n_inst):
            @pl.when(j != i)
            def _(j=j):
                first(0, j).wait_recv()
        for t in range(per):
            mixed = jnp.dot(kmat[:, 0:both * n_inst], rb[:, t].reshape(both * n_inst, width),
                            precision=lax.Precision.HIGHEST, preferred_element_type=F32)
            ob[:, t] = mixed.reshape(chips, 2 * both, width)
        lax.fori_loop(0, mid, prepare, 0)
        for d in range(1, chips):
            second(d).start()
        rq[pl.ds(per * x, per)] = ob[x]
        to_hubs(raw_half)
        to_hubs(halfway)
        for d in range(1, chips):
            second(d).wait_recv()
        pass_rq.start()
        lax.fori_loop(0, mid, drive, 0)
        give.wait_recv()
        rerun(vin[1, 0:both], vin[1, both:])
        early.start()
        late.wait_recv()
        for t in range(tiles):
            out[:, t, :] = s0[:, t, :] + u[inv[t], 0:local, :]
        early.wait_send()
        pass_rq.wait_send()
        for d in range(1, chips):
            second(d).wait_send()

    @pl.when(hub)
    def _():
        def scan(c):
            part = pl.ds(pl.multiple_of(c * CHUNK, CHUNK), CHUNK)
            return remote(so.at[part], si.at[part], sc_send.at[c], sc_recv.at[c],
                          axial=y * NZ + lax.rem(z + 1, NZ))

        scan_data = remote(so.at[data], si.at[data], sd_sem.at[0], sd_sem.at[1],
                           axial=y * NZ + lax.rem(z + 1, NZ))

        def spread(src, c, d):
            part = pl.ds(pl.multiple_of(c * CHUNK, CHUNK), CHUNK)
            return remote(src.at[part], pm.at[x, part], g2_send.at[d - 1, c], g2_recv.at[d - 1, c],
                          inst=lax.rem(i + 2 * d, n_inst))

        def down(zz):
            return remote(uin.at[0], uin.at[1], up_send.at[zz], up_recv.at[0],
                          axial=lax.rem(y + 1, last + 1) * NZ + zz)

        def mix(rows):
            made = [jnp.dot(kmat[pl.ds(pl.multiple_of(2 * both * x, 8), 2 * both), 0:both * n_inst], part,
                            precision=lax.Precision.HIGHEST, preferred_element_type=F32)
                    for part in unpack(rows[...].reshape(both * n_inst, 2 * width))]
            return made[0][:both], made[0][both:] + made[1][:both]

        count = jnp.where(y == 0, 0, chunks)

        tg[x, pl.ds(cols, cols)] = tx[0:cols]
        tgm[x, pl.ds(cols, cols)] = txm[0:cols]
        raw[i] = tx[cols:]
        rawm[i] = txm[cols:]
        whole(0, i - 1).wait_recv()

        @pl.when((z == 0) & (y > 0))
        def _():
            so[0:block] = tg[x]
            lax.fori_loop(0, count, lambda c, k: (scan(c).start(), k)[1], 0)

        lax.fori_loop(0, mid, prepare, 0)
        store_map(tw, block * x, tg[x])
        for d in FAR_LAST:
            there = lax.rem(x + d, chips)
            for j in range(2):
                whole(0, 2 * there + j).wait_recv()
            store_map(tw, block * there, tg[there])

        to_hubs(raw_half)
        to_hubs(halfway)

        @pl.when(z > 0)
        def _():
            def chunk_step(c, carry):
                scan(c).wait_recv()
                part = pl.ds(pl.multiple_of(c * CHUNK, CHUNK), CHUNK)

                @pl.when(z < NZ - 1)
                def _():
                    so[part] = pack(*through(tw, *unpack(si[part])))
                    scan(c).start()

                for d in FAR_FIRST:
                    spread(si, c, d).start()
                return carry

            lax.fori_loop(0, count, chunk_step, 0)

        for j in range(n_inst):
            @pl.when(j != i)
            def _(j=j):
                raw_whole(0, j).wait_recv()
        bp, bg = mix(raw)

        @pl.when(z == 0)
        def _():
            so[data] = pack(bp, bg)
            scan_data.start()

        @pl.when(z > 0)
        def _():
            scan_data.wait_recv()

            @pl.when((z < NZ - 1) | (y == 0))
            def _():
                p, g = through(tw, *unpack(si[data]))
                so[data] = pack(p + bp, g + bg)

            @pl.when(z < NZ - 1)
            def _():
                scan_data.start()

        @pl.when((y == 0) & (z == NZ - 1))
        def _():
            uin[0] = so[data]
            for zz in range(NZ):
                down(zz).start()

        def give_out(p, g):
            vin[0, 0:both] = p
            vin[0, both:] = g
            give.start()

        @pl.when(y == 0)
        def _():
            @pl.when(z == 0)
            def _():
                give_out(zero, zero)

            @pl.when(z > 0)
            def _():
                give_out(*unpack(si[data]))

        pass_rq.wait_recv()
        lax.fori_loop(0, mid, drive, 0)
        for j in range(n_inst):
            @pl.when(j != i)
            def _(j=j):
                raw_half(0, j).wait_recv()
                halfway(0, j).wait_recv()
        mp, mg = mix(rawm)
        for xx in range(chips):
            store_map(tq, block * xx, tgm[xx])

        @pl.when(mapped)
        def _():
            store_map(tp, block * x, si[0:block])
            for d in FAR_LAST:
                there = lax.rem(x + chips - d, chips)
                for c in range(chunks):
                    spread(si, c, d).wait_recv()
                store_map(tp, block * there, pm[there])

        @pl.when(y > 0)
        def _():
            down(0).wait_recv()

        @pl.when(mapped)
        def _():
            p, g = through(tp, *unpack(uin[1]))
            own_p, own_g = unpack(si[data])
            p, g = p + own_p, g + own_g

            @pl.when(lead)
            def _():
                next_p, next_g = through(tw, p, g)
                uin[0] = pack(next_p + bp, next_g + bg)
                for zz in range(NZ):
                    down(zz).start()

            give_out(p, g)

        @pl.when((y > 0) & (z == 0))
        def _():
            give_out(*unpack(uin[1]))

        p, g = through(tq, vin[0, 0:both], vin[0, both:])
        rerun(p + mp, g + mg)
        late.start()
        early.wait_recv()
        for t in range(tiles):
            out[:, t, :] = s0[:, t, :] + u[inv[t], local:both, :]

        late.wait_send()
        give.wait_send()

        @pl.when(z < NZ - 1)
        def _():
            scan_data.wait_send()
            lax.fori_loop(0, count, lambda c, k: (scan(c).wait_send(), k)[1], 0)

        @pl.when(mapped)
        def _():
            for d in range(1, chips):
                for c in range(chunks):
                    spread(si, c, d).wait_send()

        @pl.when(lead)
        def _():
            for zz in range(NZ):
                down(zz).wait_send()

    for xx in range(chips):
        @pl.when(2 * xx != i)
        def _(xx=xx):
            first(xx, i).wait_send()

        @pl.when(2 * xx + 1 != i)
        def _(xx=xx):
            whole(xx, i).wait_send()
            halfway(xx, i).wait_send()
            raw_whole(xx, i).wait_send()
            raw_half(xx, i).wait_send()


def solution(mesh):
    n_inst, n_axial = mesh.shape["inst"], mesh.shape["axial"]

    def on_device(flow_state, forcing, tile_inverse, coupling, sweep_order):
        local, tiles, width = flow_state.shape
        chips = n_inst // 2
        per = tiles // chips
        cols = width // n_inst
        block = 2 * cols
        pad = -(-width // 128) * 128
        both = 2 * local
        chunks = block // CHUNK
        size = both * n_inst
        kmat = np.zeros((10 * size, 128), np.float32)
        kmat[:size, :size] = exchange_matrix(local * n_inst, n_inst)
        kmat = jnp.asarray(kmat)
        hbm = pl.BlockSpec(memory_space=pl.ANY)
        vmem = pl.BlockSpec(memory_space=pltpu.VMEM)
        dma = pltpu.SemaphoreType.DMA
        return pl.pallas_call(
            functools.partial(kernel, n_inst, n_axial),
            out_shape=jax.ShapeDtypeStruct(flow_state.shape, F32),
            in_specs=[pl.BlockSpec(memory_space=pltpu.SMEM), hbm, hbm, hbm, hbm, hbm],
            out_specs=vmem,
            scratch_shapes=[
                pltpu.VMEM((size, 128), F32),
                pltpu.VMEM(flow_state.shape, F32),
                pltpu.VMEM(flow_state.shape, F32),
                pltpu.VMEM((tiles, width, width), BF16),
                pltpu.VMEM((tiles, width, width), BF16),
                pltpu.VMEM((tiles, both, width), F32),
                pltpu.VMEM((n_inst, per, both, width), F32),
                pltpu.VMEM((chips, per, 2 * both, width), F32),
                pltpu.VMEM((tiles, 2 * both, width), F32),
                pltpu.VMEM((tiles, both, width), F32),
                pltpu.VMEM((cols + both, width), F32),
                pltpu.VMEM((cols + both, width), F32),
                pltpu.VMEM((cols + both, width), F32),
                pltpu.VMEM((cols + both, 2 * width), F32),
                pltpu.VMEM((cols + both, 2 * width), F32),
                pltpu.VMEM((chips, block, 2 * width), F32),
                pltpu.VMEM((chips, block, 2 * width), F32),
                pltpu.VMEM((n_inst, both, 2 * width), F32),
                pltpu.VMEM((n_inst, both, 2 * width), F32),
                pltpu.VMEM((width, 4 * pad), BF16),
                pltpu.VMEM((width, 4 * pad), BF16),
                pltpu.VMEM((width, 4 * pad), BF16),
                pltpu.VMEM((block + both, 2 * width), F32),
                pltpu.VMEM((block + both, 2 * width), F32),
                pltpu.VMEM((chips, block, 2 * width), F32),
                pltpu.VMEM((2, both, 2 * width), F32),
                pltpu.VMEM((2, 2 * both, width), F32),
                pltpu.VMEM((tiles // 2, width, width), BF16),
                pltpu.VMEM((tiles // 2, width, 2 * pad), BF16),
                pltpu.VMEM((tiles // 2, 2 * both, width), F32),
                pltpu.SMEM((tiles,), jnp.int32),
                dma((5,)),
                dma((chips,)), dma((n_inst,)), dma((chips,)), dma((chips,)),
                dma((chips,)), dma((n_inst,)), dma((chips,)), dma((n_inst,)),
                dma((chips,)), dma((n_inst,)), dma((chips,)), dma((n_inst,)),
                dma((10,)),
                dma((chunks,)), dma((chunks,)), dma((2,)),
                dma((chips - 1, chunks)), dma((chips - 1, chunks)),
                dma((NZ,)), dma((1,)),
            ],
            compiler_params=pltpu.CompilerParams(collective_id=0, has_side_effects=True, vmem_limit_bytes=VMEM_BYTES),
        )(sweep_order, kmat, flow_state, forcing, tile_inverse, coupling)

    return jax.shard_map(
        on_device,
        mesh=mesh,
        in_specs=(P("inst", "axial", None), P("inst", "axial", None), P("axial", None, None),
                  P("axial", None, None), P("axial")),
        out_specs=P("inst", "axial", None),
        check_vma=False,
    )
```

```python
import functools

import jax
import jax.numpy as jnp
import numpy as np
from jax import lax
from jax.experimental import pallas as pl
from jax.experimental.pallas import tpu as pltpu
from jax.sharding import PartitionSpec as P

ITERS = 2
SPECTRAL_GAIN = 2.0
NZ = 8
VMEM_BYTES = 56_400_000
FAR_FIRST, FAR_LAST = (2, 1, 3), (1, 3, 2)
UNROLL = 4
CHUNK = 8
MESH = pl.DeviceIdType.MESH
F32, BF16 = jnp.float32, jnp.bfloat16
NT = (((1,), (1,)), ((), ()))
NN = (((1,), (0,)), ((), ()))


def exchange_matrix(period, groups):
    idx = np.arange(period)
    dist = idx[:, None] - idx[None, :]
    angle = np.pi * dist / period
    safe = np.where(dist == 0, 1.0, np.sin(angle))
    deriv = np.where(dist == 0, 0.0, 0.5 * (1.0 - 2.0 * (dist % 2)) * np.cos(angle) / safe)
    e = deriv * (SPECTRAL_GAIN / period) + np.eye(period)
    whole = np.block([[-e @ e, e], [-2.0 * e, 2.0 * np.eye(period)]])
    local = period // groups
    given = [part * period + dev * local + n for dev in range(groups) for part in range(2) for n in range(local)]
    wide = 2 * local
    made = [part * period + chip * wide + n for chip in range(groups // 2) for part in range(2) for n in range(wide)]
    return whole[np.ix_(made, given)].astype(np.float32)


def halves(x):
    high = x.astype(BF16)
    low = (x - high.astype(F32)).astype(BF16)
    return high, low


def split(x):
    high = x.astype(BF16).astype(F32)
    return jnp.concatenate([high, x - high], 0).astype(BF16)


def times(x, w, dims=NT):
    m = x.shape[0]
    y = lax.dot_general(split(x), w, dims, preferred_element_type=F32)
    return y[:m] + y[m:]


def pack(p, g):
    whole = p.shape[1] // 128 * 128
    return jnp.concatenate([p[:, :whole], g[:, :whole], p[:, whole:], g[:, whole:]], 1)


def unpack(b):
    width = b.shape[1] // 2
    whole = width // 128 * 128
    middle = whole + width
    return (jnp.concatenate([b[:, :whole], b[:, 2 * whole:middle]], 1),
            jnp.concatenate([b[:, whole:2 * whole], b[:, middle:]], 1))


def store_map(dst, row, block):
    pad = dst.shape[1] // 4
    for part, rows in enumerate(unpack(block)):
        width = rows.shape[1]
        at = pl.ds(pl.multiple_of(row, 16), rows.shape[0])
        high, low = halves(rows)
        dst[at, part * pad:part * pad + width] = high
        dst[at, (2 + part) * pad:(2 + part) * pad + width] = low


def through(m, p, g):
    rows, width = p.shape
    pad = m.shape[1] // 4
    x = jnp.concatenate([p, g], 0)
    y = lax.dot_general(split(x), m[:, 0:2 * pad], NN, preferred_element_type=F32)
    z = lax.dot_general(x.astype(BF16), m[:, 2 * pad:], NN, preferred_element_type=F32)
    y = y[:2 * rows] + y[2 * rows:] + z
    return y[:rows, :width], y[rows:, :width] + y[:rows, pad:pad + width]


def kernel(n_inst, n_axial, order, k_hbm, s_hbm, f_hbm, a_hbm, c_hbm, out,
           kmat, s0, f, wa, wc, sb, rb, ob, rq, u, ps, gs, pv, tx, txm, tg, tgm, raw, rawm, tw, tp, tq, si, so, pm, uin, vin, at, nt, ya, inv,
           w_sem, x1_send, x1_recv, x2_send, x2_recv, g1_send, g1_recv, gm_send, gm_recv, r1_send, r1_recv, rm_send, rm_recv, pair_sem,
           sc_send, sc_recv, sd_sem, g2_send, g2_recv, up_send, up_recv):
    i = lax.axis_index("inst")
    a = lax.axis_index("axial")
    local, tiles, width = s0.shape
    chips = n_inst // 2
    per = tiles // chips
    mid = tiles // 2
    cols = width // n_inst
    block = 2 * cols
    both = 2 * local
    x, core = i // 2, lax.rem(i, 2)
    y, z = a // NZ, lax.rem(a, NZ)
    last = n_axial // NZ - 1
    chunks = block // CHUNK
    hub = core == 1
    lead = (z == NZ - 1) & (y < last)
    mapped = (y > 0) & (z > 0)
    data = pl.ds(block, both)

    loads = [pltpu.make_async_copy(src, dst, w_sem.at[n]) for n, (src, dst) in enumerate(
        [(s_hbm, s0), (f_hbm, f), (c_hbm, wc), (a_hbm, wa), (k_hbm.at[pl.ds(0, kmat.shape[0])], kmat)])]
    for load in loads:
        load.start()

    def remote(src, dst, send, recv, **there):
        return pltpu.make_async_remote_copy(
            src_ref=src, dst_ref=dst, send_sem=send, recv_sem=recv, device_id=there, device_id_type=MESH)

    barrier = pltpu.get_barrier_semaphore()
    for d in range(1, n_inst):
        pl.semaphore_signal(barrier, inc=1, device_id={"inst": lax.rem(i + d, n_inst)}, device_id_type=MESH)

    @pl.when(hub)
    def _():
        for d in (1, NZ - 1):
            there = y * NZ + lax.rem(z + d, NZ)
            pl.semaphore_signal(barrier, inc=1, device_id={"axial": there}, device_id_type=MESH)

        @pl.when(lead)
        def _():
            for zz in range(NZ):
                pl.semaphore_signal(barrier, inc=1, device_id={"axial": (y + 1) * NZ + zz}, device_id_type=MESH)

        @pl.when(y > 0)
        def _():
            pl.semaphore_signal(barrier, inc=1, device_id={"axial": y * NZ - 1}, device_id_type=MESH)

    loads[0].wait()
    loads[1].wait()
    for t in range(tiles):
        sb[t, 0:local, :] = s0[:, t, :]
        sb[t, local:both, :] = f[:, t, :]
    row = lax.broadcasted_iota(jnp.int32, (cols, width), 0)
    col = lax.broadcasted_iota(jnp.int32, (cols, width), 1)
    ps[0:cols] = jnp.where(col == row + i * cols, 1.0, 0.0).astype(F32)
    ps[cols:] = jnp.zeros((both, width), F32)
    gs[...] = jnp.zeros((cols + both, width), F32)

    def first(xx, sender):
        return remote(sb.at[pl.ds(per * xx, per)], rb.at[sender], x1_send.at[xx], x1_recv.at[sender], inst=2 * xx)

    def second(d):
        xx = lax.rem(x + d, chips)
        return remote(ob.at[xx], rq.at[pl.ds(per * x, per)], x2_send.at[d], x2_recv.at[d], inst=2 * xx)

    def gather(src, dst, send, recv, xx, sender):
        half = pl.ds(pl.multiple_of(lax.rem(sender, 2) * cols, 8), cols)
        return remote(src.at[0:cols], dst.at[sender // 2, half], send.at[xx], recv.at[sender], inst=2 * xx + 1)

    def whole(xx, sender):
        return gather(tx, tg, g1_send, g1_recv, xx, sender)

    def halfway(xx, sender):
        return gather(txm, tgm, gm_send, gm_recv, xx, sender)

    def raw_whole(xx, sender):
        return remote(tx.at[cols:cols + both], raw.at[sender], r1_send.at[xx], r1_recv.at[sender], inst=2 * xx + 1)

    def raw_half(xx, sender):
        return remote(txm.at[cols:cols + both], rawm.at[sender], rm_send.at[xx], rm_recv.at[sender], inst=2 * xx + 1)

    def to_hubs(copy):
        for xx in range(chips):
            @pl.when(2 * xx + 1 != i)
            def _(xx=xx):
                copy(xx, i).start()

    other = i + 1 - 2 * core
    pass_rq = remote(rq, rq, pair_sem.at[0], pair_sem.at[1], inst=other)
    give = remote(vin.at[0], vin.at[1], pair_sem.at[4], pair_sem.at[5], inst=other)
    early = remote(u.at[pl.ds(0, mid)], u.at[pl.ds(0, mid)], pair_sem.at[6], pair_sem.at[7], inst=other)
    late = remote(u.at[pl.ds(mid, mid)], u.at[pl.ds(mid, mid)], pair_sem.at[8], pair_sem.at[9], inst=other)

    for load in loads[2:]:
        load.wait()

    def nt_dot(v, w):
        return lax.dot_general(v, w, NT, preferred_element_type=F32)

    def joined(v):
        m = v.shape[0] // 2
        return v[:m] + v[m:]

    def driven(t, b):
        return jnp.concatenate([-b[:cols], sb[t] - b[cols:]], 0)

    t = order[0]
    ps[...] = times(driven(t, times(ps[...], wc[t])), wa[t])

    def column_steps(start, made):
        def steps(n, carry):
            p, g = ps[...], gs[...]
            for j in range(UNROLL):
                k = start + n * UNROLL + j
                before, here = order[k], order[jnp.minimum(k + 1, tiles - 1)]
                high_p, high_g = split(p), split(g)
                bp, bg = nt_dot(high_p, wc[here]), nt_dot(high_g, wc[before])
                last_p = p
                bp, bg = driven(here, joined(bp)), p + joined(bg)
                p, g = nt_dot(split(bp), wa[here]), nt_dot(split(bg), wa[before])
                p, g = joined(p), -joined(g)
            ps[...] = p
            gs[...] = g
            pv[...] = last_p
            return carry
        lax.fori_loop(0, mid // UNROLL, steps, 0)
        made[...] = pack(pv[...], gs[...])

    column_steps(0, txm)

    pl.semaphore_wait(barrier, n_inst - 1 + jnp.where(
        hub, 2 + jnp.where(lead, NZ, 0) + jnp.where(y > 0, 1, 0), 0))
    for xx in range(chips):
        @pl.when(2 * xx != i)
        def _(xx=xx):
            first(xx, i).start()

    column_steps(mid, tx)
    to_hubs(whole)
    to_hubs(raw_whole)

    for t in range(tiles):
        pos = jnp.int32(0)
        for k in range(tiles):
            pos = jnp.where(order[k] == t, k, pos)
        inv[t] = pos

    pad = nt.shape[2] // 2

    def prepare(n, carry):
        t = order[mid * core + n]
        turned = wa[t].T
        at[n] = turned
        high, low = halves(lax.dot_general(wc[t].T, turned, NN, preferred_element_type=F32))
        nt[n, :, 0:width] = high
        nt[n, :, pad:pad + width] = low
        return carry

    def drive(n, carry):
        ya[n] = times(rq[order[mid * core + n]], at[n], NN)
        return carry

    def by_pair(v, n):
        m = joined(lax.dot_general(split(v), nt[n], NN, preferred_element_type=F32))
        return m[:, :width] + m[:, pad:pad + width]

    def rerun(p, g):
        p = ya[0, 0:both] - by_pair(p, 0)
        for n in range(mid):
            old = p
            if n + 1 < mid:
                p = ya[n + 1, 0:both] - by_pair(old, n + 1)
            g = ya[n, both:] - by_pair(g, n) - times(old, at[n], NN)
            u[mid * core + n] = g

    zero = jnp.zeros((both, width), F32)

    @pl.when(core == 0)
    def _():
        rb[i] = sb[pl.ds(per * x, per)]
        for j in range(n_inst):
            @pl.when(j != i)
            def _(j=j):
                first(0, j).wait_recv()
        for t in range(per):
            mixed = jnp.dot(kmat[:, 0:both * n_inst], rb[:, t].reshape(both * n_inst, width),
                            precision=lax.Precision.HIGHEST, preferred_element_type=F32)
            ob[:, t] = mixed.reshape(chips, 2 * both, width)
        lax.fori_loop(0, mid, prepare, 0)
        for d in range(1, chips):
            second(d).start()
        rq[pl.ds(per * x, per)] = ob[x]
        to_hubs(raw_half)
        to_hubs(halfway)
        for d in range(1, chips):
            second(d).wait_recv()
        pass_rq.start()
        lax.fori_loop(0, mid, drive, 0)
        give.wait_recv()
        rerun(vin[1, 0:both], vin[1, both:])
        early.start()
        late.wait_recv()
        for t in range(tiles):
            out[:, t, :] = s0[:, t, :] + u[inv[t], 0:local, :]
        early.wait_send()
        pass_rq.wait_send()
        for d in range(1, chips):
            second(d).wait_send()

    @pl.when(hub)
    def _():
        def scan(c):
            part = pl.ds(pl.multiple_of(c * CHUNK, CHUNK), CHUNK)
            return remote(so.at[part], si.at[part], sc_send.at[c], sc_recv.at[c],
                          axial=y * NZ + lax.rem(z + 1, NZ))

        scan_data = remote(so.at[data], si.at[data], sd_sem.at[0], sd_sem.at[1],
                           axial=y * NZ + lax.rem(z + 1, NZ))

        def spread(src, c, d):
            part = pl.ds(pl.multiple_of(c * CHUNK, CHUNK), CHUNK)
            return remote(src.at[part], pm.at[x, part], g2_send.at[d - 1, c], g2_recv.at[d - 1, c],
                          inst=lax.rem(i + 2 * d, n_inst))

        def down(zz):
            return remote(uin.at[0], uin.at[1], up_send.at[zz], up_recv.at[0],
                          axial=lax.rem(y + 1, last + 1) * NZ + zz)

        def mix(rows):
            made = [jnp.dot(kmat[pl.ds(pl.multiple_of(2 * both * x, 8), 2 * both), 0:both * n_inst], part,
                            precision=lax.Precision.HIGHEST, preferred_element_type=F32)
                    for part in unpack(rows[...].reshape(both * n_inst, 2 * width))]
            return made[0][:both], made[0][both:] + made[1][:both]

        count = jnp.where(y == 0, 0, chunks)

        tg[x, pl.ds(cols, cols)] = tx[0:cols]
        tgm[x, pl.ds(cols, cols)] = txm[0:cols]
        raw[i] = tx[cols:]
        rawm[i] = txm[cols:]
        whole(0, i - 1).wait_recv()

        @pl.when((z == 0) & (y > 0))
        def _():
            so[0:block] = tg[x]
            lax.fori_loop(0, count, lambda c, k: (scan(c).start(), k)[1], 0)

        lax.fori_loop(0, mid, prepare, 0)
        store_map(tw, block * x, tg[x])
        for d in FAR_LAST:
            there = lax.rem(x + d, chips)
            for j in range(2):
                whole(0, 2 * there + j).wait_recv()
            store_map(tw, block * there, tg[there])

        to_hubs(raw_half)
        to_hubs(halfway)

        @pl.when(z > 0)
        def _():
            def chunk_step(c, carry):
                scan(c).wait_recv()
                part = pl.ds(pl.multiple_of(c * CHUNK, CHUNK), CHUNK)

                @pl.when(z < NZ - 1)
                def _():
                    so[part] = pack(*through(tw, *unpack(si[part])))
                    scan(c).start()

                for d in FAR_FIRST:
                    spread(si, c, d).start()
                return carry

            lax.fori_loop(0, count, chunk_step, 0)

        for j in range(n_inst):
            @pl.when(j != i)
            def _(j=j):
                raw_whole(0, j).wait_recv()
        bp, bg = mix(raw)

        @pl.when(z == 0)
        def _():
            so[data] = pack(bp, bg)
            scan_data.start()

        @pl.when(z > 0)
        def _():
            scan_data.wait_recv()

            @pl.when((z < NZ - 1) | (y == 0))
            def _():
                p, g = through(tw, *unpack(si[data]))
                so[data] = pack(p + bp, g + bg)

            @pl.when(z < NZ - 1)
            def _():
                scan_data.start()

        @pl.when((y == 0) & (z == NZ - 1))
        def _():
            uin[0] = so[data]
            for zz in range(NZ):
                down(zz).start()

        def give_out(p, g):
            vin[0, 0:both] = p
            vin[0, both:] = g
            give.start()

        @pl.when(y == 0)
        def _():
            @pl.when(z == 0)
            def _():
                give_out(zero, zero)

            @pl.when(z > 0)
            def _():
                give_out(*unpack(si[data]))

        pass_rq.wait_recv()
        lax.fori_loop(0, mid, drive, 0)
        for j in range(n_inst):
            @pl.when(j != i)
            def _(j=j):
                raw_half(0, j).wait_recv()
                halfway(0, j).wait_recv()
        mp, mg = mix(rawm)
        for xx in range(chips):
            store_map(tq, block * xx, tgm[xx])

        @pl.when(mapped)
        def _():
            store_map(tp, block * x, si[0:block])
            for d in FAR_LAST:
                there = lax.rem(x + chips - d, chips)
                for c in range(chunks):
                    spread(si, c, d).wait_recv()
                store_map(tp, block * there, pm[there])

        @pl.when(y > 0)
        def _():
            down(0).wait_recv()

        @pl.when(mapped)
        def _():
            p, g = through(tp, *unpack(uin[1]))
            own_p, own_g = unpack(si[data])
            p, g = p + own_p, g + own_g

            @pl.when(lead)
            def _():
                next_p, next_g = through(tw, p, g)
                uin[0] = pack(next_p + bp, next_g + bg)
                for zz in range(NZ):
                    down(zz).start()

            give_out(p, g)

        @pl.when((y > 0) & (z == 0))
        def _():
            give_out(*unpack(uin[1]))

        p, g = through(tq, vin[0, 0:both], vin[0, both:])
        rerun(p + mp, g + mg)
        late.start()
        early.wait_recv()
        for t in range(tiles):
            out[:, t, :] = s0[:, t, :] + u[inv[t], local:both, :]

        late.wait_send()
        give.wait_send()

        @pl.when(z < NZ - 1)
        def _():
            scan_data.wait_send()
            lax.fori_loop(0, count, lambda c, k: (scan(c).wait_send(), k)[1], 0)

        @pl.when(mapped)
        def _():
            for d in range(1, chips):
                for c in range(chunks):
                    spread(si, c, d).wait_send()

        @pl.when(lead)
        def _():
            for zz in range(NZ):
                down(zz).wait_send()

    for xx in range(chips):
        @pl.when(2 * xx != i)
        def _(xx=xx):
            first(xx, i).wait_send()

        @pl.when(2 * xx + 1 != i)
        def _(xx=xx):
            whole(xx, i).wait_send()
            halfway(xx, i).wait_send()
            raw_whole(xx, i).wait_send()
            raw_half(xx, i).wait_send()


def solution(mesh):
    n_inst, n_axial = mesh.shape["inst"], mesh.shape["axial"]

    def on_device(flow_state, forcing, tile_inverse, coupling, sweep_order):
        local, tiles, width = flow_state.shape
        chips = n_inst // 2
        per = tiles // chips
        cols = width // n_inst
        block = 2 * cols
        pad = -(-width // 128) * 128
        both = 2 * local
        chunks = block // CHUNK
        size = both * n_inst
        kmat = np.zeros((10 * size, 128), np.float32)
        kmat[:size, :size] = exchange_matrix(local * n_inst, n_inst)
        kmat = jnp.asarray(kmat)
        hbm = pl.BlockSpec(memory_space=pl.ANY)
        vmem = pl.BlockSpec(memory_space=pltpu.VMEM)
        dma = pltpu.SemaphoreType.DMA
        return pl.pallas_call(
            functools.partial(kernel, n_inst, n_axial),
            out_shape=jax.ShapeDtypeStruct(flow_state.shape, F32),
            in_specs=[pl.BlockSpec(memory_space=pltpu.SMEM), hbm, hbm, hbm, hbm, hbm],
            out_specs=vmem,
            scratch_shapes=[
                pltpu.VMEM((size, 128), F32),
                pltpu.VMEM(flow_state.shape, F32),
                pltpu.VMEM(flow_state.shape, F32),
                pltpu.VMEM((tiles, width, width), BF16),
                pltpu.VMEM((tiles, width, width), BF16),
                pltpu.VMEM((tiles, both, width), F32),
                pltpu.VMEM((n_inst, per, both, width), F32),
                pltpu.VMEM((chips, per, 2 * both, width), F32),
                pltpu.VMEM((tiles, 2 * both, width), F32),
                pltpu.VMEM((tiles, both, width), F32),
                pltpu.VMEM((cols + both, width), F32),
                pltpu.VMEM((cols + both, width), F32),
                pltpu.VMEM((cols + both, width), F32),
                pltpu.VMEM((cols + both, 2 * width), F32),
                pltpu.VMEM((cols + both, 2 * width), F32),
                pltpu.VMEM((chips, block, 2 * width), F32),
                pltpu.VMEM((chips, block, 2 * width), F32),
                pltpu.VMEM((n_inst, both, 2 * width), F32),
                pltpu.VMEM((n_inst, both, 2 * width), F32),
                pltpu.VMEM((width, 4 * pad), BF16),
                pltpu.VMEM((width, 4 * pad), BF16),
                pltpu.VMEM((width, 4 * pad), BF16),
                pltpu.VMEM((block + both, 2 * width), F32),
                pltpu.VMEM((block + both, 2 * width), F32),
                pltpu.VMEM((chips, block, 2 * width), F32),
                pltpu.VMEM((2, both, 2 * width), F32),
                pltpu.VMEM((2, 2 * both, width), F32),
                pltpu.VMEM((tiles // 2, width, width), BF16),
                pltpu.VMEM((tiles // 2, width, 2 * pad), BF16),
                pltpu.VMEM((tiles // 2, 2 * both, width), F32),
                pltpu.SMEM((tiles,), jnp.int32),
                dma((5,)),
                dma((chips,)), dma((n_inst,)), dma((chips,)), dma((chips,)),
                dma((chips,)), dma((n_inst,)), dma((chips,)), dma((n_inst,)),
                dma((chips,)), dma((n_inst,)), dma((chips,)), dma((n_inst,)),
                dma((10,)),
                dma((chunks,)), dma((chunks,)), dma((2,)),
                dma((chips - 1, chunks)), dma((chips - 1, chunks)),
                dma((NZ,)), dma((1,)),
            ],
            compiler_params=pltpu.CompilerParams(collective_id=0, has_side_effects=True, vmem_limit_bytes=VMEM_BYTES),
        )(sweep_order, kmat, flow_state, forcing, tile_inverse, coupling)

    return jax.shard_map(
        on_device,
        mesh=mesh,
        in_specs=(P("inst", "axial", None), P("inst", "axial", None), P("axial", None, None),
                  P("axial", None, None), P("axial")),
        out_specs=P("inst", "axial", None),
        check_vma=False,
    )
```

```python
import functools

import jax
import jax.numpy as jnp
import numpy as np
from jax import lax
from jax.experimental import pallas as pl
from jax.experimental.pallas import tpu as pltpu
from jax.sharding import PartitionSpec as P

ITERS = 2
SPECTRAL_GAIN = 2.0
NZ = 8
VMEM_BYTES = 56_400_000
FAR_FIRST, FAR_LAST = (2, 1, 3), (1, 3, 2)
UNROLL = 8
CHUNK = 8
MESH = pl.DeviceIdType.MESH
F32, BF16 = jnp.float32, jnp.bfloat16
NT = (((1,), (1,)), ((), ()))
NN = (((1,), (0,)), ((), ()))


def exchange_matrix(period, groups):
    idx = np.arange(period)
    dist = idx[:, None] - idx[None, :]
    angle = np.pi * dist / period
    safe = np.where(dist == 0, 1.0, np.sin(angle))
    deriv = np.where(dist == 0, 0.0, 0.5 * (1.0 - 2.0 * (dist % 2)) * np.cos(angle) / safe)
    e = deriv * (SPECTRAL_GAIN / period) + np.eye(period)
    whole = np.block([[-e @ e, e], [-2.0 * e, 2.0 * np.eye(period)]])
    local = period // groups
    given = [part * period + dev * local + n for dev in range(groups) for part in range(2) for n in range(local)]
    wide = 2 * local
    made = [part * period + chip * wide + n for chip in range(groups // 2) for part in range(2) for n in range(wide)]
    return whole[np.ix_(made, given)].astype(np.float32)


def halves(x):
    high = x.astype(BF16)
    low = (x - high.astype(F32)).astype(BF16)
    return high, low


def split(x):
    high = x.astype(BF16).astype(F32)
    return jnp.concatenate([high, x - high], 0).astype(BF16)


def times(x, w, dims=NT):
    m = x.shape[0]
    y = lax.dot_general(split(x), w, dims, preferred_element_type=F32)
    return y[:m] + y[m:]


def pack(p, g):
    whole = p.shape[1] // 128 * 128
    return jnp.concatenate([p[:, :whole], g[:, :whole], p[:, whole:], g[:, whole:]], 1)


def unpack(b):
    width = b.shape[1] // 2
    whole = width // 128 * 128
    middle = whole + width
    return (jnp.concatenate([b[:, :whole], b[:, 2 * whole:middle]], 1),
            jnp.concatenate([b[:, whole:2 * whole], b[:, middle:]], 1))


def store_map(dst, row, block):
    pad = dst.shape[1] // 4
    for part, rows in enumerate(unpack(block)):
        width = rows.shape[1]
        at = pl.ds(pl.multiple_of(row, 16), rows.shape[0])
        high, low = halves(rows)
        dst[at, part * pad:part * pad + width] = high
        dst[at, (2 + part) * pad:(2 + part) * pad + width] = low


def through(m, p, g):
    rows, width = p.shape
    pad = m.shape[1] // 4
    x = jnp.concatenate([p, g], 0)
    y = lax.dot_general(split(x), m[:, 0:2 * pad], NN, preferred_element_type=F32)
    z = lax.dot_general(x.astype(BF16), m[:, 2 * pad:], NN, preferred_element_type=F32)
    y = y[:2 * rows] + y[2 * rows:] + z
    return y[:rows, :width], y[rows:, :width] + y[:rows, pad:pad + width]


def kernel(n_inst, n_axial, order, k_hbm, s_hbm, f_hbm, a_hbm, c_hbm, out,
           kmat, s0, f, wa, wc, sb, rb, ob, rq, u, ps, gs, pv, tx, txm, tg, tgm, raw, rawm, tw, tp, tq, si, so, pm, uin, vin, at, nt, ya, inv,
           w_sem, x1_send, x1_recv, x2_send, x2_recv, g1_send, g1_recv, gm_send, gm_recv, r1_send, r1_recv, rm_send, rm_recv, pair_sem,
           sc_send, sc_recv, sd_sem, g2_send, g2_recv, up_send, up_recv):
    i = lax.axis_index("inst")
    a = lax.axis_index("axial")
    local, tiles, width = s0.shape
    chips = n_inst // 2
    per = tiles // chips
    mid = tiles // 2
    cols = width // n_inst
    block = 2 * cols
    both = 2 * local
    x, core = i // 2, lax.rem(i, 2)
    y, z = a // NZ, lax.rem(a, NZ)
    last = n_axial // NZ - 1
    chunks = block // CHUNK
    hub = core == 1
    lead = (z == NZ - 1) & (y < last)
    mapped = (y > 0) & (z > 0)
    data = pl.ds(block, both)

    loads = [pltpu.make_async_copy(src, dst, w_sem.at[n]) for n, (src, dst) in enumerate(
        [(s_hbm, s0), (f_hbm, f), (c_hbm, wc), (a_hbm, wa), (k_hbm.at[pl.ds(0, kmat.shape[0])], kmat)])]
    for load in loads:
        load.start()

    def remote(src, dst, send, recv, **there):
        return pltpu.make_async_remote_copy(
            src_ref=src, dst_ref=dst, send_sem=send, recv_sem=recv, device_id=there, device_id_type=MESH)

    barrier = pltpu.get_barrier_semaphore()
    for d in range(1, n_inst):
        pl.semaphore_signal(barrier, inc=1, device_id={"inst": lax.rem(i + d, n_inst)}, device_id_type=MESH)

    @pl.when(hub)
    def _():
        for d in (1, NZ - 1):
            there = y * NZ + lax.rem(z + d, NZ)
            pl.semaphore_signal(barrier, inc=1, device_id={"axial": there}, device_id_type=MESH)

        @pl.when(lead)
        def _():
            for zz in range(NZ):
                pl.semaphore_signal(barrier, inc=1, device_id={"axial": (y + 1) * NZ + zz}, device_id_type=MESH)

        @pl.when(y > 0)
        def _():
            pl.semaphore_signal(barrier, inc=1, device_id={"axial": y * NZ - 1}, device_id_type=MESH)

    loads[0].wait()
    loads[1].wait()
    for t in range(tiles):
        sb[t, 0:local, :] = s0[:, t, :]
        sb[t, local:both, :] = f[:, t, :]
    row = lax.broadcasted_iota(jnp.int32, (cols, width), 0)
    col = lax.broadcasted_iota(jnp.int32, (cols, width), 1)
    ps[0:cols] = jnp.where(col == row + i * cols, 1.0, 0.0).astype(F32)
    ps[cols:] = jnp.zeros((both, width), F32)
    gs[...] = jnp.zeros((cols + both, width), F32)

    def first(xx, sender):
        return remote(sb.at[pl.ds(per * xx, per)], rb.at[sender], x1_send.at[xx], x1_recv.at[sender], inst=2 * xx)

    def second(d):
        xx = lax.rem(x + d, chips)
        return remote(ob.at[xx], rq.at[pl.ds(per * x, per)], x2_send.at[d], x2_recv.at[d], inst=2 * xx)

    def gather(src, dst, send, recv, xx, sender):
        half = pl.ds(pl.multiple_of(lax.rem(sender, 2) * cols, 8), cols)
        return remote(src.at[0:cols], dst.at[sender // 2, half], send.at[xx], recv.at[sender], inst=2 * xx + 1)

    def whole(xx, sender):
        return gather(tx, tg, g1_send, g1_recv, xx, sender)

    def halfway(xx, sender):
        return gather(txm, tgm, gm_send, gm_recv, xx, sender)

    def raw_whole(xx, sender):
        return remote(tx.at[cols:cols + both], raw.at[sender], r1_send.at[xx], r1_recv.at[sender], inst=2 * xx + 1)

    def raw_half(xx, sender):
        return remote(txm.at[cols:cols + both], rawm.at[sender], rm_send.at[xx], rm_recv.at[sender], inst=2 * xx + 1)

    def to_hubs(copy):
        for xx in range(chips):
            @pl.when(2 * xx + 1 != i)
            def _(xx=xx):
                copy(xx, i).start()

    other = i + 1 - 2 * core
    pass_rq = remote(rq, rq, pair_sem.at[0], pair_sem.at[1], inst=other)
    give = remote(vin.at[0], vin.at[1], pair_sem.at[4], pair_sem.at[5], inst=other)
    early = remote(u.at[pl.ds(0, mid)], u.at[pl.ds(0, mid)], pair_sem.at[6], pair_sem.at[7], inst=other)
    late = remote(u.at[pl.ds(mid, mid)], u.at[pl.ds(mid, mid)], pair_sem.at[8], pair_sem.at[9], inst=other)

    for load in loads[2:]:
        load.wait()

    def nt_dot(v, w):
        return lax.dot_general(v, w, NT, preferred_element_type=F32)

    def joined(v):
        m = v.shape[0] // 2
        return v[:m] + v[m:]

    def driven(t, b):
        return jnp.concatenate([-b[:cols], sb[t] - b[cols:]], 0)

    t = order[0]
    ps[...] = times(driven(t, times(ps[...], wc[t])), wa[t])

    def column_steps(start, made):
        def steps(n, carry):
            p, g = ps[...], gs[...]
            for j in range(UNROLL):
                k = start + n * UNROLL + j
                before, here = order[k], order[jnp.minimum(k + 1, tiles - 1)]
                high_p, high_g = split(p), split(g)
                bp, bg = nt_dot(high_p, wc[here]), nt_dot(high_g, wc[before])
                last_p = p
                bp, bg = driven(here, joined(bp)), p + joined(bg)
                p, g = nt_dot(split(bp), wa[here]), nt_dot(split(bg), wa[before])
                p, g = joined(p), -joined(g)
            ps[...] = p
            gs[...] = g
            pv[...] = last_p
            return carry
        lax.fori_loop(0, mid // UNROLL, steps, 0)
        made[...] = pack(pv[...], gs[...])

    column_steps(0, txm)

    pl.semaphore_wait(barrier, n_inst - 1 + jnp.where(
        hub, 2 + jnp.where(lead, NZ, 0) + jnp.where(y > 0, 1, 0), 0))
    for xx in range(chips):
        @pl.when(2 * xx != i)
        def _(xx=xx):
            first(xx, i).start()

    column_steps(mid, tx)
    to_hubs(whole)
    to_hubs(raw_whole)

    for t in range(tiles):
        pos = jnp.int32(0)
        for k in range(tiles):
            pos = jnp.where(order[k] == t, k, pos)
        inv[t] = pos

    pad = nt.shape[2] // 2

    def prepare(n, carry):
        t = order[mid * core + n]
        turned = wa[t].T
        at[n] = turned
        high, low = halves(lax.dot_general(wc[t].T, turned, NN, preferred_element_type=F32))
        nt[n, :, 0:width] = high
        nt[n, :, pad:pad + width] = low
        return carry

    def drive(n, carry):
        ya[n] = times(rq[order[mid * core + n]], at[n], NN)
        return carry

    def by_pair(v, n):
        m = joined(lax.dot_general(split(v), nt[n], NN, preferred_element_type=F32))
        return m[:, :width] + m[:, pad:pad + width]

    def rerun(p, g):
        p = ya[0, 0:both] - by_pair(p, 0)
        for n in range(mid):
            old = p
            if n + 1 < mid:
                p = ya[n + 1, 0:both] - by_pair(old, n + 1)
            g = ya[n, both:] - by_pair(g, n) - times(old, at[n], NN)
            u[mid * core + n] = g

    zero = jnp.zeros((both, width), F32)

    @pl.when(core == 0)
    def _():
        rb[i] = sb[pl.ds(per * x, per)]
        for j in range(n_inst):
            @pl.when(j != i)
            def _(j=j):
                first(0, j).wait_recv()
        for t in range(per):
            mixed = jnp.dot(kmat[:, 0:both * n_inst], rb[:, t].reshape(both * n_inst, width),
                            precision=lax.Precision.HIGHEST, preferred_element_type=F32)
            ob[:, t] = mixed.reshape(chips, 2 * both, width)
        lax.fori_loop(0, mid, prepare, 0)
        for d in range(1, chips):
            second(d).start()
        rq[pl.ds(per * x, per)] = ob[x]
        to_hubs(raw_half)
        to_hubs(halfway)
        for d in range(1, chips):
            second(d).wait_recv()
        pass_rq.start()
        lax.fori_loop(0, mid, drive, 0)
        give.wait_recv()
        rerun(vin[1, 0:both], vin[1, both:])
        early.start()
        late.wait_recv()
        for t in range(tiles):
            out[:, t, :] = s0[:, t, :] + u[inv[t], 0:local, :]
        early.wait_send()
        pass_rq.wait_send()
        for d in range(1, chips):
            second(d).wait_send()

    @pl.when(hub)
    def _():
        def scan(c):
            part = pl.ds(pl.multiple_of(c * CHUNK, CHUNK), CHUNK)
            return remote(so.at[part], si.at[part], sc_send.at[c], sc_recv.at[c],
                          axial=y * NZ + lax.rem(z + 1, NZ))

        scan_data = remote(so.at[data], si.at[data], sd_sem.at[0], sd_sem.at[1],
                           axial=y * NZ + lax.rem(z + 1, NZ))

        def spread(src, c, d):
            part = pl.ds(pl.multiple_of(c * CHUNK, CHUNK), CHUNK)
            return remote(src.at[part], pm.at[x, part], g2_send.at[d - 1, c], g2_recv.at[d - 1, c],
                          inst=lax.rem(i + 2 * d, n_inst))

        def down(zz):
            return remote(uin.at[0], uin.at[1], up_send.at[zz], up_recv.at[0],
                          axial=lax.rem(y + 1, last + 1) * NZ + zz)

        def mix(rows):
            made = [jnp.dot(kmat[pl.ds(pl.multiple_of(2 * both * x, 8), 2 * both), 0:both * n_inst], part,
                            precision=lax.Precision.HIGHEST, preferred_element_type=F32)
                    for part in unpack(rows[...].reshape(both * n_inst, 2 * width))]
            return made[0][:both], made[0][both:] + made[1][:both]

        count = jnp.where(y == 0, 0, chunks)

        tg[x, pl.ds(cols, cols)] = tx[0:cols]
        tgm[x, pl.ds(cols, cols)] = txm[0:cols]
        raw[i] = tx[cols:]
        rawm[i] = txm[cols:]
        whole(0, i - 1).wait_recv()

        @pl.when((z == 0) & (y > 0))
        def _():
            so[0:block] = tg[x]
            lax.fori_loop(0, count, lambda c, k: (scan(c).start(), k)[1], 0)

        lax.fori_loop(0, mid, prepare, 0)
        store_map(tw, block * x, tg[x])
        for d in FAR_LAST:
            there = lax.rem(x + d, chips)
            for j in range(2):
                whole(0, 2 * there + j).wait_recv()
            store_map(tw, block * there, tg[there])

        to_hubs(raw_half)
        to_hubs(halfway)

        @pl.when(z > 0)
        def _():
            def chunk_step(c, carry):
                scan(c).wait_recv()
                part = pl.ds(pl.multiple_of(c * CHUNK, CHUNK), CHUNK)

                @pl.when(z < NZ - 1)
                def _():
                    so[part] = pack(*through(tw, *unpack(si[part])))
                    scan(c).start()

                for d in FAR_FIRST:
                    spread(si, c, d).start()
                return carry

            lax.fori_loop(0, count, chunk_step, 0)

        for j in range(n_inst):
            @pl.when(j != i)
            def _(j=j):
                raw_whole(0, j).wait_recv()
        bp, bg = mix(raw)

        @pl.when(z == 0)
        def _():
            so[data] = pack(bp, bg)
            scan_data.start()

        @pl.when(z > 0)
        def _():
            scan_data.wait_recv()

            @pl.when((z < NZ - 1) | (y == 0))
            def _():
                p, g = through(tw, *unpack(si[data]))
                so[data] = pack(p + bp, g + bg)

            @pl.when(z < NZ - 1)
            def _():
                scan_data.start()

        @pl.when((y == 0) & (z == NZ - 1))
        def _():
            uin[0] = so[data]
            for zz in range(NZ):
                down(zz).start()

        def give_out(p, g):
            vin[0, 0:both] = p
            vin[0, both:] = g
            give.start()

        @pl.when(y == 0)
        def _():
            @pl.when(z == 0)
            def _():
                give_out(zero, zero)

            @pl.when(z > 0)
            def _():
                give_out(*unpack(si[data]))

        pass_rq.wait_recv()
        lax.fori_loop(0, mid, drive, 0)
        for j in range(n_inst):
            @pl.when(j != i)
            def _(j=j):
                raw_half(0, j).wait_recv()
                halfway(0, j).wait_recv()
        mp, mg = mix(rawm)
        for xx in range(chips):
            store_map(tq, block * xx, tgm[xx])

        @pl.when(mapped)
        def _():
            store_map(tp, block * x, si[0:block])
            for d in FAR_LAST:
                there = lax.rem(x + chips - d, chips)
                for c in range(chunks):
                    spread(si, c, d).wait_recv()
                store_map(tp, block * there, pm[there])

        @pl.when(y > 0)
        def _():
            down(0).wait_recv()

        @pl.when(mapped)
        def _():
            p, g = through(tp, *unpack(uin[1]))
            own_p, own_g = unpack(si[data])
            p, g = p + own_p, g + own_g

            @pl.when(lead)
            def _():
                next_p, next_g = through(tw, p, g)
                uin[0] = pack(next_p + bp, next_g + bg)
                for zz in range(NZ):
                    down(zz).start()

            give_out(p, g)

        @pl.when((y > 0) & (z == 0))
        def _():
            give_out(*unpack(uin[1]))

        p, g = through(tq, vin[0, 0:both], vin[0, both:])
        rerun(p + mp, g + mg)
        late.start()
        early.wait_recv()
        for t in range(tiles):
            out[:, t, :] = s0[:, t, :] + u[inv[t], local:both, :]

        late.wait_send()
        give.wait_send()

        @pl.when(z < NZ - 1)
        def _():
            scan_data.wait_send()
            lax.fori_loop(0, count, lambda c, k: (scan(c).wait_send(), k)[1], 0)

        @pl.when(mapped)
        def _():
            for d in range(1, chips):
                for c in range(chunks):
                    spread(si, c, d).wait_send()

        @pl.when(lead)
        def _():
            for zz in range(NZ):
                down(zz).wait_send()

    for xx in range(chips):
        @pl.when(2 * xx != i)
        def _(xx=xx):
            first(xx, i).wait_send()

        @pl.when(2 * xx + 1 != i)
        def _(xx=xx):
            whole(xx, i).wait_send()
            halfway(xx, i).wait_send()
            raw_whole(xx, i).wait_send()
            raw_half(xx, i).wait_send()


def solution(mesh):
    n_inst, n_axial = mesh.shape["inst"], mesh.shape["axial"]

    def on_device(flow_state, forcing, tile_inverse, coupling, sweep_order):
        local, tiles, width = flow_state.shape
        chips = n_inst // 2
        per = tiles // chips
        cols = width // n_inst
        block = 2 * cols
        pad = -(-width // 128) * 128
        both = 2 * local
        chunks = block // CHUNK
        size = both * n_inst
        kmat = np.zeros((10 * size, 128), np.float32)
        kmat[:size, :size] = exchange_matrix(local * n_inst, n_inst)
        kmat = jnp.asarray(kmat)
        hbm = pl.BlockSpec(memory_space=pl.ANY)
        vmem = pl.BlockSpec(memory_space=pltpu.VMEM)
        dma = pltpu.SemaphoreType.DMA
        return pl.pallas_call(
            functools.partial(kernel, n_inst, n_axial),
            out_shape=jax.ShapeDtypeStruct(flow_state.shape, F32),
            in_specs=[pl.BlockSpec(memory_space=pltpu.SMEM), hbm, hbm, hbm, hbm, hbm],
            out_specs=vmem,
            scratch_shapes=[
                pltpu.VMEM((size, 128), F32),
                pltpu.VMEM(flow_state.shape, F32),
                pltpu.VMEM(flow_state.shape, F32),
                pltpu.VMEM((tiles, width, width), BF16),
                pltpu.VMEM((tiles, width, width), BF16),
                pltpu.VMEM((tiles, both, width), F32),
                pltpu.VMEM((n_inst, per, both, width), F32),
                pltpu.VMEM((chips, per, 2 * both, width), F32),
                pltpu.VMEM((tiles, 2 * both, width), F32),
                pltpu.VMEM((tiles, both, width), F32),
                pltpu.VMEM((cols + both, width), F32),
                pltpu.VMEM((cols + both, width), F32),
                pltpu.VMEM((cols + both, width), F32),
                pltpu.VMEM((cols + both, 2 * width), F32),
                pltpu.VMEM((cols + both, 2 * width), F32),
                pltpu.VMEM((chips, block, 2 * width), F32),
                pltpu.VMEM((chips, block, 2 * width), F32),
                pltpu.VMEM((n_inst, both, 2 * width), F32),
                pltpu.VMEM((n_inst, both, 2 * width), F32),
                pltpu.VMEM((width, 4 * pad), BF16),
                pltpu.VMEM((width, 4 * pad), BF16),
                pltpu.VMEM((width, 4 * pad), BF16),
                pltpu.VMEM((block + both, 2 * width), F32),
                pltpu.VMEM((block + both, 2 * width), F32),
                pltpu.VMEM((chips, block, 2 * width), F32),
                pltpu.VMEM((2, both, 2 * width), F32),
                pltpu.VMEM((2, 2 * both, width), F32),
                pltpu.VMEM((tiles // 2, width, width), BF16),
                pltpu.VMEM((tiles // 2, width, 2 * pad), BF16),
                pltpu.VMEM((tiles // 2, 2 * both, width), F32),
                pltpu.SMEM((tiles,), jnp.int32),
                dma((5,)),
                dma((chips,)), dma((n_inst,)), dma((chips,)), dma((chips,)),
                dma((chips,)), dma((n_inst,)), dma((chips,)), dma((n_inst,)),
                dma((chips,)), dma((n_inst,)), dma((chips,)), dma((n_inst,)),
                dma((10,)),
                dma((chunks,)), dma((chunks,)), dma((2,)),
                dma((chips - 1, chunks)), dma((chips - 1, chunks)),
                dma((NZ,)), dma((1,)),
            ],
            compiler_params=pltpu.CompilerParams(collective_id=0, has_side_effects=True, vmem_limit_bytes=VMEM_BYTES),
        )(sweep_order, kmat, flow_state, forcing, tile_inverse, coupling)

    return jax.shard_map(
        on_device,
        mesh=mesh,
        in_specs=(P("inst", "axial", None), P("inst", "axial", None), P("axial", None, None),
                  P("axial", None, None), P("axial")),
        out_specs=P("inst", "axial", None),
        check_vma=False,
    )
```
